32 devices in a mesh: lat: 4 (over z), lon: 8 (over y, x, core).
Axes of the slice: x: 2, y: 2, z: 4, core: 2. Of those that a mesh axis runs over, the one named last changes fastest.
Arguments:
- winds: bfloat16 [16, 32, 3, 40, 128], P('lat', 'lon'), may hold values from -6 to 6
- positions: float32 [4096, 3, 128], P(('lat', 'lon')), may hold values from 0 to 39, as said below
- velocity: float32 [4096, 3, 128], P(('lat', 'lon')), may hold values from -6 to 6
- increments: float32 [4096, 3, 128], P(('lat', 'lon')), may hold values from -6 to 6
- mass: float32 [4096, 8, 128], P(('lat', 'lon')), may hold values from 0.1 to 1
- requests: int32 [32, 32, 2], P(('lat', 'lon')), may hold values from 0 to 15
- block_slots: int32 [4096, 1], P(('lat', 'lon')), may hold values from 0 to 63; in each aligned block of 128 rows (0 to 127, 128 to 255, ...) at most 8 rows name the same one
- destinations: int32 [4096, 1], P(('lat', 'lon')), may hold values from 0 to 31; in each aligned block of 128 rows (0 to 127, 128 to 255, ...) at most 8 rows name the same one
- cell_keys: int32 [4096, 128], P(('lat', 'lon')), may hold values from 0 to 2047, as said below
Outputs:
- moved: float32 [4096, 3, 128], P(('lat', 'lon'))
- turbulence: float32 [4096, 3, 128], P(('lat', 'lon'))
- concentration: float32 [16, 32, 8, 40, 128], P('lat', 'lon')
The draws below stay inside these ranges and needn't reach their ends.
Inputs may be any that keep to these rules, and one draw needn't show every extreme that they name: `positions`: component 0 (cell row) lies in 0 to 7, component 1 (cell column) in 0 to 15, component 2 (level) in 0 to 39. requests[o, t, k] names a met block of tile t by its local number. `block_slots`: slot k stands for the (k % 2)-th request that the owner sends to tile k // 2; of the 128 blocks of one owner at most 8 have the same slot, and on some owners one slot gets exactly 8. `destinations`: of the 128 blocks of one owner at most 8 have the same destination; on some owners one destination gets exactly 8. `cell_keys`: a key is (local met block) * 128 + cell of the destination tile; all keys of one particle block lie in one met block.
All inputs are finite; a program needn't handle non-finite values.
Results may differ from the reference program's by a relative error of at most 0.0027.
Values may be sent and summed in bfloat16 or wider, within the bound.
A program may use at most 64 MiB of HBM per device.

```python
import math
import jax
import jax.numpy as jnp
import numpy as np
from jax import lax

BY = 8
BX = 16
MBC = 128
LEV = 40
S = 8
BLK = 128
MBR = 4
MBK = 4
MB = 16
Q = 2
PB = 128
CAP = 8
BLOCKS = 4096
N_LAT = 4
N_LON = 8
DEVICES = 32


def draw_positions(key, part):
    unit = jax.random.uniform(jax.random.fold_in(key, 11), (BLOCKS, 3, BLK), jnp.float32)
    upper = jnp.array([BY - 1, BX - 1, LEV - 1], jnp.float32)
    return unit * upper[None, :, None]


def draw_cell_keys(key, part):
    first, second = jax.random.split(jax.random.fold_in(key, 7))
    home = jax.random.randint(first, (BLOCKS, 1), 0, MBR * MBK)
    inside = jax.random.randint(second, (BLOCKS, BLK), 0, MBC)
    return (home * MBC + inside).astype(jnp.int32)


def plant(drawn, rng, least, largest):
    index_at = [jax.random.randint(jax.random.fold_in(rng, axis), (), 0, length) for axis, length in enumerate(drawn.shape)]
    longest = drawn.shape.index(max(drawn.shape))
    neighbour = index_at[:longest] + [(index_at[longest] + 1) % drawn.shape[longest]] + index_at[longest + 1:]
    return drawn.at[tuple(index_at)].set(least).at[tuple(neighbour)].set(largest)


def block_levels(rng, shape, pieces, low, top_value):
    def one(dim, parts):
        heights = jax.random.uniform(jax.random.fold_in(jax.random.fold_in(rng, 6), dim), (parts,), jnp.float32, low / len(pieces), top_value / len(pieces))
        return jnp.repeat(jnp.exp(heights), shape[dim] // parts).reshape((-1,) + (1,) * (len(shape) - dim - 1))

    gain = one(*pieces[0])
    for cut in pieces[1:]:
        gain = gain * one(*cut)
    return gain


def shared_out(own_key, own, number, rows, count, top, most, lean):
    order = jax.random.permutation(own_key, count)
    heavy_load, ordinary = load_shares(count, rows * top, most, lean, True), load_shares(count, rows * top, most, lean, False)
    places = jnp.arange(count)

    def named(lengths, rotation):
        used = int((lengths > 0).sum())
        fixed = max(1, used // 4)
        shifted = fixed + (places - fixed + rotation * (used - fixed)) % max(1, count - fixed)
        return jnp.zeros((count,), jnp.int32).at[order[jnp.where(places < fixed, places, shifted)]].set(jnp.asarray(lengths, jnp.int32))

    lengths = jnp.where(number % 4 == 0, named(heavy_load, number // 4), named(ordinary, number - number // 4 - 1))
    mixed = jax.random.permutation(jax.random.fold_in(own, 3), count)
    donor, sink = mixed[0:count // 2 * 2:2], mixed[1:count // 2 * 2:2]
    margin = jnp.minimum(lengths[donor] - 1, most - lengths[sink]) // 2
    margin = jnp.where((donor == order[0]) | (sink == order[0]) | (lengths[sink] == 0), 0, jnp.maximum(margin, 0))
    shifted = jax.random.randint(jax.random.fold_in(own, 4), (count // 2,), 0, 1 << 20) % (margin + 1)
    lengths = lengths.at[donor].add(-shifted).at[sink].add(shifted)
    items = jnp.searchsorted(jnp.cumsum(lengths), jnp.arange(rows * top), side="right").astype(jnp.int32)
    grid = items.reshape(top, rows).T
    grid = grid[jax.random.permutation(jax.random.fold_in(own, 1), rows)]
    rotation = jax.random.randint(jax.random.fold_in(own, 2), (rows, 1), 0, top)
    return jnp.take_along_axis(grid, (jnp.arange(top)[None, :] + rotation) % top, axis=1)


def load_shares(count, total, limit, skew, full):
    weights = [(1 << 20) // math.isqrt(grade ** skew) + 1 for grade in range(1, count + 1)]
    largest = limit if full else min(limit, max(-(-total // count), total * weights[0] // sum(weights)))
    least = 1 if total - largest >= count - 1 else 0
    counts, rest = [largest] + [least] * (count - 1), total - largest - least * (count - 1)
    while rest > 0:
        free = [i for i in range(1, count) if counts[i] < largest] or [i for i in range(1, count) if counts[i] < limit]
        whole, budget = sum([weights[i] for i in free]), rest
        for i in free:
            addition = min(limit - counts[i], max(1, budget * weights[i] // whole), rest)
            counts[i] = counts[i] + addition
            rest = rest - addition
    return np.array(counts)


def normal_values(stream_key, extent, deviation, limit, pieces=(), kind=jnp.bfloat16):
    gain = block_levels(stream_key, extent, pieces, -0.22, 0.18) if pieces else 1.0
    values = jax.random.normal(stream_key, extent, jnp.float32) * deviation * gain
    return jnp.minimum(jnp.maximum(values, -limit), limit).astype(kind)


def setup_inputs(seed: int = 0) -> dict:
    streams_of = jax.random.split(jax.random.key(seed), 10)
    winds = normal_values(streams_of[0], (MBR * N_LAT, MBK * N_LON, 3, LEV, MBC), 1.0, 6.0, ((0, 4), (1, 8)))
    positions = draw_positions(jax.random.fold_in(streams_of[9], 71), 0)
    velocity = normal_values(streams_of[2], (BLOCKS, 3, BLK), 1.0, 6.0, ((0, 32),), jnp.float32)
    increments = normal_values(streams_of[3], (BLOCKS, 3, BLK), 1.0, 6.0, ((0, 32),), jnp.float32)
    mass = jnp.clip(jnp.exp(math.log(1.0) - 2.3025851 * jax.random.uniform(streams_of[4], (BLOCKS, S, BLK), jnp.float32) ** block_levels(streams_of[4], (BLOCKS, S, BLK), ((0, 32),), -0.2, 0.2)), 0.1, 1.0)
    requests = plant(jax.random.randint(streams_of[5], (DEVICES, DEVICES, Q), 0, MB), jax.random.fold_in(streams_of[5], 1), 0, MB - 1).astype(jnp.int32)
    block_slots_keys = jax.random.split(jax.random.fold_in(streams_of[6], 1), BLOCKS // PB)
    block_slots_turns = jax.random.permutation(jax.random.fold_in(streams_of[6], 3), BLOCKS // PB)
    block_slots = jax.vmap(lambda own, number: shared_out(jax.random.fold_in(streams_of[6], 2), own, number, PB, DEVICES * Q, 1, CAP, 2))(block_slots_keys, block_slots_turns).reshape((BLOCKS, 1))
    destinations_keys = jax.random.split(jax.random.fold_in(streams_of[7], 1), BLOCKS // PB)
    destinations_turns = jax.random.permutation(jax.random.fold_in(streams_of[7], 3), BLOCKS // PB)
    destinations = jax.vmap(lambda own, number: shared_out(jax.random.fold_in(streams_of[7], 2), own, number, PB, DEVICES, 1, CAP, 2))(destinations_keys, destinations_turns).reshape((BLOCKS, 1))
    cell_keys = draw_cell_keys(jax.random.fold_in(streams_of[9], 71), 0)
    return dict(winds=winds, positions=positions, velocity=velocity, increments=increments, mass=mass, requests=requests, block_slots=block_slots, destinations=destinations, cell_keys=cell_keys)


DECAY = 0.8
KICK = 0.6
STEP = 0.5


def corner(coord, top):
    base = jnp.clip(jnp.floor(coord), 0, top - 1).astype(jnp.int32)
    frac = coord - base.astype(coord.dtype)
    return base, frac


def reference(winds, positions, velocity, increments, mass, requests, block_slots, destinations, cell_keys):
    devices = N_LAT * N_LON
    block_cols = MBK * N_LON
    table = winds.reshape(-1)
    conc = jnp.zeros((MBR * N_LAT * block_cols * S * LEV * MBC,), jnp.float32)
    upper = jnp.array([BY - 1, BX - 1, LEV - 1], jnp.float32)

    def owner_step(total, items):
        pos, vel, noise, share, asked, slots, target, keys = items
        source = slots // Q
        local = asked[source, slots % Q]
        grow = (source // N_LON) * MBR + local // MBK
        gcol = (source % N_LON) * MBK + local % MBK
        blockid = (grow * block_cols + gcol)[:, None]
        row0, fy = corner(pos[:, 0], BY - 1)
        col0, fx = corner(pos[:, 1], BX - 1)
        lev0, fz = corner(pos[:, 2], LEV - 1)
        wz0 = (1.0 - fz).astype(jnp.bfloat16).astype(jnp.float32)
        wz1 = fz.astype(jnp.bfloat16).astype(jnp.float32)
        winds_at = []
        for comp in range(3):
            acc = jnp.zeros(fy.shape, jnp.float32)
            for di in range(2):
                hy = (1.0 - fy) if di == 0 else fy
                for dj in range(2):
                    hx = (1.0 - fx) if dj == 0 else fx
                    cell = (row0 + di) * BX + col0 + dj
                    base = (blockid * 3 + comp) * LEV
                    low = table[(base + lev0) * MBC + cell].astype(jnp.float32)
                    high = table[(base + lev0 + 1) * MBC + cell].astype(jnp.float32)
                    acc = acc + (hy * hx) * (wz0 * low + wz1 * high)
            winds_at.append(acc)
        wind = jnp.stack(winds_at, axis=1)
        new_vel = DECAY * vel + KICK * noise
        new_pos = jnp.clip(pos + STEP * (wind + new_vel), 0.0, upper[None, :, None])
        lz, tz = corner(new_pos[:, 2], LEV - 1)
        dest = target[:, 0][:, None]
        home = keys // MBC
        cell = keys % MBC
        grow = (dest // N_LON) * MBR + home // MBK
        gcol = (dest % N_LON) * MBK + home % MBK
        base = (grow * block_cols + gcol) * S
        indices = []
        values = []
        for s in range(S):
            for dl in range(2):
                weight = (1.0 - tz) if dl == 0 else tz
                indices.append(((base + s) * LEV + lz + dl) * MBC + cell)
                values.append((share[:, s] * weight).astype(jnp.bfloat16).astype(jnp.float32))
        total = total.at[jnp.stack(indices).reshape(-1)].add(jnp.stack(values).reshape(-1))
        return total, (new_pos, new_vel)

    items = (positions.reshape(devices, PB, 3, BLK), velocity.reshape(devices, PB, 3, BLK),
             increments.reshape(devices, PB, 3, BLK), mass.reshape(devices, PB, S, BLK),
             requests, block_slots.reshape(devices, PB), destinations.reshape(devices, PB, 1),
             cell_keys.reshape(devices, PB, BLK))
    conc, (new_pos, new_vel) = lax.scan(owner_step, conc, items)
    moved = new_pos.reshape(BLOCKS, 3, BLK)
    turbulence = new_vel.reshape(BLOCKS, 3, BLK)
    concentration = conc.reshape(MBR * N_LAT, block_cols, S, LEV, MBC)
    return moved, turbulence, concentration
```

```python
import functools

import jax
import jax.numpy as jnp
from jax import lax
from jax.experimental import pallas as pl
from jax.experimental.pallas import tpu as pltpu
from jax.sharding import PartitionSpec as P

BY = 8
BX = 16
MBC = 128
LEV = 40
S = 8
BLK = 128
MBR = 4
MBK = 4
Q = 2
MB = MBR * MBK

DECAY = 0.8
KICK = 0.6
STEP = 0.5

FULL = 65535.0
GUST = 6.1
GROUP = 4
BUNCH = 4
VMEM = pl.BlockSpec(memory_space=pltpu.VMEM)
SMEM = pl.BlockSpec(memory_space=pltpu.SMEM)


def up8(rows):
    return -(-rows // 8) * 8


def hat(offset):
    return jnp.maximum(0.0, 1.0 - jnp.abs(offset))


def low(word):
    return (word & 0xFFFF).astype(jnp.float32)


def high(word):
    return lax.shift_right_logical(word, 16).astype(jnp.float32)


def code(value, scale):
    return (value * scale + 0.5).astype(jnp.int32)


def aligned(start):
    return pl.multiple_of(start, 8)


def bits(mask):
    return jnp.where(mask, 1.0, 0.0).astype(jnp.bfloat16)


def halves(value):
    top = (value >> 8).astype(jnp.float32).astype(jnp.bfloat16)
    return top, (value & 255).astype(jnp.float32).astype(jnp.bfloat16)


def product(left, right):
    return jnp.dot(left, right, preferred_element_type=jnp.float32)


def chooser(place, pairs):
    index = lax.broadcasted_iota(jnp.int32, (pairs, place.shape[1]), 0)
    picks = jnp.concatenate(
        [jnp.where(place == 2 * index + odd, 1.0, 0.0) for odd in range(2)], axis=0
    )
    return jnp.concatenate([picks * 256.0, picks], axis=1).astype(jnp.bfloat16)


def chosen(picks, values):
    pairs = picks.shape[0] // 2
    parts = [halves(value) for value in values]
    data = jnp.concatenate(
        [
            jnp.concatenate([top for top, _ in parts], axis=1),
            jnp.concatenate([rest for _, rest in parts], axis=1),
        ],
        axis=0,
    )
    found = product(picks, data).astype(jnp.int32)
    return found[:pairs] | (found[pairs:] << 16)


class Mail:
    def __init__(self, n_lat, n_lon):
        self.n_lat, self.n_lon = n_lat, n_lon
        self.n = n_lat * n_lon
        self.me = lax.axis_index("lat") * n_lon + lax.axis_index("lon")

    def to(self, j):
        return lax.rem(self.me + j, self.n)

    def source(self, j):
        return lax.rem(self.me + self.n - j, self.n)

    def device(self, j):
        t = self.to(j)
        return (t // self.n_lon, lax.rem(t, self.n_lon))

    def greet(self):
        barrier = pltpu.get_barrier_semaphore()
        for j in range(1, self.n):
            pl.semaphore_signal(
                barrier, inc=1, device_id=self.device(j), device_id_type=pl.DeviceIdType.MESH
            )

    def meet(self):
        pl.semaphore_wait(pltpu.get_barrier_semaphore(), self.n - 1)

    def order(self):
        far = [j for j in range(1, self.n) if self.n_lon <= j <= self.n - self.n_lon]
        return far + [j for j in range(1, self.n) if j not in far]

    def copy(self, src, dst, rows, used, send, recv, j):
        return pltpu.make_async_remote_copy(
            src_ref=src.at[pl.ds(aligned(self.to(j) * rows), used)],
            dst_ref=dst.at[pl.ds(aligned(self.me * rows), used)],
            send_sem=send.at[j], recv_sem=recv.at[j],
            device_id=self.device(j), device_id_type=pl.DeviceIdType.MESH,
        )

    def own(self, src, dst, rows, used, sem):
        part = pl.ds(aligned(self.me * rows), used)
        return pltpu.make_async_copy(src.at[part], dst.at[part], sem)

    def post(self, *args):
        src, dst, rows, used, send, recv = args
        for j in self.order():
            self.copy(*args, j).start()
        self.own(src, dst, rows, used, send.at[0]).start()

    def collect(self, *args):
        src, dst, rows, used, send, recv = args
        self.own(src, dst, rows, used, send.at[0]).wait()
        for j in self.order():
            self.copy(*args, j).wait_recv()

    def settle(self, *args):
        for j in self.order():
            self.copy(*args, j).wait_send()


def send_kernel(
    dims, slots, targets, requests, positions, mass, keys,
    spots, heads, mass_msg, places,
    msg, table, sorted_spots, sorted_mass, own_heads, send, recv,
):
    n_lat, n_lon, blocks, room, spot_rows, back_rows, mass_rows = dims
    mail = Mail(n_lat, n_lon)
    mail.greet()
    n = mail.n
    entries = Q * room
    half = entries // 2
    few = room // 2
    f32 = jnp.float32
    rows = lax.broadcasted_iota(jnp.int32, (blocks, blocks), 0)
    cols = lax.broadcasted_iota(jnp.int32, (blocks, blocks), 1)
    tiles = lax.broadcasted_iota(jnp.int32, (n, blocks), 0)
    lanes = lax.broadcasted_iota(jnp.int32, (blocks, BLK), 1)
    slot_row = slots[...]
    dest_row = targets[...]
    table[...] = jnp.zeros_like(table)
    table[0:1, :] = slot_row.astype(f32)
    table[1:2, :] = dest_row.astype(f32)
    table[2:4, 0:n] = requests[...].astype(f32)
    turned = table[...].T
    slot_col = turned[:, 0:1].astype(jnp.int32)
    dest_col = turned[:, 1:2].astype(jnp.int32)
    same_slot = jnp.where((slot_col == slot_row) & (rows < cols), 1.0, 0.0)
    slot_rank = jnp.sum(same_slot, axis=0, keepdims=True).astype(jnp.int32)
    same_dest = jnp.where((dest_col == dest_row) & (rows < cols), 1.0, 0.0)
    dest_rank = jnp.sum(same_dest, axis=0, keepdims=True).astype(jnp.int32)
    entry = (slot_row & 1) * room + slot_rank
    places[0:1, :] = (((slot_row >> 1) * back_rows + (entry >> 1)) << 1) | (entry & 1)
    places[1:2, :] = dest_row * room + dest_rank

    words = chosen(
        chooser(slot_row * room + slot_rank, n * half),
        [
            code(positions[0], FULL / (BY - 1)),
            code(positions[1], FULL / (BX - 1)),
            code(positions[2], FULL / (LEV - 1)),
        ],
    )
    for c in range(3):
        sorted_spots[c] = words[:, c * BLK : (c + 1) * BLK]
    counts = product(bits((slot_row >> 1) == tiles), bits(lanes == (slot_col & 1)))
    asked = turned[0:n] if n < BLK else turned
    front = lanes[0:n]
    own_heads[...] = jnp.where((front == 2) | (front == 3), asked, counts).astype(jnp.int32)

    def address(t, carry):
        for c in range(3):
            msg[pl.ds(t * spot_rows + c * half, half), :] = sorted_spots[c, pl.ds(t * half, half), :]
        msg[pl.ds(t * spot_rows + 3 * half, 1), :] = own_heads[pl.ds(t, 1), :]
        return carry

    lax.fori_loop(0, n, address, 0, unroll=8)
    mail.meet()
    parcel = (msg, spots, spot_rows, 3 * half + 1, send, recv)
    mail.post(*parcel)

    picks = chooser(dest_row * room + dest_rank, n * few)
    for s in range(0, S, 2):
        words = chosen(picks, [code(mass[:, s + i, :], FULL) for i in range(2)])
        for i in range(2):
            sorted_mass[s + i] = words[:, i * BLK : (i + 1) * BLK]
    sorted_mass[S] = chosen(picks, [keys[...]])
    before = bits((dest_col == dest_row) & (cols < rows))
    rank_col = product(before, jnp.ones((blocks, BLK), jnp.bfloat16)).astype(jnp.int32)
    homes = jnp.where(lanes == rank_col, (keys[...] >> 7).astype(f32), 0.0)
    homes = jnp.where(lanes == room, 1.0, homes).astype(jnp.bfloat16)
    sorted_mass[S + 1, 0:n, :] = product(bits(dest_row == tiles), homes).astype(jnp.int32)

    def wrap(t, carry):
        for s in range(S + 1):
            mass_msg[pl.ds(t * mass_rows + s * few, few), :] = sorted_mass[s, pl.ds(t * few, few), :]
        mass_msg[pl.ds(t * mass_rows + (S + 1) * few, 1), :] = sorted_mass[S + 1, pl.ds(t, 1), :]
        return carry

    lax.fori_loop(0, n, wrap, 0, unroll=4)
    mail.collect(*parcel)
    for o in range(n):
        heads[o : o + 1, :] = spots[o * spot_rows + 3 * half : o * spot_rows + 3 * half + 1, :]
    mail.settle(*parcel)


def list_pairs(n, room, head, todo, group):
    def source(o, at):
        for k in range(2):
            def put(i, at, base=o * 256 + k * (room // 2)):
                todo[at] = base + i
                return at + 1

            at = lax.fori_loop(0, (head[o, k] + 1) >> 1, put, at)
        return at

    total = lax.fori_loop(0, n, source, 0)
    for j in range(group - 1):
        todo[total + j] = 0
    return total


def wind_kernel(dims, head, spots, tiles, back, todo):
    n, room, spot_rows, back_rows = dims
    half = Q * room // 2
    total = list_pairs(n, room, head, todo, GROUP)
    levels = lax.broadcasted_iota(jnp.int32, (LEV, BLK), 0).astype(jnp.float32)
    cols = lax.broadcasted_iota(jnp.int32, (BX, BLK), 0).astype(jnp.float32)

    def weights(y, x):
        y = y * ((BY - 1) / FULL)
        x = x * ((BX - 1) / FULL)
        hx = hat(x - cols)
        flat = jnp.concatenate([hat(y - float(i)) * hx for i in range(BY)], axis=0)
        flat_hi = flat.astype(jnp.bfloat16)
        flat_lo = (flat - flat_hi.astype(jnp.float32)).astype(jnp.bfloat16)
        return jnp.concatenate([flat_hi, flat_lo], axis=0)

    def pair(o, k):
        base = o * spot_rows + k
        ys = spots[pl.ds(base, 1), :]
        xs = spots[pl.ds(base + half, 1), :]
        zs = spots[pl.ds(base + 2 * half, 1), :]
        block = tiles[head[o, 2 + k // (room // 2)]]
        seen = product(
            jnp.concatenate([block, block], axis=1),
            jnp.concatenate([weights(low(ys), low(xs)), weights(high(ys), high(xs))], axis=1),
        )
        codes = []
        for i, z in enumerate((low(zs), high(zs))):
            wz = hat(z * ((LEV - 1) / FULL) - levels).astype(jnp.bfloat16).astype(jnp.float32)
            for c in range(3):
                part = seen[c * LEV : (c + 1) * LEV, i * BLK : (i + 1) * BLK]
                wind = jnp.sum(part * wz, axis=0, keepdims=True)
                codes.append(code(wind + GUST, FULL / (2 * GUST)))
        return [codes[c] | (codes[3 + c] << 16) for c in range(3)]

    def several(i, carry):
        results = []
        for j in range(GROUP):
            item = todo[i * GROUP + j]
            o = item >> 8
            k = item & 255
            results.append((o * back_rows + k, pair(o, k)))
        for base, words in results:
            for c in range(3):
                back[pl.ds(base + c * half, 1), :] = words[c]
        return carry

    lax.fori_loop(0, (total + GROUP - 1) // GROUP, several, 0)


def move_kernel(
    dims, place, places, back, mass_msg, positions, velocity, increments,
    moved, turbulence, shares, heights, heads,
    winds, z_msg, found, sorted_z, sems,
):
    n_lat, n_lon, blocks, room, back_rows, mass_rows, z_rows = dims
    mail = Mail(n_lat, n_lon)
    mail.greet()
    n = mail.n
    half = Q * room // 2
    few = room // 2
    for c in range(3):
        turbulence[c] = DECAY * velocity[c] + KICK * increments[c]
    back_parcel = (back, winds, back_rows, 3 * half, sems.at[0], sems.at[1])
    mass_parcel = (mass_msg, shares, mass_rows, (S + 1) * few + 1, sems.at[2], sems.at[3])
    z_parcel = (z_msg, heights, z_rows, few, sems.at[4], sems.at[5])
    mail.meet()
    mail.post(*back_parcel)
    mail.post(*mass_parcel)
    picks = chooser(places[1:2, :], n * few)
    mail.collect(*back_parcel)

    def fetch(b, carry):
        spot = place[0, b]
        row = spot >> 1
        odd = 16 * (spot & 1)
        for c in range(3):
            word = winds[pl.ds(row + c * half, 1), :]
            found[c, pl.ds(b, 1), :] = lax.shift_right_logical(word, jnp.full_like(word, odd))
        return carry

    lax.fori_loop(0, blocks, fetch, 0, unroll=8)
    for c, top in enumerate((BY - 1.0, BX - 1.0, LEV - 1.0)):
        wind = low(found[c]) * (2 * GUST / FULL) - GUST
        moved[c] = jnp.clip(positions[c] + STEP * (wind + turbulence[c]), 0.0, top)
    sorted_z[...] = chosen(picks, [code(moved[2], FULL / (LEV - 1))])

    def wrap(t, carry):
        z_msg[pl.ds(t * z_rows, few), :] = sorted_z[pl.ds(t * few, few), :]
        return carry

    lax.fori_loop(0, n, wrap, 0, unroll=8)
    mail.post(*z_parcel)
    mail.collect(*mass_parcel)
    for o in range(n):
        row = o * mass_rows + (S + 1) * few
        heads[o : o + 1, :] = shares[row : row + 1, :]
    mail.collect(*z_parcel)
    for parcel in (back_parcel, mass_parcel, z_parcel):
        mail.settle(*parcel)


def deposit_kernel(dims, head, heights, shares, out, todo, filled):
    n, room, mass_rows, z_rows = dims
    most = n * room
    few = room // 2

    def clear(h, carry):
        filled[h] = 0
        return carry

    lax.fori_loop(0, MB, clear, 0)

    def source(o, carry):
        def put(q, carry):
            h = head[o, q]
            at = filled[h]
            todo[h * most + at] = (o << 8) | q
            filled[h] = at + 1
            return carry

        return lax.fori_loop(0, head[o, room], put, carry)

    lax.fori_loop(0, n, source, 0)
    levels = lax.broadcasted_iota(jnp.int32, (LEV, BLK), 0).astype(jnp.float32)
    cells = lax.broadcasted_iota(jnp.int32, (MBC, BLK), 0)

    def spread(h, at):
        valid = at < filled[h]
        item = jnp.where(valid, todo[h * most + at], 0)
        o = item >> 8
        q = item & 255
        base = o * mass_rows + (q >> 1)
        odd = 16 * (q & 1)

        def half_of(word):
            return lax.shift_right_logical(word, jnp.full_like(word, odd))

        key = half_of(shares[pl.ds(base + S * few, 1), :])
        inside = (key & (MBC - 1)) + jnp.where(valid, 0, MBC)
        z = low(half_of(heights[pl.ds(o * z_rows + (q >> 1), 1), :])) * ((LEV - 1) / FULL)
        vert = hat(z - levels)
        parts = low(half_of(shares[pl.ds(base, S, stride=few), :])) * (1 / FULL)
        weights = jnp.concatenate([parts[s : s + 1] * vert for s in range(S)], axis=0)
        return weights.astype(jnp.bfloat16), bits(inside == cells)

    def home(h, carry):
        out[h] = jnp.zeros((S * LEV, MBC), jnp.float32)

        def several(i, carry):
            parts = [spread(h, i * BUNCH + j) for j in range(BUNCH)]
            out[h] += lax.dot_general(
                jnp.concatenate([w for w, _ in parts], axis=1),
                jnp.concatenate([p for _, p in parts], axis=1),
                (((1,), (1,)), ((), ())),
                preferred_element_type=jnp.float32,
            )
            return carry

        return lax.fori_loop(0, (filled[h] + BUNCH - 1) // BUNCH, several, carry)

    lax.fori_loop(0, MB, home, 0)


def body(
    winds, positions, velocity, increments, mass, requests, block_slots, destinations, cell_keys
):
    n_lat = lax.axis_size("lat")
    n_lon = lax.axis_size("lon")
    n = n_lat * n_lon
    blocks = positions.shape[0]
    room = 2 * blocks // n
    half = Q * room // 2
    few = room // 2
    spot_rows = up8(3 * half + 1)
    back_rows = up8(3 * half)
    mass_rows = up8((S + 1) * few + 1)
    z_rows = up8(few)
    i32 = jnp.int32
    f32 = jnp.float32
    like = jax.ShapeDtypeStruct
    dma = pltpu.SemaphoreType.DMA

    positions, velocity, increments = (
        each.transpose(1, 0, 2) for each in (positions, velocity, increments)
    )
    spots, heads, mass_msg, places = pl.pallas_call(
        functools.partial(
            send_kernel, (n_lat, n_lon, blocks, room, spot_rows, back_rows, mass_rows)
        ),
        out_shape=(
            like((n * spot_rows, BLK), i32),
            like((n, BLK), i32),
            like((n * mass_rows, BLK), i32),
            like((8, blocks), i32),
        ),
        in_specs=[VMEM] * 6,
        out_specs=(VMEM,) * 4,
        scratch_shapes=[
            pltpu.VMEM((n * spot_rows, BLK), i32),
            pltpu.VMEM((BLK, BLK), f32),
            pltpu.VMEM((3, n * half, BLK), i32),
            pltpu.VMEM((S + 2, n * few, BLK), i32),
            pltpu.VMEM((n, BLK), i32),
            dma((n,)),
            dma((n,)),
        ],
        compiler_params=pltpu.CompilerParams(collective_id=0, has_side_effects=True),
        name="send",
    )(
        block_slots.reshape(1, -1), destinations.reshape(1, -1), requests[0].T,
        positions, mass, cell_keys,
    )
    back = pl.pallas_call(
        functools.partial(wind_kernel, (n, room, spot_rows, back_rows)),
        out_shape=like((n * back_rows, BLK), i32),
        in_specs=[SMEM, VMEM, VMEM],
        out_specs=VMEM,
        scratch_shapes=[pltpu.SMEM((n * half + GROUP,), i32)],
        name="wind",
    )(heads, spots, winds.reshape(MB, 3 * LEV, MBC))
    moved, turbulence, shares, heights, landed = pl.pallas_call(
        functools.partial(
            move_kernel, (n_lat, n_lon, blocks, room, back_rows, mass_rows, z_rows)
        ),
        out_shape=(
            like(positions.shape, f32),
            like(positions.shape, f32),
            like((n * mass_rows, BLK), i32),
            like((n * z_rows, BLK), i32),
            like((n, BLK), i32),
        ),
        in_specs=[SMEM] + [VMEM] * 6,
        out_specs=(VMEM,) * 5,
        scratch_shapes=[
            pltpu.VMEM((n * back_rows, BLK), i32),
            pltpu.VMEM((n * z_rows, BLK), i32),
            pltpu.VMEM((3, blocks, BLK), i32),
            pltpu.VMEM((n * few, BLK), i32),
            dma((6, n)),
        ],
        compiler_params=pltpu.CompilerParams(collective_id=1, has_side_effects=True),
        name="move",
    )(places, places, back, mass_msg, positions, velocity, increments)
    total = pl.pallas_call(
        functools.partial(deposit_kernel, (n, room, mass_rows, z_rows)),
        out_shape=like((MB, S * LEV, MBC), f32),
        in_specs=[SMEM, VMEM, VMEM],
        out_specs=VMEM,
        scratch_shapes=[
            pltpu.SMEM((MB * n * room + BUNCH,), i32),
            pltpu.SMEM((MB,), i32),
        ],
        name="deposit",
    )(landed, heights, shares)
    concentration = total.reshape(MBR, MBK, S, LEV, MBC)
    return (moved.transpose(1, 0, 2), turbulence.transpose(1, 0, 2), concentration)


def solution(mesh):
    rows = ("lat", "lon")
    in_specs = (
        P("lat", "lon", None, None, None),
        P(rows, None, None),
        P(rows, None, None),
        P(rows, None, None),
        P(rows, None, None),
        P(rows, None, None),
        P(rows, None),
        P(rows, None),
        P(rows, None),
    )
    out_specs = (
        P(rows, None, None),
        P(rows, None, None),
        P("lat", "lon", None, None, None),
    )
    return jax.shard_map(body, mesh=mesh, in_specs=in_specs, out_specs=out_specs, check_vma=False)
```

```python
import functools

import jax
import jax.numpy as jnp
from jax import lax
from jax.experimental import pallas as pl
from jax.experimental.pallas import tpu as pltpu
from jax.sharding import PartitionSpec as P

BY = 8
BX = 16
MBC = 128
LEV = 40
S = 8
BLK = 128
MBR = 4
MBK = 4
Q = 2
MB = MBR * MBK

DECAY = 0.8
KICK = 0.6
STEP = 0.5

FULL = 65535.0
GUST = 6.1
BUNCH = 4
SHIFT = 64
VMEM = pl.BlockSpec(memory_space=pltpu.VMEM)
SMEM = pl.BlockSpec(memory_space=pltpu.SMEM)


def up8(rows):
    return -(-rows // 8) * 8


def hat(offset):
    return jnp.maximum(0.0, 1.0 - jnp.abs(offset))


def low(word):
    return (word & 0xFFFF).astype(jnp.float32)


def high(word):
    return lax.shift_right_logical(word, 16).astype(jnp.float32)


def code(value, scale):
    return (value * scale + 0.5).astype(jnp.int32)


def aligned(start):
    return pl.multiple_of(start, 8)


def bits(mask):
    return jnp.where(mask, 1.0, 0.0).astype(jnp.bfloat16)


def halves(value):
    top = (value >> 8).astype(jnp.float32).astype(jnp.bfloat16)
    return top, (value & 255).astype(jnp.float32).astype(jnp.bfloat16)


def product(left, right):
    return jnp.dot(left, right, preferred_element_type=jnp.float32)


def chooser(place, pairs):
    index = lax.broadcasted_iota(jnp.int32, (pairs, place.shape[1]), 0)
    picks = jnp.concatenate(
        [jnp.where(place == 2 * index + odd, 1.0, 0.0) for odd in range(2)], axis=0
    )
    return jnp.concatenate([picks * 256.0, picks], axis=1).astype(jnp.bfloat16)


def chosen(picks, values):
    pairs = picks.shape[0] // 2
    parts = [halves(value) for value in values]
    data = jnp.concatenate(
        [
            jnp.concatenate([top for top, _ in parts], axis=1),
            jnp.concatenate([rest for _, rest in parts], axis=1),
        ],
        axis=0,
    )
    found = product(picks, data).astype(jnp.int32)
    return found[:pairs] | (found[pairs:] << 16)


class Mail:
    def __init__(self, n_lat, n_lon):
        self.n_lat, self.n_lon = n_lat, n_lon
        self.n = n_lat * n_lon
        self.lat = lax.axis_index("lat")
        self.lon = lax.axis_index("lon")
        self.me = self.lat * n_lon + self.lon

    def split(self, i):
        if isinstance(i, int):
            return i // self.n_lon, i % self.n_lon
        return lax.div(i, self.n_lon), lax.rem(i, self.n_lon)

    def device(self, i):
        k, j = self.split(i)
        return lax.rem(self.lat + k, self.n_lat), lax.rem(self.lon + j, self.n_lon)

    def origin(self, i):
        k, j = self.split(i)
        return (
            lax.rem(self.lat - k + self.n_lat, self.n_lat),
            lax.rem(self.lon - j + self.n_lon, self.n_lon),
        )

    def number(self, device):
        return device[0] * self.n_lon + device[1]

    def greet(self):
        barrier = pltpu.get_barrier_semaphore()
        for i in range(1, self.n):
            pl.semaphore_signal(
                barrier, inc=1, device_id=self.device(i), device_id_type=pl.DeviceIdType.MESH
            )

    def meet(self):
        pl.semaphore_wait(pltpu.get_barrier_semaphore(), self.n - 1)


class Parcel:
    def __init__(self, mail, src, dst, rows, used, send, recv):
        self.mail, self.src, self.dst = mail, src, dst
        self.rows, self.used = rows, used
        self.send, self.recv = send, recv

    def part(self, ref, t):
        return ref.at[pl.ds(aligned(t * self.rows), self.used)]

    def copy(self, i, back=False):
        mail = self.mail
        device = mail.origin(i) if back else mail.device(i)
        return pltpu.make_async_remote_copy(
            src_ref=self.part(self.src, mail.number(device)),
            dst_ref=self.part(self.dst, mail.me),
            send_sem=self.send.at[i], recv_sem=self.recv.at[i],
            device_id=device, device_id_type=pl.DeviceIdType.MESH,
        )

    def own(self):
        me = self.mail.me
        return pltpu.make_async_copy(
            self.part(self.src, me), self.part(self.dst, me), self.send.at[0]
        )

    def post(self, order):
        for i in order:
            self.copy(i).start()
        self.own().start()

    def collect(self, back=False):
        self.own().wait()
        for i in range(1, self.mail.n):
            self.copy(i, back).wait_recv()

    def settle(self, back=False):
        for i in range(1, self.mail.n):
            self.copy(i, back).wait_send()


def advect_kernel(
    dims, slots, targets, requests, positions, velocity, increments, mass, keys, tiles,
    moved, turbulence, heights, shares, heads,
    spot_msg, spots, back_msg, winds, mass_msg, z_msg,
    table, places, sorted_spots, sorted_mass, own_heads, scaled, parts, found, sorted_z,
    asked_of, place, spot_sems, back_sems, mass_sems, z_sems, local,
):
    n_lat, n_lon, blocks, room, spot_rows, back_rows, mass_rows, z_rows = dims
    mail = Mail(n_lat, n_lon)
    mail.greet()
    n = mail.n
    entries = Q * room
    half = entries // 2
    few = room // 2
    f32 = jnp.float32
    bf16 = jnp.bfloat16
    rows = lax.broadcasted_iota(jnp.int32, (blocks, blocks), 0)
    cols = lax.broadcasted_iota(jnp.int32, (blocks, blocks), 1)
    tile_ids = lax.broadcasted_iota(jnp.int32, (n, blocks), 0)
    lanes = lax.broadcasted_iota(jnp.int32, (blocks, BLK), 1)
    slot_row = slots[...]
    dest_row = targets[...]
    table[...] = jnp.zeros_like(table)
    table[0:1, :] = slot_row.astype(f32)
    table[1:2, :] = dest_row.astype(f32)
    table[2:4, 0:n] = requests[...].astype(f32)
    turned = table[...].T
    slot_col = turned[:, 0:1].astype(jnp.int32)
    dest_col = turned[:, 1:2].astype(jnp.int32)
    same_slot = jnp.where((slot_col == slot_row) & (rows < cols), 1.0, 0.0)
    slot_rank = jnp.sum(same_slot, axis=0, keepdims=True).astype(jnp.int32)
    same_dest = jnp.where((dest_col == dest_row) & (rows < cols), 1.0, 0.0)
    dest_rank = jnp.sum(same_dest, axis=0, keepdims=True).astype(jnp.int32)
    entry = (slot_row & 1) * room + slot_rank
    places[...] = jnp.zeros_like(places)
    places[0:1, :] = (((slot_row >> 1) * back_rows + (entry >> 1)) << 1) | (entry & 1)

    words = chosen(
        chooser(slot_row * room + slot_rank, n * half),
        [
            code(positions[0], FULL / (BY - 1)),
            code(positions[1], FULL / (BX - 1)),
            code(positions[2], FULL / (LEV - 1)),
        ],
    )
    for c in range(3):
        sorted_spots[c] = words[:, c * BLK : (c + 1) * BLK]
    counts = product(bits((slot_row >> 1) == tile_ids), bits(lanes == (slot_col & 1)))
    asked = turned[0:n] if n < BLK else turned
    front = lanes[0:n]
    before = bits((dest_col == dest_row) & (cols < rows))
    rank_col = product(before, jnp.ones((blocks, BLK), bf16)).astype(jnp.int32)
    homes = jnp.where(lanes == SHIFT + rank_col, (keys[...] >> 7).astype(f32), 0.0)
    homes = jnp.where(lanes == SHIFT + room, 1.0, homes).astype(bf16)
    landing = product(bits(dest_row == tile_ids), homes)
    counts = jnp.where((front == 2) | (front == 3), asked, counts)
    own_heads[...] = (counts + landing).astype(jnp.int32)

    def address(t, carry):
        for c in range(3):
            spot_msg[pl.ds(t * spot_rows + c * half, half), :] = sorted_spots[
                c, pl.ds(t * half, half), :
            ]
        spot_msg[pl.ds(t * spot_rows + 3 * half, 1), :] = own_heads[pl.ds(t, 1), :]
        return carry

    lax.fori_loop(0, n, address, 0, unroll=8)
    spot_mail = Parcel(
        mail, spot_msg, spots, spot_rows, 3 * half + 1, spot_sems.at[0], spot_sems.at[1]
    )
    back_mail = Parcel(mail, back_msg, winds, back_rows, 3 * half, back_sems.at[0], back_sems.at[1])
    mass_mail = Parcel(
        mail, mass_msg, shares, mass_rows, (S + 1) * few, mass_sems.at[0], mass_sems.at[1]
    )
    z_mail = Parcel(mail, z_msg, heights, z_rows, few, z_sems.at[0], z_sems.at[1])
    order = list(range(1, n))
    mail.meet()
    spot_mail.post(order)
    placing = pltpu.make_async_copy(places, place, local.at[1])
    placing.start()

    dest_place = dest_row * room + dest_rank
    picks = chooser(dest_place, n * few)
    for s in range(0, S, 2):
        words = chosen(picks, [code(mass[:, s + i, :], FULL) for i in range(2)])
        for i in range(2):
            sorted_mass[s + i] = words[:, i * BLK : (i + 1) * BLK]
    sorted_mass[S] = chosen(picks, [keys[...]])

    def wrap_mass(t, carry):
        for s in range(S + 1):
            mass_msg[pl.ds(t * mass_rows + s * few, few), :] = sorted_mass[s, pl.ds(t * few, few), :]
        return carry

    lax.fori_loop(0, n, wrap_mass, 0, unroll=4)
    mass_mail.post(order)
    for c in range(3):
        turbulence[c] = DECAY * velocity[c] + KICK * increments[c]

    levels = lax.broadcasted_iota(jnp.int32, (LEV, BLK), 0).astype(f32)
    xs_at = lax.broadcasted_iota(jnp.int32, (BX, BLK), 0).astype(f32)
    ys_at = lax.broadcasted_iota(jnp.int32, (BY, BLK), 0).astype(f32)

    def asking(i):
        row = mail.number(mail.origin(i)) * spot_rows + 3 * half
        return pltpu.make_async_copy(
            spots.at[pl.ds(aligned(row) if half % 8 == 0 else row, 1)], asked_of, local.at[0]
        )

    def weights(y, x):
        hy = hat(y - ys_at)
        hx = hat(x - xs_at)
        flat = jnp.concatenate([hy[i : i + 1] * hx for i in range(BY)], axis=0)
        flat_hi = flat.astype(bf16)
        flat_lo = (flat - flat_hi.astype(f32)).astype(bf16)
        return jnp.concatenate([flat_hi, flat_lo], axis=0)

    def interpolate(i, mets):
        o = mail.number(mail.origin(i))
        base = o * spot_rows
        for c, top in enumerate((BY - 1, BX - 1, LEV - 1)):
            word = spots[pl.ds(base + c * half, half), :]
            scaled[c] = low(word) * (top / FULL)
            scaled[3 + c] = high(word) * (top / FULL)
        for k in range(half):
            block = tiles[mets[k // few]]
            seen = product(
                jnp.concatenate([block, block], axis=1),
                jnp.concatenate(
                    [
                        weights(scaled[3 * side, k : k + 1, :], scaled[3 * side + 1, k : k + 1, :])
                        for side in range(2)
                    ],
                    axis=1,
                ),
            )
            for side in range(2):
                wz = hat(scaled[3 * side + 2, k : k + 1, :] - levels).astype(bf16).astype(f32)
                for c in range(3):
                    part = seen[c * LEV : (c + 1) * LEV, side * BLK : (side + 1) * BLK] * wz
                    total = part[0:8]
                    for v in range(8, LEV, 8):
                        total = total + part[v : v + 8]
                    parts[3 * side + c, 8 * k : 8 * k + 8, :] = total
        for c in range(3):
            codes = []
            for side in range(2):
                wind = parts[3 * side + c, pl.ds(0, half, stride=8), :]
                for v in range(1, 8):
                    wind = wind + parts[3 * side + c, pl.ds(v, half, stride=8), :]
                codes.append(code(wind + GUST, FULL / (2 * GUST)))
            back_msg[pl.ds(o * back_rows + c * half, half), :] = codes[0] | (codes[1] << 16)

    spot_mail.own().wait()
    asking(0).start()
    asking(0).wait()

    def serve(i, carry):
        mets = [jnp.clip(asked_of[0, 2 + k], 0, MB - 1) for k in range(Q)]

        @pl.when(i + 1 < n)
        def _():
            spot_mail.copy(i + 1).wait_recv()
            asking(i + 1).start()

        interpolate(i, mets)

        @pl.when(i > 0)
        def _():
            back_mail.copy(i, back=True).start()

        @pl.when(i == 0)
        def _():
            back_mail.own().start()

        @pl.when(i + 1 < n)
        def _():
            asking(i + 1).wait()

        return carry

    lax.fori_loop(0, n, serve, 0)
    placing.wait()
    back_mail.collect()

    def fetch(b, carry):
        spot = place[0, b]
        row = jnp.clip(spot >> 1, 0, n * back_rows - 2 * half - 1)
        odd = 16 * (spot & 1)
        for c in range(3):
            word = winds[pl.ds(row + c * half, 1), :]
            found[c, pl.ds(b, 1), :] = lax.shift_right_logical(word, jnp.full_like(word, odd))
        return carry

    lax.fori_loop(0, blocks, fetch, 0, unroll=8)
    for c, top in enumerate((BY - 1.0, BX - 1.0, LEV - 1.0)):
        wind = low(found[c]) * (2 * GUST / FULL) - GUST
        moved[c] = jnp.clip(positions[c] + STEP * (wind + turbulence[c]), 0.0, top)
    sorted_z[...] = chosen(picks, [code(moved[2], FULL / (LEV - 1))])

    def wrap(t, carry):
        z_msg[pl.ds(t * z_rows, few), :] = sorted_z[pl.ds(t * few, few), :]
        return carry

    lax.fori_loop(0, n, wrap, 0, unroll=8)
    z_mail.post(order)
    for o in range(n):
        row = o * spot_rows + 3 * half
        heads[o : o + 1, :] = spots[row : row + 1, :]
    z_mail.collect()
    mass_mail.collect()
    spot_mail.settle()
    back_mail.settle()
    mass_mail.settle()
    z_mail.settle()


def deposit_kernel(dims, head, heights, mass, out, shares, todo, filled, landed):
    n, room, mass_rows, z_rows = dims
    most = n * room
    few = room // 2
    load = pltpu.make_async_copy(mass, shares, landed)
    load.start()

    def clear(h, carry):
        filled[h] = 0
        return carry

    lax.fori_loop(0, MB, clear, 0)

    def source(o, carry):
        def put(q, carry):
            h = head[o, SHIFT + q]
            at = filled[h]
            todo[h * most + at] = (o << 8) | q
            filled[h] = at + 1
            return carry

        return lax.fori_loop(0, head[o, SHIFT + room], put, carry)

    lax.fori_loop(0, n, source, 0)
    load.wait()
    levels = lax.broadcasted_iota(jnp.int32, (LEV, BLK), 0).astype(jnp.float32)
    cells = lax.broadcasted_iota(jnp.int32, (MBC, BLK), 0)

    def spread(h, at):
        valid = at < filled[h]
        item = jnp.where(valid, todo[h * most + at], 0)
        o = item >> 8
        q = item & 255
        base = o * mass_rows + (q >> 1)
        odd = 16 * (q & 1)

        def half_of(word):
            return lax.shift_right_logical(word, jnp.full_like(word, odd))

        key = half_of(shares[pl.ds(base + S * few, 1), :])
        inside = (key & (MBC - 1)) + jnp.where(valid, 0, MBC)
        z = low(half_of(heights[pl.ds(o * z_rows + (q >> 1), 1), :])) * ((LEV - 1) / FULL)
        vert = hat(z - levels)
        parts = low(half_of(shares[pl.ds(base, S, stride=few), :])) * (1 / FULL)
        weights = jnp.concatenate([parts[s : s + 1] * vert for s in range(S)], axis=0)
        return weights.astype(jnp.bfloat16), bits(inside == cells)

    def home(h, carry):
        out[h] = jnp.zeros((S * LEV, MBC), jnp.float32)

        def several(i, carry):
            parts = [spread(h, i * BUNCH + j) for j in range(BUNCH)]
            out[h] += lax.dot_general(
                jnp.concatenate([w for w, _ in parts], axis=1),
                jnp.concatenate([p for _, p in parts], axis=1),
                (((1,), (1,)), ((), ())),
                preferred_element_type=jnp.float32,
            )
            return carry

        return lax.fori_loop(0, (filled[h] + BUNCH - 1) // BUNCH, several, carry)

    lax.fori_loop(0, MB, home, 0)


def body(
    winds, positions, velocity, increments, mass, requests, block_slots, destinations, cell_keys
):
    n_lat = lax.axis_size("lat")
    n_lon = lax.axis_size("lon")
    n = n_lat * n_lon
    blocks = positions.shape[0]
    room = 2 * blocks // n
    half = Q * room // 2
    few = room // 2
    spot_rows = up8(3 * half + 1)
    back_rows = up8(3 * half)
    mass_rows = up8((S + 1) * few)
    z_rows = up8(few)
    i32 = jnp.int32
    f32 = jnp.float32
    like = jax.ShapeDtypeStruct
    dma = pltpu.SemaphoreType.DMA

    positions, velocity, increments = (
        each.transpose(1, 0, 2) for each in (positions, velocity, increments)
    )
    moved, turbulence, heights, shares, heads = pl.pallas_call(
        functools.partial(
            advect_kernel,
            (n_lat, n_lon, blocks, room, spot_rows, back_rows, mass_rows, z_rows),
        ),
        out_shape=(
            like(positions.shape, f32),
            like(positions.shape, f32),
            like((n * z_rows, BLK), i32),
            like((n * mass_rows, BLK), i32),
            like((n, BLK), i32),
        ),
        in_specs=[VMEM] * 9,
        out_specs=(VMEM,) * 5,
        scratch_shapes=[
            pltpu.VMEM((n * spot_rows, BLK), i32),
            pltpu.VMEM((n * spot_rows, BLK), i32),
            pltpu.VMEM((n * back_rows, BLK), i32),
            pltpu.VMEM((n * back_rows, BLK), i32),
            pltpu.VMEM((n * mass_rows, BLK), i32),
            pltpu.VMEM((n * z_rows, BLK), i32),
            pltpu.VMEM((BLK, BLK), f32),
            pltpu.VMEM((8, blocks), i32),
            pltpu.VMEM((3, n * half, BLK), i32),
            pltpu.VMEM((S + 1, n * few, BLK), i32),
            pltpu.VMEM((n, BLK), i32),
            pltpu.VMEM((6, half, BLK), f32),
            pltpu.VMEM((6, 8 * half, BLK), f32),
            pltpu.VMEM((3, blocks, BLK), i32),
            pltpu.VMEM((n * few, BLK), i32),
            pltpu.SMEM((1, BLK), i32),
            pltpu.SMEM((8, blocks), i32),
            dma((2, n)),
            dma((2, n)),
            dma((2, n)),
            dma((2, n)),
            dma((2,)),
        ],
        compiler_params=pltpu.CompilerParams(collective_id=0, has_side_effects=True),
        name="advect",
    )(
        block_slots.reshape(1, -1), destinations.reshape(1, -1), requests[0].T,
        positions, velocity, increments, mass, cell_keys, winds.reshape(MB, 3 * LEV, MBC),
    )
    total = pl.pallas_call(
        functools.partial(deposit_kernel, (n, room, mass_rows, z_rows)),
        out_shape=like((MB, S * LEV, MBC), f32),
        in_specs=[SMEM, VMEM, pl.BlockSpec(memory_space=pl.ANY)],
        out_specs=VMEM,
        scratch_shapes=[
            pltpu.VMEM((n * mass_rows, BLK), i32),
            pltpu.SMEM((MB * n * room + BUNCH,), i32),
            pltpu.SMEM((MB,), i32),
            dma(()),
        ],
        name="deposit",
    )(heads, heights, shares)
    concentration = total.reshape(MBR, MBK, S, LEV, MBC)
    return (moved.transpose(1, 0, 2), turbulence.transpose(1, 0, 2), concentration)


def solution(mesh):
    rows = ("lat", "lon")
    in_specs = (
        P("lat", "lon", None, None, None),
        P(rows, None, None),
        P(rows, None, None),
        P(rows, None, None),
        P(rows, None, None),
        P(rows, None, None),
        P(rows, None),
        P(rows, None),
        P(rows, None),
    )
    out_specs = (
        P(rows, None, None),
        P(rows, None, None),
        P("lat", "lon", None, None, None),
    )
    return jax.shard_map(body, mesh=mesh, in_specs=in_specs, out_specs=out_specs, check_vma=False)
```

```python
import functools

import jax
import jax.numpy as jnp
from jax import lax
from jax.experimental import pallas as pl
from jax.experimental.pallas import tpu as pltpu
from jax.sharding import PartitionSpec as P

BY = 8
BX = 16
MBC = 128
LEV = 40
S = 8
BLK = 128
MBR = 4
MBK = 4
Q = 2
MB = MBR * MBK

DECAY = 0.8
KICK = 0.6
STEP = 0.5

FULL = 65535.0
GUST = 6.1
BUNCH = 4
SHIFT = 64
SPLIT = 16
SPAN = LEV - SPLIT
VMEM = pl.BlockSpec(memory_space=pltpu.VMEM)
SMEM = pl.BlockSpec(memory_space=pltpu.SMEM)


def up8(rows):
    return -(-rows // 8) * 8


def hat(offset):
    return jnp.maximum(0.0, 1.0 - jnp.abs(offset))


def low(word):
    return (word & 0xFFFF).astype(jnp.float32)


def high(word):
    return lax.shift_right_logical(word, 16).astype(jnp.float32)


def code(value, scale):
    return (value * scale + 0.5).astype(jnp.int32)


def aligned(start):
    return pl.multiple_of(start, 8)


def bits(mask):
    return jnp.where(mask, 1.0, 0.0).astype(jnp.bfloat16)


def halves(value):
    top = (value >> 8).astype(jnp.float32).astype(jnp.bfloat16)
    return top, (value & 255).astype(jnp.float32).astype(jnp.bfloat16)


def product(left, right):
    return jnp.dot(left, right, preferred_element_type=jnp.float32)


def chooser(place, pairs):
    index = lax.broadcasted_iota(jnp.int32, (pairs, place.shape[1]), 0)
    picks = jnp.concatenate(
        [jnp.where(place == 2 * index + odd, 1.0, 0.0) for odd in range(2)], axis=0
    )
    return jnp.concatenate([picks * 256.0, picks], axis=1).astype(jnp.bfloat16)


def chosen(picks, values):
    pairs = picks.shape[0] // 2
    parts = [halves(value) for value in values]
    data = jnp.concatenate(
        [
            jnp.concatenate([top for top, _ in parts], axis=1),
            jnp.concatenate([rest for _, rest in parts], axis=1),
        ],
        axis=0,
    )
    found = product(picks, data).astype(jnp.int32)
    return found[:pairs] | (found[pairs:] << 16)


class Mail:
    def __init__(self, n_lat, n_lon):
        self.n_lat, self.n_lon = n_lat, n_lon
        self.n = n_lat * n_lon
        self.lat = lax.axis_index("lat")
        self.lon = lax.axis_index("lon")
        self.me = self.lat * n_lon + self.lon

    def split(self, i):
        if isinstance(i, int):
            return i // self.n_lon, i % self.n_lon
        return lax.div(i, self.n_lon), lax.rem(i, self.n_lon)

    def device(self, i):
        k, j = self.split(i)
        return lax.rem(self.lat + k, self.n_lat), lax.rem(self.lon + j, self.n_lon)

    def origin(self, i):
        k, j = self.split(i)
        return (
            lax.rem(self.lat - k + self.n_lat, self.n_lat),
            lax.rem(self.lon - j + self.n_lon, self.n_lon),
        )

    def number(self, device):
        return device[0] * self.n_lon + device[1]

    def greet(self):
        barrier = pltpu.get_barrier_semaphore()
        for i in range(1, self.n):
            pl.semaphore_signal(
                barrier, inc=1, device_id=self.device(i), device_id_type=pl.DeviceIdType.MESH
            )

    def meet(self):
        pl.semaphore_wait(pltpu.get_barrier_semaphore(), self.n - 1)


class Parcel:
    def __init__(self, mail, src, dst, rows, used, send, recv):
        self.mail, self.src, self.dst = mail, src, dst
        self.rows, self.used = rows, used
        self.send, self.recv = send, recv

    def part(self, ref, t):
        return ref.at[pl.ds(aligned(t * self.rows), self.used)]

    def copy(self, i, back=False):
        mail = self.mail
        device = mail.origin(i) if back else mail.device(i)
        return pltpu.make_async_remote_copy(
            src_ref=self.part(self.src, mail.number(device)),
            dst_ref=self.part(self.dst, mail.me),
            send_sem=self.send.at[i], recv_sem=self.recv.at[i],
            device_id=device, device_id_type=pl.DeviceIdType.MESH,
        )

    def own(self):
        me = self.mail.me
        return pltpu.make_async_copy(
            self.part(self.src, me), self.part(self.dst, me), self.send.at[0]
        )

    def post(self, order):
        for i in order:
            self.copy(i).start()
        self.own().start()

    def collect(self, back=False):
        self.own().wait()
        for i in range(1, self.mail.n):
            self.copy(i, back).wait_recv()

    def settle(self, back=False):
        for i in range(1, self.mail.n):
            self.copy(i, back).wait_send()


def arrange(heads, room, plan):
    n = heads.shape[0]
    f32 = jnp.float32
    count = n * room
    spaces = plan.shape[1]
    tall = up8(MB + 1)

    def index(shape, dim):
        return lax.broadcasted_iota(jnp.int32, shape, dim)

    place = lax.rem(index((BLK, count), 1), room)
    spread = product(heads.astype(jnp.bfloat16), bits(index((BLK, count), 0) == place + SHIFT))
    entry = index((n, count), 1)
    mine = lax.div(entry, room) == index((n, count), 0)
    held = heads[:, SHIFT + room : SHIFT + room + 1]
    homes = jnp.where(lax.rem(entry, room).astype(f32) < held, spread, float(MB))
    homes = jnp.sum(jnp.where(mine, homes, 0.0), axis=0, keepdims=True).astype(jnp.int32)
    member = jnp.where(index((tall, count), 0) == homes, 1.0, 0.0)
    earlier = bits(index((count, count), 0) < index((count, count), 1))
    rank = product(member.astype(jnp.bfloat16), earlier)
    sizes = jnp.sum(member, axis=1, keepdims=True).astype(jnp.int32)
    sizes = (sizes + (BUNCH - 1)) // BUNCH * BUNCH
    sizes = jnp.where(index((tall, count), 0) < MB, sizes, 0)
    wide = sizes.astype(f32).astype(jnp.bfloat16)
    first = product(bits(index((tall, tall), 1) < index((tall, tall), 0)), wide)
    space = jnp.sum(member * (first + rank), axis=0, keepdims=True).astype(jnp.int32)
    space = jnp.where(homes < MB, space, -1)
    number = (index((8, count), 1) + 1).astype(f32).astype(jnp.bfloat16)
    found = lax.dot_general(
        number, bits(index((spaces, count), 0) == space),
        (((1,), (1,)), ((), ())), preferred_element_type=f32,
    )
    plan[...] = found.astype(jnp.int32)
    ends = first.astype(jnp.int32)[:MB, :BLK] + sizes[:MB, :BLK]
    over = jnp.where(ends <= BUNCH * index((MB, BLK), 1), 1, 0)
    plan[1:2, 0:BLK] = jnp.sum(over, axis=0, keepdims=True)
    plan[2:3, 0:BLK] = jnp.max(ends, axis=0, keepdims=True)


def advect_kernel(
    dims, slots, targets, requests, positions, velocity, increments, mass, keys, tiles,
    moved, turbulence, heights, shares, plan,
    spot_msg, spots, back_msg, winds, mass_msg, z_msg,
    table, places, sorted_spots, sorted_mass, own_heads, heads, scaled, parts, found, sorted_z,
    asked_of, place, spot_sems, back_sems, mass_sems, z_sems, local,
):
    n_lat, n_lon, blocks, room, spot_rows, back_rows, mass_rows, z_rows = dims
    mail = Mail(n_lat, n_lon)
    mail.greet()
    n = mail.n
    entries = Q * room
    half = entries // 2
    few = room // 2
    f32 = jnp.float32
    bf16 = jnp.bfloat16
    rows = lax.broadcasted_iota(jnp.int32, (blocks, blocks), 0)
    cols = lax.broadcasted_iota(jnp.int32, (blocks, blocks), 1)
    tile_ids = lax.broadcasted_iota(jnp.int32, (n, blocks), 0)
    lanes = lax.broadcasted_iota(jnp.int32, (blocks, BLK), 1)
    slot_row = slots[...]
    dest_row = targets[...]
    table[...] = jnp.zeros_like(table)
    table[0:1, :] = slot_row.astype(f32)
    table[1:2, :] = dest_row.astype(f32)
    table[2:4, 0:n] = requests[...].astype(f32)
    turned = table[...].T
    slot_col = turned[:, 0:1].astype(jnp.int32)
    dest_col = turned[:, 1:2].astype(jnp.int32)
    same_slot = jnp.where((slot_col == slot_row) & (rows < cols), 1.0, 0.0)
    slot_rank = jnp.sum(same_slot, axis=0, keepdims=True).astype(jnp.int32)
    same_dest = jnp.where((dest_col == dest_row) & (rows < cols), 1.0, 0.0)
    dest_rank = jnp.sum(same_dest, axis=0, keepdims=True).astype(jnp.int32)
    entry = (slot_row & 1) * room + slot_rank
    places[...] = jnp.zeros_like(places)
    places[0:1, :] = (((slot_row >> 1) * back_rows + (entry >> 1)) << 1) | (entry & 1)

    words = chosen(
        chooser(slot_row * room + slot_rank, n * half),
        [
            code(positions[0], FULL / (BY - 1)),
            code(positions[1], FULL / (BX - 1)),
            code(positions[2], FULL / (LEV - 1)),
        ],
    )
    for c in range(3):
        sorted_spots[c] = words[:, c * BLK : (c + 1) * BLK]
    counts = product(bits((slot_row >> 1) == tile_ids), bits(lanes == (slot_col & 1)))
    asked = turned[0:n] if n < BLK else turned
    front = lanes[0:n]
    before = bits((dest_col == dest_row) & (cols < rows))
    rank_col = product(before, jnp.ones((blocks, BLK), bf16)).astype(jnp.int32)
    homes = jnp.where(lanes == SHIFT + rank_col, (keys[...] >> 7).astype(f32), 0.0)
    homes = jnp.where(lanes == SHIFT + room, 1.0, homes).astype(bf16)
    landing = product(bits(dest_row == tile_ids), homes)
    counts = jnp.where((front == 2) | (front == 3), asked, counts)
    own_heads[...] = (counts + landing).astype(jnp.int32)

    def address(t, carry):
        for c in range(3):
            spot_msg[pl.ds(t * spot_rows + c * half, half), :] = sorted_spots[
                c, pl.ds(t * half, half), :
            ]
        spot_msg[pl.ds(t * spot_rows + 3 * half, 1), :] = own_heads[pl.ds(t, 1), :]
        return carry

    lax.fori_loop(0, n, address, 0, unroll=8)
    spot_mail = Parcel(
        mail, spot_msg, spots, spot_rows, 3 * half + 1, spot_sems.at[0], spot_sems.at[1]
    )
    back_mail = Parcel(mail, back_msg, winds, back_rows, 3 * half, back_sems.at[0], back_sems.at[1])
    mass_mail = Parcel(
        mail, mass_msg, shares, mass_rows, (S + 1) * few, mass_sems.at[0], mass_sems.at[1]
    )
    z_mail = Parcel(mail, z_msg, heights, z_rows, few, z_sems.at[0], z_sems.at[1])
    order = list(range(1, n))
    mail.meet()
    spot_mail.post(order)
    placing = pltpu.make_async_copy(places, place, local.at[1])
    placing.start()

    dest_place = dest_row * room + dest_rank
    picks = chooser(dest_place, n * few)
    for s in range(0, S, 2):
        words = chosen(picks, [code(mass[:, s + i, :], FULL) for i in range(2)])
        for i in range(2):
            sorted_mass[s + i] = words[:, i * BLK : (i + 1) * BLK]
    sorted_mass[S] = chosen(picks, [keys[...]])

    def wrap_mass(t, carry):
        for s in range(S + 1):
            mass_msg[pl.ds(t * mass_rows + s * few, few), :] = sorted_mass[s, pl.ds(t * few, few), :]
        return carry

    lax.fori_loop(0, n, wrap_mass, 0, unroll=4)
    mass_mail.post(order)
    for c in range(3):
        turbulence[c] = DECAY * velocity[c] + KICK * increments[c]

    levels = lax.broadcasted_iota(jnp.int32, (LEV, BLK), 0).astype(f32)
    xs_at = lax.broadcasted_iota(jnp.int32, (BX, BLK), 0).astype(f32)
    ys_at = lax.broadcasted_iota(jnp.int32, (BY, BLK), 0).astype(f32)

    def asking(i):
        row = mail.number(mail.origin(i)) * spot_rows + 3 * half
        return pltpu.make_async_copy(
            spots.at[pl.ds(aligned(row) if half % 8 == 0 else row, 1)], asked_of, local.at[0]
        )

    def weights(y, x):
        hy = hat(y - ys_at)
        hx = hat(x - xs_at)
        flat = jnp.concatenate([hy[i : i + 1] * hx for i in range(BY)], axis=0)
        flat_hi = flat.astype(bf16)
        flat_lo = (flat - flat_hi.astype(f32)).astype(bf16)
        return jnp.concatenate([flat_hi, flat_lo], axis=0)

    def interpolate(i, mets):
        o = mail.number(mail.origin(i))
        base = o * spot_rows
        for c, top in enumerate((BY - 1, BX - 1, LEV - 1)):
            word = spots[pl.ds(base + c * half, half), :]
            scaled[c] = low(word) * (top / FULL)
            scaled[3 + c] = high(word) * (top / FULL)
        for k in range(half):
            block = tiles[mets[k // few]]
            seen = product(
                jnp.concatenate([block, block], axis=1),
                jnp.concatenate(
                    [
                        weights(scaled[3 * side, k : k + 1, :], scaled[3 * side + 1, k : k + 1, :])
                        for side in range(2)
                    ],
                    axis=1,
                ),
            )
            for side in range(2):
                wz = hat(scaled[3 * side + 2, k : k + 1, :] - levels).astype(bf16).astype(f32)
                for c in range(3):
                    part = seen[c * LEV : (c + 1) * LEV, side * BLK : (side + 1) * BLK] * wz
                    total = part[0:8]
                    for v in range(8, LEV, 8):
                        total = total + part[v : v + 8]
                    parts[3 * side + c, 8 * k : 8 * k + 8, :] = total
        for c in range(3):
            codes = []
            for side in range(2):
                wind = parts[3 * side + c, pl.ds(0, half, stride=8), :]
                for v in range(1, 8):
                    wind = wind + parts[3 * side + c, pl.ds(v, half, stride=8), :]
                codes.append(code(wind + GUST, FULL / (2 * GUST)))
            back_msg[pl.ds(o * back_rows + c * half, half), :] = codes[0] | (codes[1] << 16)

    spot_mail.own().wait()
    asking(0).start()
    asking(0).wait()

    def serve(i, carry):
        mets = [jnp.clip(asked_of[0, 2 + k], 0, MB - 1) for k in range(Q)]

        @pl.when(i + 1 < n)
        def _():
            spot_mail.copy(i + 1).wait_recv()
            asking(i + 1).start()

        interpolate(i, mets)

        @pl.when(i > 0)
        def _():
            back_mail.copy(i, back=True).start()

        @pl.when(i == 0)
        def _():
            back_mail.own().start()

        @pl.when(i + 1 < n)
        def _():
            asking(i + 1).wait()

        return carry

    lax.fori_loop(0, n, serve, 0)
    for o in range(n):
        row = o * spot_rows + 3 * half
        heads[o : o + 1, :] = spots[row : row + 1, :]
    arrange(heads[...].astype(f32), room, plan)
    placing.wait()
    back_mail.collect()

    def fetch(b, carry):
        spot = place[0, b]
        row = jnp.clip(spot >> 1, 0, n * back_rows - 2 * half - 1)
        odd = 16 * (spot & 1)
        for c in range(3):
            word = winds[pl.ds(row + c * half, 1), :]
            found[c, pl.ds(b, 1), :] = lax.shift_right_logical(word, jnp.full_like(word, odd))
        return carry

    lax.fori_loop(0, blocks, fetch, 0, unroll=8)
    for c, top in enumerate((BY - 1.0, BX - 1.0, LEV - 1.0)):
        wind = low(found[c]) * (2 * GUST / FULL) - GUST
        moved[c] = jnp.clip(positions[c] + STEP * (wind + turbulence[c]), 0.0, top)
    sorted_z[...] = chosen(picks, [code(moved[2], FULL / (LEV - 1))])

    def wrap(t, carry):
        z_msg[pl.ds(t * z_rows, few), :] = sorted_z[pl.ds(t * few, few), :]
        return carry

    lax.fori_loop(0, n, wrap, 0, unroll=8)
    z_mail.post(order)
    z_mail.collect()
    mass_mail.collect()
    spot_mail.settle()
    back_mail.settle()
    mass_mail.settle()
    z_mail.settle()


def deposit_kernel(
    dims, plan, heights, shares, moved_in, turbulence_in,
    moved, turbulence, out,
    total, made, moved_held, turbulence_held, left, right, left_keys, right_keys, sems,
):
    room, mass_rows, z_rows = dims
    few = room // 2
    into = [
        pltpu.make_async_copy(moved_in, moved_held, sems.at[0]),
        pltpu.make_async_copy(turbulence_in, turbulence_held, sems.at[1]),
    ]
    onward = [
        pltpu.make_async_copy(moved_held, moved, sems.at[2]),
        pltpu.make_async_copy(turbulence_held, turbulence, sems.at[3]),
    ]
    for copy in into:
        copy.start()
    levels = lax.broadcasted_iota(jnp.int32, (SPAN, BLK), 0).astype(jnp.float32)
    columns = lax.broadcasted_iota(jnp.int32, (2 * MBC, BLK), 0)

    def clear(h, carry):
        total[h] = jnp.zeros((S * SPAN, 2 * MBC), jnp.float32)
        return carry

    lax.fori_loop(0, MB, clear, 0)

    def prepare(c, weights, cells):
        for j in range(BUNCH):
            number = plan[0, c * BUNCH + j]
            entry = jnp.maximum(number - 1, 0)
            o = lax.div(entry, room)
            q = lax.rem(entry, room)
            base = o * mass_rows + (q >> 1)
            odd = 16 * (q & 1)

            def half_of(word):
                return lax.shift_right_logical(word, jnp.full_like(word, odd))

            key = half_of(shares[pl.ds(base + S * few, 1), :]) & (MBC - 1)
            z = low(half_of(heights[pl.ds(o * z_rows + (q >> 1), 1), :])) * ((LEV - 1) / FULL)
            upper = z >= SPLIT
            z = z - jnp.where(upper, float(SPLIT), 0.0)
            key = key + jnp.where(upper, MBC, 0)
            cells[j : j + 1, :] = key + jnp.where(number > 0, 0, 4 * MBC)
            vert = hat(z - levels) * (1 / FULL)
            parts = low(half_of(shares[pl.ds(base, S, stride=few), :]))
            for s in range(S):
                weights[s * SPAN : (s + 1) * SPAN, j * BLK : (j + 1) * BLK] = (
                    parts[s : s + 1] * vert
                ).astype(jnp.bfloat16)

    def multiply(c, weights, cells):
        h = jnp.minimum(plan[1, c], MB - 1)
        picks = jnp.concatenate(
            [bits(cells[j : j + 1, :] == columns) for j in range(BUNCH)], axis=1
        )
        total[h] += lax.dot_general(
            weights[...], picks, (((1,), (1,)), ((), ())), preferred_element_type=jnp.float32
        )

    prepare(0, left, left_keys)

    def several(i, carry):
        prepare(2 * i + 1, right, right_keys)
        multiply(2 * i, left, left_keys)
        prepare(2 * i + 2, left, left_keys)
        multiply(2 * i + 1, right, right_keys)
        return carry

    chunks = plan[2, 0] // BUNCH
    lax.fori_loop(0, (chunks + 1) // 2, several, 0)
    for copy in into:
        copy.wait()
    for copy in onward:
        copy.start()

    def leave(h):
        return pltpu.make_async_copy(made.at[h], out.at[h], sems.at[4 + h])

    def finish(h, carry):
        for s in range(S):
            low_part = total[h, s * SPAN : (s + 1) * SPAN, 0:MBC]
            high_part = total[h, s * SPAN : (s + 1) * SPAN, MBC : 2 * MBC]
            shared = SPAN - SPLIT
            made[h, s * LEV : s * LEV + SPLIT, :] = low_part[:SPLIT]
            made[h, s * LEV + SPLIT : s * LEV + SPAN, :] = low_part[SPLIT:] + high_part[:shared]
            made[h, s * LEV + SPAN : (s + 1) * LEV, :] = high_part[shared:]
        leave(h).start()
        return carry

    lax.fori_loop(0, MB, finish, 0)
    for copy in onward:
        copy.wait()
    for h in range(MB):
        leave(h).wait()


def body(
    winds, positions, velocity, increments, mass, requests, block_slots, destinations, cell_keys
):
    n_lat = lax.axis_size("lat")
    n_lon = lax.axis_size("lon")
    n = n_lat * n_lon
    blocks = positions.shape[0]
    room = 2 * blocks // n
    half = Q * room // 2
    few = room // 2
    spot_rows = up8(3 * half + 1)
    back_rows = up8(3 * half)
    mass_rows = up8((S + 1) * few)
    z_rows = up8(few)
    spaces = -(-(n * room + (MB + 2) * BUNCH) // BLK) * BLK
    i32 = jnp.int32
    f32 = jnp.float32
    like = jax.ShapeDtypeStruct
    dma = pltpu.SemaphoreType.DMA

    positions, velocity, increments = (
        each.transpose(1, 0, 2) for each in (positions, velocity, increments)
    )
    moved, turbulence, heights, shares, plan = pl.pallas_call(
        functools.partial(
            advect_kernel,
            (n_lat, n_lon, blocks, room, spot_rows, back_rows, mass_rows, z_rows),
        ),
        out_shape=(
            like(positions.shape, f32),
            like(positions.shape, f32),
            like((n * z_rows, BLK), i32),
            like((n * mass_rows, BLK), i32),
            like((8, spaces), i32),
        ),
        in_specs=[VMEM] * 9,
        out_specs=(VMEM,) * 5,
        scratch_shapes=[
            pltpu.VMEM((n * spot_rows, BLK), i32),
            pltpu.VMEM((n * spot_rows, BLK), i32),
            pltpu.VMEM((n * back_rows, BLK), i32),
            pltpu.VMEM((n * back_rows, BLK), i32),
            pltpu.VMEM((n * mass_rows, BLK), i32),
            pltpu.VMEM((n * z_rows, BLK), i32),
            pltpu.VMEM((BLK, BLK), f32),
            pltpu.VMEM((8, blocks), i32),
            pltpu.VMEM((3, n * half, BLK), i32),
            pltpu.VMEM((S + 1, n * few, BLK), i32),
            pltpu.VMEM((n, BLK), i32),
            pltpu.VMEM((n, BLK), i32),
            pltpu.VMEM((6, half, BLK), f32),
            pltpu.VMEM((6, 8 * half, BLK), f32),
            pltpu.VMEM((3, blocks, BLK), i32),
            pltpu.VMEM((n * few, BLK), i32),
            pltpu.SMEM((1, BLK), i32),
            pltpu.SMEM((8, blocks), i32),
            dma((2, n)),
            dma((2, n)),
            dma((2, n)),
            dma((2, n)),
            dma((2,)),
        ],
        compiler_params=pltpu.CompilerParams(collective_id=0, has_side_effects=True),
        name="advect",
    )(
        block_slots.reshape(1, -1), destinations.reshape(1, -1), requests[0].T,
        positions, velocity, increments, mass, cell_keys, winds.reshape(MB, 3 * LEV, MBC),
    )
    anywhere = pl.BlockSpec(memory_space=pl.ANY)
    moved, turbulence, total = pl.pallas_call(
        functools.partial(deposit_kernel, (room, mass_rows, z_rows)),
        out_shape=(
            like(positions.shape, f32),
            like(positions.shape, f32),
            like((MB, S * LEV, MBC), f32),
        ),
        in_specs=[SMEM, VMEM, VMEM, anywhere, anywhere],
        out_specs=(anywhere,) * 3,
        scratch_shapes=[
            pltpu.VMEM((MB, S * SPAN, 2 * MBC), f32),
            pltpu.VMEM((MB, S * LEV, MBC), f32),
            pltpu.VMEM(positions.shape, f32),
            pltpu.VMEM(positions.shape, f32),
            pltpu.VMEM((S * SPAN, BUNCH * BLK), jnp.bfloat16),
            pltpu.VMEM((S * SPAN, BUNCH * BLK), jnp.bfloat16),
            pltpu.VMEM((8, BLK), i32),
            pltpu.VMEM((8, BLK), i32),
            dma((4 + MB,)),
        ],
        name="deposit",
    )(plan, heights, shares, moved, turbulence)
    concentration = total.reshape(MBR, MBK, S, LEV, MBC)
    return (moved.transpose(1, 0, 2), turbulence.transpose(1, 0, 2), concentration)


def solution(mesh):
    rows = ("lat", "lon")
    in_specs = (
        P("lat", "lon", None, None, None),
        P(rows, None, None),
        P(rows, None, None),
        P(rows, None, None),
        P(rows, None, None),
        P(rows, None, None),
        P(rows, None),
        P(rows, None),
        P(rows, None),
    )
    out_specs = (
        P(rows, None, None),
        P(rows, None, None),
        P("lat", "lon", None, None, None),
    )
    return jax.shard_map(body, mesh=mesh, in_specs=in_specs, out_specs=out_specs, check_vma=False)
```

```python
import functools

import jax
import jax.numpy as jnp
from jax import lax
from jax.experimental import pallas as pl
from jax.experimental.pallas import tpu as pltpu
from jax.sharding import PartitionSpec as P

BY = 8
BX = 16
MBC = 128
LEV = 40
S = 8
BLK = 128
MBR = 4
MBK = 4
Q = 2
MB = MBR * MBK

DECAY = 0.8
KICK = 0.6
STEP = 0.5

FULL = 65535.0
GUST = 6.1
BUNCH = 4
SHIFT = 64
CHUNKS = 4
SPLIT = 16
SPAN = LEV - SPLIT
VMEM = pl.BlockSpec(memory_space=pltpu.VMEM)
SMEM = pl.BlockSpec(memory_space=pltpu.SMEM)


def up8(rows):
    return -(-rows // 8) * 8


def hat(offset):
    return jnp.maximum(0.0, 1.0 - jnp.abs(offset))


def low(word):
    return (word & 0xFFFF).astype(jnp.float32)


def high(word):
    return lax.shift_right_logical(word, 16).astype(jnp.float32)


def code(value, scale):
    return (value * scale + 0.5).astype(jnp.int32)


def aligned(start):
    return pl.multiple_of(start, 8)


def bits(mask):
    return jnp.where(mask, 1.0, 0.0).astype(jnp.bfloat16)


def halves(value):
    top = (value >> 8).astype(jnp.float32).astype(jnp.bfloat16)
    return top, (value & 255).astype(jnp.float32).astype(jnp.bfloat16)


def product(left, right):
    return jnp.dot(left, right, preferred_element_type=jnp.float32)


def chooser(place, pairs):
    index = lax.broadcasted_iota(jnp.int32, (pairs, place.shape[1]), 0)
    picks = jnp.concatenate(
        [jnp.where(place == 2 * index + odd, 1.0, 0.0) for odd in range(2)], axis=0
    )
    return jnp.concatenate([picks * 256.0, picks], axis=1).astype(jnp.bfloat16)


def chosen(picks, values):
    pairs = picks.shape[0] // 2
    parts = [halves(value) for value in values]
    data = jnp.concatenate(
        [
            jnp.concatenate([top for top, _ in parts], axis=1),
            jnp.concatenate([rest for _, rest in parts], axis=1),
        ],
        axis=0,
    )
    found = product(picks, data).astype(jnp.int32)
    return found[:pairs] | (found[pairs:] << 16)


class Mail:
    def __init__(self, n_lat, n_lon):
        self.n_lat, self.n_lon = n_lat, n_lon
        self.n = n_lat * n_lon
        self.lat = lax.axis_index("lat")
        self.lon = lax.axis_index("lon")
        self.me = self.lat * n_lon + self.lon

    def split(self, i):
        if isinstance(i, int):
            return i // self.n_lon, i % self.n_lon
        return lax.div(i, self.n_lon), lax.rem(i, self.n_lon)

    def device(self, i):
        k, j = self.split(i)
        return lax.rem(self.lat + k, self.n_lat), lax.rem(self.lon + j, self.n_lon)

    def origin(self, i):
        k, j = self.split(i)
        return (
            lax.rem(self.lat - k + self.n_lat, self.n_lat),
            lax.rem(self.lon - j + self.n_lon, self.n_lon),
        )

    def number(self, device):
        return device[0] * self.n_lon + device[1]

    def greet(self):
        barrier = pltpu.get_barrier_semaphore()
        for i in range(1, self.n):
            pl.semaphore_signal(
                barrier, inc=1, device_id=self.device(i), device_id_type=pl.DeviceIdType.MESH
            )

    def meet(self):
        pl.semaphore_wait(pltpu.get_barrier_semaphore(), self.n - 1)


class Parcel:
    def __init__(self, mail, src, dst, rows, used, send, recv):
        self.mail, self.src, self.dst = mail, src, dst
        self.rows, self.used = rows, used
        self.send, self.recv = send, recv

    def part(self, ref, t):
        return ref.at[pl.ds(aligned(t * self.rows), self.used)]

    def copy(self, i, back=False):
        mail = self.mail
        device = mail.origin(i) if back else mail.device(i)
        return pltpu.make_async_remote_copy(
            src_ref=self.part(self.src, mail.number(device)),
            dst_ref=self.part(self.dst, mail.me),
            send_sem=self.send.at[i], recv_sem=self.recv.at[i],
            device_id=device, device_id_type=pl.DeviceIdType.MESH,
        )

    def own(self):
        me = self.mail.me
        return pltpu.make_async_copy(
            self.part(self.src, me), self.part(self.dst, me), self.send.at[0]
        )

    def post(self, order):
        for i in order:
            if i:
                self.copy(i).start()
            else:
                self.own().start()

    def collect(self, back=False):
        self.own().wait()
        for i in range(1, self.mail.n):
            self.copy(i, back).wait_recv()

    def settle(self, back=False):
        for i in range(1, self.mail.n):
            self.copy(i, back).wait_send()


def arrange(heads, room, plan):
    n = heads.shape[0]
    f32 = jnp.float32
    count = n * room
    spaces = plan.shape[1]
    tall = up8(MB + 1)

    def index(shape, dim):
        return lax.broadcasted_iota(jnp.int32, shape, dim)

    place = lax.rem(index((BLK, count), 1), room)
    spread = product(heads.astype(jnp.bfloat16), bits(index((BLK, count), 0) == place + SHIFT))
    entry = index((n, count), 1)
    mine = lax.div(entry, room) == index((n, count), 0)
    held = heads[:, SHIFT + room : SHIFT + room + 1]
    homes = jnp.where(lax.rem(entry, room).astype(f32) < held, spread, float(MB))
    homes = jnp.sum(jnp.where(mine, homes, 0.0), axis=0, keepdims=True).astype(jnp.int32)
    member = jnp.where(index((tall, count), 0) == homes, 1.0, 0.0)
    earlier = bits(index((count, count), 0) < index((count, count), 1))
    rank = product(member.astype(jnp.bfloat16), earlier)
    sizes = jnp.sum(member, axis=1, keepdims=True).astype(jnp.int32)
    sizes = (sizes + (BUNCH - 1)) // BUNCH * BUNCH
    sizes = jnp.where(index((tall, count), 0) < MB, sizes, 0)
    wide = sizes.astype(f32).astype(jnp.bfloat16)
    first = product(bits(index((tall, tall), 1) < index((tall, tall), 0)), wide)
    space = jnp.sum(member * (first + rank), axis=0, keepdims=True).astype(jnp.int32)
    space = jnp.where(homes < MB, space, -1)
    number = (index((8, count), 1) + 1).astype(f32).astype(jnp.bfloat16)
    found = lax.dot_general(
        number, bits(index((spaces, count), 0) == space),
        (((1,), (1,)), ((), ())), preferred_element_type=f32,
    )
    plan[...] = found.astype(jnp.int32)
    ends = first.astype(jnp.int32)[:MB, :BLK] + sizes[:MB, :BLK]
    over = jnp.where(ends <= BUNCH * index((MB, BLK), 1), 1, 0)
    plan[1:2, 0:BLK] = jnp.sum(over, axis=0, keepdims=True)
    plan[2:3, 0:BLK] = jnp.max(ends, axis=0, keepdims=True)


def advect_kernel(
    dims, slots, targets, requests, *refs,
):
    far = refs[:6]
    moved, turbulence, heights, shares, plan = refs[6:11]
    positions, velocity, increments, mass, keys, tiles = near = refs[11:17]
    advect(
        dims, slots, targets, requests, far, near, positions, velocity, increments, mass, keys,
        tiles, moved, turbulence, heights, shares, plan, *refs[17:],
    )


def advect(
    dims, slots, targets, requests, far, near, positions, velocity, increments, mass, keys, tiles,
    moved, turbulence, heights, shares, plan,
    spot_msg, spots, back_msg, winds, mass_msg, z_msg,
    table, places, sorted_spots, sorted_mass, own_heads, heads, scaled, parts, found, sorted_z,
    asked_of, place, spot_sems, back_sems, mass_sems, z_sems, local,
):
    n_lat, n_lon, blocks, room, spot_rows, back_rows, mass_rows, z_rows = dims
    mail = Mail(n_lat, n_lon)
    mail.greet()
    fetches = [
        pltpu.make_async_copy(far[i], near[i], local.at[2 + i]) for i in (0, 4, 3, 5, 1, 2)
    ]
    for copy in fetches:
        copy.start()
    n = mail.n
    entries = Q * room
    half = entries // 2
    few = room // 2
    f32 = jnp.float32
    bf16 = jnp.bfloat16
    rows = lax.broadcasted_iota(jnp.int32, (blocks, blocks), 0)
    cols = lax.broadcasted_iota(jnp.int32, (blocks, blocks), 1)
    tile_ids = lax.broadcasted_iota(jnp.int32, (n, blocks), 0)
    lanes = lax.broadcasted_iota(jnp.int32, (blocks, BLK), 1)
    slot_row = slots[...]
    dest_row = targets[...]
    table[...] = jnp.zeros_like(table)
    table[0:1, :] = slot_row.astype(f32)
    table[1:2, :] = dest_row.astype(f32)
    table[2:4, 0:n] = requests[...].astype(f32)
    turned = table[...].T
    slot_col = turned[:, 0:1].astype(jnp.int32)
    dest_col = turned[:, 1:2].astype(jnp.int32)
    same_slot = jnp.where((slot_col == slot_row) & (rows < cols), 1.0, 0.0)
    slot_rank = jnp.sum(same_slot, axis=0, keepdims=True).astype(jnp.int32)
    same_dest = jnp.where((dest_col == dest_row) & (rows < cols), 1.0, 0.0)
    dest_rank = jnp.sum(same_dest, axis=0, keepdims=True).astype(jnp.int32)
    entry = (slot_row & 1) * room + slot_rank
    places[...] = jnp.zeros_like(places)
    places[0:1, :] = (((slot_row >> 1) * back_rows + (entry >> 1)) << 1) | (entry & 1)

    fetches[0].wait()
    words = chosen(
        chooser(slot_row * room + slot_rank, n * half),
        [
            code(positions[0], FULL / (BY - 1)),
            code(positions[1], FULL / (BX - 1)),
            code(positions[2], FULL / (LEV - 1)),
        ],
    )
    for c in range(3):
        sorted_spots[c] = words[:, c * BLK : (c + 1) * BLK]
    counts = product(bits((slot_row >> 1) == tile_ids), bits(lanes == (slot_col & 1)))
    asked = turned[0:n] if n < BLK else turned
    front = lanes[0:n]
    before = bits((dest_col == dest_row) & (cols < rows))
    rank_col = product(before, jnp.ones((blocks, BLK), bf16)).astype(jnp.int32)
    fetches[1].wait()
    homes = jnp.where(lanes == SHIFT + rank_col, (keys[...] >> 7).astype(f32), 0.0)
    homes = jnp.where(lanes == SHIFT + room, 1.0, homes).astype(bf16)
    landing = product(bits(dest_row == tile_ids), homes)
    counts = jnp.where((front == 2) | (front == 3), asked, counts)
    own_heads[...] = (counts + landing).astype(jnp.int32)

    def address(t, carry):
        for c in range(3):
            spot_msg[pl.ds(t * spot_rows + c * half, half), :] = sorted_spots[
                c, pl.ds(t * half, half), :
            ]
        spot_msg[pl.ds(t * spot_rows + 3 * half, 1), :] = own_heads[pl.ds(t, 1), :]
        return carry

    lax.fori_loop(0, n, address, 0, unroll=8)
    spot_mail = Parcel(
        mail, spot_msg, spots, spot_rows, 3 * half + 1, spot_sems.at[0], spot_sems.at[1]
    )
    back_mail = Parcel(mail, back_msg, winds, back_rows, 3 * half, back_sems.at[0], back_sems.at[1])
    mass_mail = Parcel(
        mail, mass_msg, shares, mass_rows, (S + 1) * few, mass_sems.at[0], mass_sems.at[1]
    )
    z_mail = Parcel(mail, z_msg, heights, z_rows, few, z_sems.at[0], z_sems.at[1])
    dest_place = dest_row * room + dest_rank
    picks = chooser(dest_place, n * few)
    fetches[2].wait()
    for s in range(0, S, 2):
        words = chosen(picks, [code(mass[pl.ds(s + i, blocks, stride=S), :], FULL) for i in range(2)])
        for i in range(2):
            sorted_mass[s + i] = words[:, i * BLK : (i + 1) * BLK]
    sorted_mass[S] = chosen(picks, [keys[...]])

    def wrap_mass(t, carry):
        for s in range(S + 1):
            mass_msg[pl.ds(t * mass_rows + s * few, few), :] = sorted_mass[s, pl.ds(t * few, few), :]
        return carry

    lax.fori_loop(0, n, wrap_mass, 0, unroll=4)
    order = list(range(n))
    lats = [order[k * n_lon : (k + 1) * n_lon] for k in range(n_lat)]
    mail.meet()
    spot_mail.post(order)
    placing = pltpu.make_async_copy(places, place, local.at[1])
    placing.start()

    mass_mail.post(lats[0])
    mass_mail.post(lats[1])
    for copy in fetches[3:]:
        copy.wait()
    for c in range(3):
        turbulence[c] = DECAY * velocity[c] + KICK * increments[c]

    levels = lax.broadcasted_iota(jnp.int32, (LEV, BLK), 0).astype(f32)
    xs_at = lax.broadcasted_iota(jnp.int32, (BX, BLK), 0).astype(f32)
    ys_at = lax.broadcasted_iota(jnp.int32, (BY, BLK), 0).astype(f32)

    def asking(i):
        row = mail.number(mail.origin(i)) * spot_rows + 3 * half
        return pltpu.make_async_copy(
            spots.at[pl.ds(aligned(row) if half % 8 == 0 else row, 1)], asked_of, local.at[0]
        )

    def weights(y, x):
        hy = hat(y - ys_at)
        hx = hat(x - xs_at)
        flat = jnp.concatenate([hy[i : i + 1] * hx for i in range(BY)], axis=0)
        flat_hi = flat.astype(bf16)
        flat_lo = (flat - flat_hi.astype(f32)).astype(bf16)
        return jnp.concatenate([flat_hi, flat_lo], axis=0)

    def interpolate(i, mets):
        o = mail.number(mail.origin(i))
        base = o * spot_rows
        for c, top in enumerate((BY - 1, BX - 1, LEV - 1)):
            word = spots[pl.ds(base + c * half, half), :]
            scaled[c] = low(word) * (top / FULL)
            scaled[3 + c] = high(word) * (top / FULL)
        for k in range(half):
            block = tiles[mets[k // few]]
            seen = product(
                jnp.concatenate([block, block], axis=1),
                jnp.concatenate(
                    [
                        weights(scaled[3 * side, k : k + 1, :], scaled[3 * side + 1, k : k + 1, :])
                        for side in range(2)
                    ],
                    axis=1,
                ),
            )
            for side in range(2):
                wz = hat(scaled[3 * side + 2, k : k + 1, :] - levels).astype(bf16).astype(f32)
                for c in range(3):
                    part = seen[c * LEV : (c + 1) * LEV, side * BLK : (side + 1) * BLK] * wz
                    total = part[0:8]
                    for v in range(8, LEV, 8):
                        total = total + part[v : v + 8]
                    parts[3 * side + c, 8 * k : 8 * k + 8, :] = total
        for c in range(3):
            codes = []
            for side in range(2):
                wind = parts[3 * side + c, pl.ds(0, half, stride=8), :]
                for v in range(1, 8):
                    wind = wind + parts[3 * side + c, pl.ds(v, half, stride=8), :]
                codes.append(code(wind + GUST, FULL / (2 * GUST)))
            back_msg[pl.ds(o * back_rows + c * half, half), :] = codes[0] | (codes[1] << 16)

    spot_mail.own().wait()
    asking(0).start()
    asking(0).wait()

    def serve(i, carry):
        mets = [jnp.clip(asked_of[0, 2 + k], 0, MB - 1) for k in range(Q)]

        @pl.when(i + 1 < n)
        def _():
            spot_mail.copy(i + 1).wait_recv()
            asking(i + 1).start()

        interpolate(i, mets)

        @pl.when(i > 0)
        def _():
            back_mail.copy(i, back=True).start()

        @pl.when(i == 0)
        def _():
            back_mail.own().start()

        @pl.when(i + 1 < n)
        def _():
            asking(i + 1).wait()

        return carry

    lax.fori_loop(0, n, serve, 0)
    for o in range(n):
        row = o * spot_rows + 3 * half
        heads[o : o + 1, :] = spots[row : row + 1, :]
    arrange(heads[...].astype(f32), room, plan)
    mass_mail.post(lats[3])
    placing.wait()
    back_mail.collect()

    def fetch(b, carry):
        spot = place[0, b]
        row = jnp.clip(spot >> 1, 0, n * back_rows - 2 * half - 1)
        odd = 16 * (spot & 1)
        for c in range(3):
            word = winds[pl.ds(row + c * half, 1), :]
            found[c, pl.ds(b, 1), :] = lax.shift_right_logical(word, jnp.full_like(word, odd))
        return carry

    lax.fori_loop(0, blocks, fetch, 0, unroll=8)
    for c, top in enumerate((BY - 1.0, BX - 1.0, LEV - 1.0)):
        wind = low(found[c]) * (2 * GUST / FULL) - GUST
        moved[c] = jnp.clip(positions[c] + STEP * (wind + turbulence[c]), 0.0, top)
    sorted_z[...] = chosen(picks, [code(moved[2], FULL / (LEV - 1))])

    def wrap(t, carry):
        z_msg[pl.ds(t * z_rows, few), :] = sorted_z[pl.ds(t * few, few), :]
        return carry

    lax.fori_loop(0, n, wrap, 0, unroll=8)
    z_mail.post(order)
    mass_mail.post(lats[2])
    z_mail.collect()
    mass_mail.collect()
    spot_mail.settle()
    back_mail.settle()
    mass_mail.settle()
    z_mail.settle()


def deposit_kernel(
    dims, plan, heights, shares, moved_in, turbulence_in,
    moved, turbulence, out,
    total, made, moved_held, turbulence_held, columns, sems,
):
    room, mass_rows, z_rows = dims
    few = room // 2
    into = [
        pltpu.make_async_copy(moved_in, moved_held, sems.at[0]),
        pltpu.make_async_copy(turbulence_in, turbulence_held, sems.at[1]),
    ]
    onward = [
        pltpu.make_async_copy(moved_held, moved, sems.at[2]),
        pltpu.make_async_copy(turbulence_held, turbulence, sems.at[3]),
    ]
    for copy in into:
        copy.start()
    levels = lax.broadcasted_iota(jnp.int32, (SPAN, BLK), 0).astype(jnp.float32)
    columns[...] = lax.broadcasted_iota(jnp.int32, (2 * MBC, BLK), 0)

    def clear(h, carry):
        total[h] = jnp.zeros((S * SPAN, 2 * MBC), jnp.float32)
        return carry

    lax.fori_loop(0, MB, clear, 0)

    def operands(number):
        entry = jnp.maximum(number - 1, 0)
        o = lax.div(entry, room)
        q = lax.rem(entry, room)
        base = o * mass_rows + (q >> 1)
        odd = 16 * (q & 1)

        def half_of(word):
            return lax.shift_right_logical(word, jnp.full_like(word, odd))

        key = half_of(shares[pl.ds(base + S * few, 1), :]) & (MBC - 1)
        z = low(half_of(heights[pl.ds(o * z_rows + (q >> 1), 1), :])) * ((LEV - 1) / FULL)
        upper = z >= SPLIT
        z = z - jnp.where(upper, float(SPLIT), 0.0)
        key = key + jnp.where(upper, MBC, 0) + jnp.where(number > 0, 0, 4 * MBC)
        vert = hat(z - levels)
        parts = low(half_of(shares[pl.ds(base, S, stride=few), :])) * (1 / FULL)
        weights = jnp.concatenate([parts[s : s + 1] * vert for s in range(S)], axis=0)
        return weights.astype(jnp.bfloat16), bits(key == columns[...])

    def multiply(c):
        h = jnp.minimum(plan[1, c], MB - 1)
        pairs = [operands(plan[0, c * BUNCH + j]) for j in range(BUNCH)]
        total[h] += lax.dot_general(
            jnp.concatenate([w for w, _ in pairs], axis=1),
            jnp.concatenate([p for _, p in pairs], axis=1),
            (((1,), (1,)), ((), ())),
            preferred_element_type=jnp.float32,
        )

    def several(i, carry):
        for j in range(CHUNKS):
            multiply(CHUNKS * i + j)
        return carry

    chunks = plan[2, 0] // BUNCH
    lax.fori_loop(0, (chunks + CHUNKS - 1) // CHUNKS, several, 0)
    for copy in into:
        copy.wait()
    for copy in onward:
        copy.start()

    def leave(h):
        return pltpu.make_async_copy(made.at[h], out.at[h], sems.at[4 + h])

    def finish(h, carry):
        for s in range(S):
            low_part = total[h, s * SPAN : (s + 1) * SPAN, 0:MBC]
            high_part = total[h, s * SPAN : (s + 1) * SPAN, MBC : 2 * MBC]
            shared = SPAN - SPLIT
            made[h, s * LEV : s * LEV + SPLIT, :] = low_part[:SPLIT]
            made[h, s * LEV + SPLIT : s * LEV + SPAN, :] = low_part[SPLIT:] + high_part[:shared]
            made[h, s * LEV + SPAN : (s + 1) * LEV, :] = high_part[shared:]
        leave(h).start()
        return carry

    lax.fori_loop(0, MB, finish, 0)
    for copy in onward:
        copy.wait()
    for h in range(MB):
        leave(h).wait()


def body(
    winds, positions, velocity, increments, mass, requests, block_slots, destinations, cell_keys
):
    n_lat = lax.axis_size("lat")
    n_lon = lax.axis_size("lon")
    n = n_lat * n_lon
    blocks = positions.shape[0]
    room = 2 * blocks // n
    half = Q * room // 2
    few = room // 2
    spot_rows = up8(3 * half + 1)
    back_rows = up8(3 * half)
    mass_rows = up8((S + 1) * few)
    z_rows = up8(few)
    spaces = -(-(n * room + (MB + CHUNKS) * BUNCH) // BLK) * BLK
    i32 = jnp.int32
    f32 = jnp.float32
    like = jax.ShapeDtypeStruct
    dma = pltpu.SemaphoreType.DMA

    anywhere = pl.BlockSpec(memory_space=pl.ANY)
    mass = mass.reshape(-1, BLK)
    winds = winds.reshape(MB, 3 * LEV, MBC)
    positions, velocity, increments = (
        each.transpose(1, 0, 2) for each in (positions, velocity, increments)
    )
    moved, turbulence, heights, shares, plan = pl.pallas_call(
        functools.partial(
            advect_kernel,
            (n_lat, n_lon, blocks, room, spot_rows, back_rows, mass_rows, z_rows),
        ),
        out_shape=(
            like(positions.shape, f32),
            like(positions.shape, f32),
            like((n * z_rows, BLK), i32),
            like((n * mass_rows, BLK), i32),
            like((8, spaces), i32),
        ),
        in_specs=[VMEM] * 3 + [anywhere] * 6,
        out_specs=(VMEM,) * 5,
        scratch_shapes=[
            pltpu.VMEM(each.shape, each.dtype)
            for each in (positions, velocity, increments, mass, cell_keys, winds)
        ]
        + [
            pltpu.VMEM((n * spot_rows, BLK), i32),
            pltpu.VMEM((n * spot_rows, BLK), i32),
            pltpu.VMEM((n * back_rows, BLK), i32),
            pltpu.VMEM((n * back_rows, BLK), i32),
            pltpu.VMEM((n * mass_rows, BLK), i32),
            pltpu.VMEM((n * z_rows, BLK), i32),
            pltpu.VMEM((BLK, BLK), f32),
            pltpu.VMEM((8, blocks), i32),
            pltpu.VMEM((3, n * half, BLK), i32),
            pltpu.VMEM((S + 1, n * few, BLK), i32),
            pltpu.VMEM((n, BLK), i32),
            pltpu.VMEM((n, BLK), i32),
            pltpu.VMEM((6, half, BLK), f32),
            pltpu.VMEM((6, 8 * half, BLK), f32),
            pltpu.VMEM((3, blocks, BLK), i32),
            pltpu.VMEM((n * few, BLK), i32),
            pltpu.SMEM((1, BLK), i32),
            pltpu.SMEM((8, blocks), i32),
            dma((2, n)),
            dma((2, n)),
            dma((2, n)),
            dma((2, n)),
            dma((8,)),
        ],
        compiler_params=pltpu.CompilerParams(collective_id=0, has_side_effects=True),
        name="advect",
    )(
        block_slots.reshape(1, -1), destinations.reshape(1, -1), requests[0].T,
        positions, velocity, increments, mass, cell_keys, winds,
    )
    moved, turbulence, total = pl.pallas_call(
        functools.partial(deposit_kernel, (room, mass_rows, z_rows)),
        out_shape=(
            like(positions.shape, f32),
            like(positions.shape, f32),
            like((MB, S * LEV, MBC), f32),
        ),
        in_specs=[SMEM, VMEM, VMEM, anywhere, anywhere],
        out_specs=(anywhere,) * 3,
        scratch_shapes=[
            pltpu.VMEM((MB, S * SPAN, 2 * MBC), f32),
            pltpu.VMEM((MB, S * LEV, MBC), f32),
            pltpu.VMEM(positions.shape, f32),
            pltpu.VMEM(positions.shape, f32),
            pltpu.VMEM((2 * MBC, BLK), i32),
            dma((4 + MB,)),
        ],
        name="deposit",
    )(plan, heights, shares, moved, turbulence)
    concentration = total.reshape(MBR, MBK, S, LEV, MBC)
    return (moved.transpose(1, 0, 2), turbulence.transpose(1, 0, 2), concentration)


def solution(mesh):
    rows = ("lat", "lon")
    in_specs = (
        P("lat", "lon", None, None, None),
        P(rows, None, None),
        P(rows, None, None),
        P(rows, None, None),
        P(rows, None, None),
        P(rows, None, None),
        P(rows, None),
        P(rows, None),
        P(rows, None),
    )
    out_specs = (
        P(rows, None, None),
        P(rows, None, None),
        P("lat", "lon", None, None, None),
    )
    return jax.shard_map(body, mesh=mesh, in_specs=in_specs, out_specs=out_specs, check_vma=False)
```

```python
import functools

import jax
import jax.numpy as jnp
from jax import lax
from jax.experimental import pallas as pl
from jax.experimental.pallas import tpu as pltpu
from jax.sharding import PartitionSpec as P

BY = 8
BX = 16
MBC = 128
LEV = 40
S = 8
BLK = 128
MBR = 4
MBK = 4
Q = 2
MB = MBR * MBK

DECAY = 0.8
KICK = 0.6
STEP = 0.5

FULL = 65535.0
GUST = 6.1
BUNCH = 4
SHIFT = 64
CHUNKS = 6
SPLIT = 16
SPAN = LEV - SPLIT
VMEM = pl.BlockSpec(memory_space=pltpu.VMEM)
SMEM = pl.BlockSpec(memory_space=pltpu.SMEM)


def up8(rows):
    return -(-rows // 8) * 8


def hat(offset):
    return jnp.maximum(0.0, 1.0 - jnp.abs(offset))


def low(word):
    return (word & 0xFFFF).astype(jnp.float32)


def high(word):
    return lax.shift_right_logical(word, 16).astype(jnp.float32)


def code(value, scale):
    return (value * scale + 0.5).astype(jnp.int32)


def aligned(start):
    return pl.multiple_of(start, 8)


def bits(mask):
    return jnp.where(mask, 1.0, 0.0).astype(jnp.bfloat16)


def halves(value):
    top = (value >> 8).astype(jnp.float32).astype(jnp.bfloat16)
    return top, (value & 255).astype(jnp.float32).astype(jnp.bfloat16)


def product(left, right):
    return jnp.dot(left, right, preferred_element_type=jnp.float32)


def chooser(place, pairs):
    index = lax.broadcasted_iota(jnp.int32, (pairs, place.shape[1]), 0)
    picks = jnp.concatenate(
        [jnp.where(place == 2 * index + odd, 1.0, 0.0) for odd in range(2)], axis=0
    )
    return jnp.concatenate([picks * 256.0, picks], axis=1).astype(jnp.bfloat16)


def chosen(picks, values):
    pairs = picks.shape[0] // 2
    parts = [halves(value) for value in values]
    data = jnp.concatenate(
        [
            jnp.concatenate([top for top, _ in parts], axis=1),
            jnp.concatenate([rest for _, rest in parts], axis=1),
        ],
        axis=0,
    )
    found = product(picks, data).astype(jnp.int32)
    return found[:pairs] | (found[pairs:] << 16)


class Mail:
    def __init__(self, n_lat, n_lon):
        self.n_lat, self.n_lon = n_lat, n_lon
        self.n = n_lat * n_lon
        self.lat = lax.axis_index("lat")
        self.lon = lax.axis_index("lon")
        self.me = self.lat * n_lon + self.lon

    def split(self, i):
        if isinstance(i, int):
            return i // self.n_lon, i % self.n_lon
        return lax.div(i, self.n_lon), lax.rem(i, self.n_lon)

    def device(self, i):
        k, j = self.split(i)
        return lax.rem(self.lat + k, self.n_lat), lax.rem(self.lon + j, self.n_lon)

    def origin(self, i):
        k, j = self.split(i)
        return (
            lax.rem(self.lat - k + self.n_lat, self.n_lat),
            lax.rem(self.lon - j + self.n_lon, self.n_lon),
        )

    def number(self, device):
        return device[0] * self.n_lon + device[1]

    def greet(self):
        barrier = pltpu.get_barrier_semaphore()
        for i in range(1, self.n):
            pl.semaphore_signal(
                barrier, inc=1, device_id=self.device(i), device_id_type=pl.DeviceIdType.MESH
            )

    def meet(self):
        pl.semaphore_wait(pltpu.get_barrier_semaphore(), self.n - 1)


class Parcel:
    def __init__(self, mail, src, dst, rows, used, send, recv):
        self.mail, self.src, self.dst = mail, src, dst
        self.rows, self.used = rows, used
        self.send, self.recv = send, recv

    def part(self, ref, t):
        return ref.at[pl.ds(aligned(t * self.rows), self.used)]

    def copy(self, i, back=False):
        mail = self.mail
        device = mail.origin(i) if back else mail.device(i)
        return pltpu.make_async_remote_copy(
            src_ref=self.part(self.src, mail.number(device)),
            dst_ref=self.part(self.dst, mail.me),
            send_sem=self.send.at[i], recv_sem=self.recv.at[i],
            device_id=device, device_id_type=pl.DeviceIdType.MESH,
        )

    def own(self):
        me = self.mail.me
        return pltpu.make_async_copy(
            self.part(self.src, me), self.part(self.dst, me), self.send.at[0]
        )

    def post(self, order):
        for i in order:
            if i:
                self.copy(i).start()
            else:
                self.own().start()

    def collect(self, back=False):
        self.own().wait()
        for i in range(1, self.mail.n):
            self.copy(i, back).wait_recv()

    def settle(self, back=False):
        for i in range(1, self.mail.n):
            self.copy(i, back).wait_send()


def arrange(heads, room, plan):
    n = heads.shape[0]
    f32 = jnp.float32
    count = n * room
    spaces = plan.shape[1]
    tall = up8(MB + 1)

    def index(shape, dim):
        return lax.broadcasted_iota(jnp.int32, shape, dim)

    place = lax.rem(index((BLK, count), 1), room)
    spread = product(heads.astype(jnp.bfloat16), bits(index((BLK, count), 0) == place + SHIFT))
    entry = index((n, count), 1)
    mine = lax.div(entry, room) == index((n, count), 0)
    held = heads[:, SHIFT + room : SHIFT + room + 1]
    homes = jnp.where(lax.rem(entry, room).astype(f32) < held, spread, float(MB))
    homes = jnp.sum(jnp.where(mine, homes, 0.0), axis=0, keepdims=True).astype(jnp.int32)
    member = jnp.where(index((tall, count), 0) == homes, 1.0, 0.0)
    earlier = bits(index((count, count), 0) < index((count, count), 1))
    rank = product(member.astype(jnp.bfloat16), earlier)
    sizes = jnp.sum(member, axis=1, keepdims=True).astype(jnp.int32)
    sizes = (sizes + (BUNCH - 1)) // BUNCH * BUNCH
    sizes = jnp.where(index((tall, count), 0) < MB, sizes, 0)
    wide = sizes.astype(f32).astype(jnp.bfloat16)
    first = product(bits(index((tall, tall), 1) < index((tall, tall), 0)), wide)
    space = jnp.sum(member * (first + rank), axis=0, keepdims=True).astype(jnp.int32)
    space = jnp.where(homes < MB, space, -1)
    number = (index((8, count), 1) + 1).astype(f32).astype(jnp.bfloat16)
    found = lax.dot_general(
        number, bits(index((spaces, count), 0) == space),
        (((1,), (1,)), ((), ())), preferred_element_type=f32,
    )
    plan[...] = found.astype(jnp.int32)
    ends = first.astype(jnp.int32)[:MB, :BLK] + sizes[:MB, :BLK]
    over = jnp.where(ends <= BUNCH * index((MB, BLK), 1), 1, 0)
    plan[1:2, 0:BLK] = jnp.sum(over, axis=0, keepdims=True)
    plan[2:3, 0:BLK] = jnp.max(ends, axis=0, keepdims=True)


def advect_kernel(dims, *refs):
    far = refs[:9]
    gone, heights, shares, plan = refs[9:11], *refs[11:14]
    near = refs[14:23]
    slots, targets, requests, positions, velocity, increments, mass, keys, tiles = near
    advect(
        dims, far, near, gone, slots, targets, requests, positions, velocity, increments, mass,
        keys, tiles, heights, shares, plan, *refs[23:],
    )


def advect(
    dims, far, near, gone, slots, targets, requests, positions, velocity, increments, mass,
    keys, tiles, heights, shares, plan, moved, turbulence,
    spot_msg, spots, back_msg, winds, mass_msg, z_msg,
    table, places, sorted_spots, sorted_mass, own_heads, heads, scaled, parts, found, sorted_z,
    asked_of, place, spot_sems, back_sems, mass_sems, z_sems, local,
):
    n_lat, n_lon, blocks, room, spot_rows, back_rows, mass_rows, z_rows = dims
    mail = Mail(n_lat, n_lon)
    mail.greet()
    fetches = [
        pltpu.make_async_copy(far[i], near[i], local.at[2 + i])
        for i in (0, 1, 2, 3, 7, 6, 8, 4, 5)
    ]
    for copy in fetches:
        copy.start()
    for copy in fetches[:3]:
        copy.wait()
    n = mail.n
    entries = Q * room
    half = entries // 2
    few = room // 2
    f32 = jnp.float32
    bf16 = jnp.bfloat16
    rows = lax.broadcasted_iota(jnp.int32, (blocks, blocks), 0)
    cols = lax.broadcasted_iota(jnp.int32, (blocks, blocks), 1)
    tile_ids = lax.broadcasted_iota(jnp.int32, (n, blocks), 0)
    lanes = lax.broadcasted_iota(jnp.int32, (blocks, BLK), 1)
    slot_row = slots[...]
    dest_row = targets[...]
    table[...] = jnp.zeros_like(table)
    table[0:1, :] = slot_row.astype(f32)
    table[1:2, :] = dest_row.astype(f32)
    table[2:4, 0:n] = requests[...].astype(f32)
    turned = table[...].T
    slot_col = turned[:, 0:1].astype(jnp.int32)
    dest_col = turned[:, 1:2].astype(jnp.int32)
    same_slot = jnp.where((slot_col == slot_row) & (rows < cols), 1.0, 0.0)
    slot_rank = jnp.sum(same_slot, axis=0, keepdims=True).astype(jnp.int32)
    same_dest = jnp.where((dest_col == dest_row) & (rows < cols), 1.0, 0.0)
    dest_rank = jnp.sum(same_dest, axis=0, keepdims=True).astype(jnp.int32)
    entry = (slot_row & 1) * room + slot_rank
    places[...] = jnp.zeros_like(places)
    places[0:1, :] = (((slot_row >> 1) * back_rows + (entry >> 1)) << 1) | (entry & 1)

    fetches[3].wait()
    words = chosen(
        chooser(slot_row * room + slot_rank, n * half),
        [
            code(positions[0], FULL / (BY - 1)),
            code(positions[1], FULL / (BX - 1)),
            code(positions[2], FULL / (LEV - 1)),
        ],
    )
    for c in range(3):
        sorted_spots[c] = words[:, c * BLK : (c + 1) * BLK]
    counts = product(bits((slot_row >> 1) == tile_ids), bits(lanes == (slot_col & 1)))
    asked = turned[0:n] if n < BLK else turned
    front = lanes[0:n]
    before = bits((dest_col == dest_row) & (cols < rows))
    rank_col = product(before, jnp.ones((blocks, BLK), bf16)).astype(jnp.int32)
    fetches[4].wait()
    homes = jnp.where(lanes == SHIFT + rank_col, (keys[...] >> 7).astype(f32), 0.0)
    homes = jnp.where(lanes == SHIFT + room, 1.0, homes).astype(bf16)
    landing = product(bits(dest_row == tile_ids), homes)
    counts = jnp.where((front == 2) | (front == 3), asked, counts)
    own_heads[...] = (counts + landing).astype(jnp.int32)

    def address(t, carry):
        for c in range(3):
            spot_msg[pl.ds(t * spot_rows + c * half, half), :] = sorted_spots[
                c, pl.ds(t * half, half), :
            ]
        spot_msg[pl.ds(t * spot_rows + 3 * half, 1), :] = own_heads[pl.ds(t, 1), :]
        return carry

    lax.fori_loop(0, n, address, 0, unroll=8)
    spot_mail = Parcel(
        mail, spot_msg, spots, spot_rows, 3 * half + 1, spot_sems.at[0], spot_sems.at[1]
    )
    back_mail = Parcel(mail, back_msg, winds, back_rows, 3 * half, back_sems.at[0], back_sems.at[1])
    mass_mail = Parcel(
        mail, mass_msg, shares, mass_rows, (S + 1) * few, mass_sems.at[0], mass_sems.at[1]
    )
    z_mail = Parcel(mail, z_msg, heights, z_rows, few, z_sems.at[0], z_sems.at[1])
    dest_place = dest_row * room + dest_rank
    picks = chooser(dest_place, n * few)
    fetches[5].wait()
    for s in range(0, S, 2):
        words = chosen(picks, [code(mass[pl.ds(s + i, blocks, stride=S), :], FULL) for i in range(2)])
        for i in range(2):
            sorted_mass[s + i] = words[:, i * BLK : (i + 1) * BLK]
    sorted_mass[S] = chosen(picks, [keys[...]])

    def wrap_mass(t, carry):
        for s in range(S + 1):
            mass_msg[pl.ds(t * mass_rows + s * few, few), :] = sorted_mass[s, pl.ds(t * few, few), :]
        return carry

    lax.fori_loop(0, n, wrap_mass, 0, unroll=4)
    order = list(range(n))
    lats = [order[k * n_lon : (k + 1) * n_lon] for k in range(n_lat)]
    mail.meet()
    spot_mail.post(order)
    placing = pltpu.make_async_copy(places, place, local.at[1])
    placing.start()

    mass_mail.post(lats[0])
    mass_mail.post(lats[1])
    for copy in fetches[6:]:
        copy.wait()
    for c in range(3):
        turbulence[c] = DECAY * velocity[c] + KICK * increments[c]

    levels = lax.broadcasted_iota(jnp.int32, (LEV, BLK), 0).astype(f32)
    xs_at = lax.broadcasted_iota(jnp.int32, (BX, BLK), 0).astype(f32)
    ys_at = lax.broadcasted_iota(jnp.int32, (BY, BLK), 0).astype(f32)

    def asking(i):
        row = mail.number(mail.origin(i)) * spot_rows + 3 * half
        return pltpu.make_async_copy(
            spots.at[pl.ds(aligned(row) if half % 8 == 0 else row, 1)], asked_of, local.at[0]
        )

    def weights(y, x):
        hy = hat(y - ys_at)
        hx = hat(x - xs_at)
        flat = jnp.concatenate([hy[i : i + 1] * hx for i in range(BY)], axis=0)
        flat_hi = flat.astype(bf16)
        flat_lo = (flat - flat_hi.astype(f32)).astype(bf16)
        return jnp.concatenate([flat_hi, flat_lo], axis=0)

    def interpolate(i, mets):
        o = mail.number(mail.origin(i))
        base = o * spot_rows
        for c, top in enumerate((BY - 1, BX - 1, LEV - 1)):
            word = spots[pl.ds(base + c * half, half), :]
            scaled[c] = low(word) * (top / FULL)
            scaled[3 + c] = high(word) * (top / FULL)
        for k in range(half):
            block = tiles[mets[k // few]]
            seen = product(
                jnp.concatenate([block, block], axis=1),
                jnp.concatenate(
                    [
                        weights(scaled[3 * side, k : k + 1, :], scaled[3 * side + 1, k : k + 1, :])
                        for side in range(2)
                    ],
                    axis=1,
                ),
            )
            for side in range(2):
                wz = hat(scaled[3 * side + 2, k : k + 1, :] - levels).astype(bf16).astype(f32)
                for c in range(3):
                    part = seen[c * LEV : (c + 1) * LEV, side * BLK : (side + 1) * BLK] * wz
                    total = part[0:8]
                    for v in range(8, LEV, 8):
                        total = total + part[v : v + 8]
                    parts[3 * side + c, 8 * k : 8 * k + 8, :] = total
        for c in range(3):
            codes = []
            for side in range(2):
                wind = parts[3 * side + c, pl.ds(0, half, stride=8), :]
                for v in range(1, 8):
                    wind = wind + parts[3 * side + c, pl.ds(v, half, stride=8), :]
                codes.append(code(wind + GUST, FULL / (2 * GUST)))
            back_msg[pl.ds(o * back_rows + c * half, half), :] = codes[0] | (codes[1] << 16)

    spot_mail.own().wait()
    asking(0).start()
    asking(0).wait()

    def serve(i, carry):
        mets = [jnp.clip(asked_of[0, 2 + k], 0, MB - 1) for k in range(Q)]

        @pl.when(i + 1 < n)
        def _():
            spot_mail.copy(i + 1).wait_recv()
            asking(i + 1).start()

        interpolate(i, mets)

        @pl.when(i > 0)
        def _():
            back_mail.copy(i, back=True).start()

        @pl.when(i == 0)
        def _():
            back_mail.own().start()

        @pl.when(i + 1 < n)
        def _():
            asking(i + 1).wait()

        return carry

    lax.fori_loop(0, n, serve, 0)
    for o in range(n):
        row = o * spot_rows + 3 * half
        heads[o : o + 1, :] = spots[row : row + 1, :]
    arrange(heads[...].astype(f32), room, plan)
    mass_mail.post(lats[3])
    placing.wait()
    back_mail.collect()

    def fetch(b, carry):
        spot = place[0, b]
        row = jnp.clip(spot >> 1, 0, n * back_rows - 2 * half - 1)
        odd = 16 * (spot & 1)
        for c in range(3):
            word = winds[pl.ds(row + c * half, 1), :]
            found[c, pl.ds(b, 1), :] = lax.shift_right_logical(word, jnp.full_like(word, odd))
        return carry

    lax.fori_loop(0, blocks, fetch, 0, unroll=8)
    for c, top in enumerate((BY - 1.0, BX - 1.0, LEV - 1.0)):
        wind = low(found[c]) * (2 * GUST / FULL) - GUST
        moved[c] = jnp.clip(positions[c] + STEP * (wind + turbulence[c]), 0.0, top)
    sorted_z[...] = chosen(picks, [code(moved[2], FULL / (LEV - 1))])

    def wrap(t, carry):
        z_msg[pl.ds(t * z_rows, few), :] = sorted_z[pl.ds(t * few, few), :]
        return carry

    lax.fori_loop(0, n, wrap, 0, unroll=8)
    z_mail.post(order)
    leaving = [
        pltpu.make_async_copy(held, gone[i], local.at[2 + i])
        for i, held in enumerate((moved, turbulence))
    ]
    for copy in leaving:
        copy.start()
    mass_mail.post(lats[2])
    for copy in leaving:
        copy.wait()
    z_mail.collect()
    mass_mail.collect()
    spot_mail.settle()
    back_mail.settle()
    mass_mail.settle()
    z_mail.settle()


def deposit_kernel(
    dims, plan, heights_in, shares_in, moved_in, turbulence_in,
    moved, turbulence, out,
    heights, shares, made, moved_held, turbulence_held, columns, sems,
):
    room, mass_rows, z_rows = dims
    few = room // 2
    into = [
        pltpu.make_async_copy(moved_in, moved_held, sems.at[0]),
        pltpu.make_async_copy(turbulence_in, turbulence_held, sems.at[1]),
    ]
    onward = [
        pltpu.make_async_copy(moved_held, moved, sems.at[2]),
        pltpu.make_async_copy(turbulence_held, turbulence, sems.at[3]),
    ]
    stock = [
        pltpu.make_async_copy(shares_in, shares, sems.at[4 + MB]),
        pltpu.make_async_copy(heights_in, heights, sems.at[5 + MB]),
    ]
    for copy in stock + into:
        copy.start()
    levels = lax.broadcasted_iota(jnp.int32, (SPAN, BLK), 0).astype(jnp.float32)
    columns[...] = lax.broadcasted_iota(jnp.int32, (2 * MBC, BLK), 0)

    def clear(h, carry):
        made[h] = jnp.zeros((S * LEV, MBC), jnp.float32)
        return carry

    lax.fori_loop(0, MB, clear, 0)
    for copy in stock:
        copy.wait()

    def operands(number):
        entry = jnp.maximum(number - 1, 0)
        o = lax.div(entry, room)
        q = lax.rem(entry, room)
        base = o * mass_rows + (q >> 1)
        odd = 16 * (q & 1)

        def half_of(word):
            return lax.shift_right_logical(word, jnp.full_like(word, odd))

        key = half_of(shares[pl.ds(base + S * few, 1), :]) & (MBC - 1)
        z = low(half_of(heights[pl.ds(o * z_rows + (q >> 1), 1), :])) * ((LEV - 1) / FULL)
        upper = z >= SPLIT
        z = z - jnp.where(upper, float(SPLIT), 0.0)
        key = key + jnp.where(upper, MBC, 0) + jnp.where(number > 0, 0, 4 * MBC)
        vert = hat(z - levels)
        parts = low(half_of(shares[pl.ds(base, S, stride=few), :])) * (1 / FULL)
        weights = jnp.concatenate([parts[s : s + 1] * vert for s in range(S)], axis=0)
        return weights.astype(jnp.bfloat16), bits(key == columns[...])

    def multiply(c):
        h = jnp.minimum(plan[1, c], MB - 1)
        pairs = [operands(plan[0, c * BUNCH + j]) for j in range(BUNCH)]
        found = lax.dot_general(
            jnp.concatenate([w for w, _ in pairs], axis=1),
            jnp.concatenate([p for _, p in pairs], axis=1),
            (((1,), (1,)), ((), ())),
            preferred_element_type=jnp.float32,
        )
        shared = SPAN - SPLIT
        for s in range(S):
            low_part = found[s * SPAN : (s + 1) * SPAN, 0:MBC]
            high_part = found[s * SPAN : (s + 1) * SPAN, MBC : 2 * MBC]
            made[h, s * LEV : s * LEV + SPLIT, :] += low_part[:SPLIT]
            made[h, s * LEV + SPLIT : s * LEV + SPAN, :] += low_part[SPLIT:] + high_part[:shared]
            made[h, s * LEV + SPAN : (s + 1) * LEV, :] += high_part[shared:]

    def several(i, carry):
        for j in range(CHUNKS):
            multiply(CHUNKS * i + j)
        return carry

    chunks = plan[2, 0] // BUNCH
    lax.fori_loop(0, (chunks + CHUNKS - 1) // CHUNKS, several, 0)
    for copy in into:
        copy.wait()
    for copy in onward:
        copy.start()

    def leave(h):
        return pltpu.make_async_copy(made.at[h], out.at[h], sems.at[4 + h])

    for h in range(MB):
        leave(h).start()
    for copy in onward:
        copy.wait()
    for h in range(MB):
        leave(h).wait()


def body(
    winds, positions, velocity, increments, mass, requests, block_slots, destinations, cell_keys
):
    n_lat = lax.axis_size("lat")
    n_lon = lax.axis_size("lon")
    n = n_lat * n_lon
    blocks = positions.shape[0]
    room = 2 * blocks // n
    half = Q * room // 2
    few = room // 2
    spot_rows = up8(3 * half + 1)
    back_rows = up8(3 * half)
    mass_rows = up8((S + 1) * few)
    z_rows = up8(few)
    spaces = -(-(n * room + (MB + CHUNKS) * BUNCH) // BLK) * BLK
    i32 = jnp.int32
    f32 = jnp.float32
    like = jax.ShapeDtypeStruct
    dma = pltpu.SemaphoreType.DMA

    anywhere = pl.BlockSpec(memory_space=pl.ANY)
    mass = mass.reshape(-1, BLK)
    winds = winds.reshape(MB, 3 * LEV, MBC)
    positions, velocity, increments = (
        each.transpose(1, 0, 2) for each in (positions, velocity, increments)
    )
    inputs = (
        block_slots.reshape(1, -1), destinations.reshape(1, -1), requests[0].T,
        positions, velocity, increments, mass, cell_keys, winds,
    )
    moved, turbulence, heights, shares, plan = pl.pallas_call(
        functools.partial(
            advect_kernel,
            (n_lat, n_lon, blocks, room, spot_rows, back_rows, mass_rows, z_rows),
        ),
        out_shape=(
            like(positions.shape, f32),
            like(positions.shape, f32),
            like((n * z_rows, BLK), i32),
            like((n * mass_rows, BLK), i32),
            like((8, spaces), i32),
        ),
        in_specs=[pl.BlockSpec(memory_space=pltpu.HBM)] * 9,
        out_specs=(anywhere,) * 4 + (VMEM,),
        scratch_shapes=[
            pltpu.VMEM(each.shape, each.dtype)
            for each in inputs + (positions, positions)
        ]
        + [
            pltpu.VMEM((n * spot_rows, BLK), i32),
            pltpu.VMEM((n * spot_rows, BLK), i32),
            pltpu.VMEM((n * back_rows, BLK), i32),
            pltpu.VMEM((n * back_rows, BLK), i32),
            pltpu.VMEM((n * mass_rows, BLK), i32),
            pltpu.VMEM((n * z_rows, BLK), i32),
            pltpu.VMEM((BLK, BLK), f32),
            pltpu.VMEM((8, blocks), i32),
            pltpu.VMEM((3, n * half, BLK), i32),
            pltpu.VMEM((S + 1, n * few, BLK), i32),
            pltpu.VMEM((n, BLK), i32),
            pltpu.VMEM((n, BLK), i32),
            pltpu.VMEM((6, half, BLK), f32),
            pltpu.VMEM((6, 8 * half, BLK), f32),
            pltpu.VMEM((3, blocks, BLK), i32),
            pltpu.VMEM((n * few, BLK), i32),
            pltpu.SMEM((1, BLK), i32),
            pltpu.SMEM((8, blocks), i32),
            dma((2, n)),
            dma((2, n)),
            dma((2, n)),
            dma((2, n)),
            dma((2 + len(inputs),)),
        ],
        compiler_params=pltpu.CompilerParams(collective_id=0, has_side_effects=True),
        name="advect",
    )(*inputs)
    moved, turbulence, total = pl.pallas_call(
        functools.partial(deposit_kernel, (room, mass_rows, z_rows)),
        out_shape=(
            like(positions.shape, f32),
            like(positions.shape, f32),
            like((MB, S * LEV, MBC), f32),
        ),
        in_specs=[SMEM] + [anywhere] * 4,
        out_specs=(anywhere,) * 3,
        scratch_shapes=[
            pltpu.VMEM(heights.shape, i32),
            pltpu.VMEM(shares.shape, i32),
            pltpu.VMEM((MB, S * LEV, MBC), f32),
            pltpu.VMEM(positions.shape, f32),
            pltpu.VMEM(positions.shape, f32),
            pltpu.VMEM((2 * MBC, BLK), i32),
            dma((6 + MB,)),
        ],
        name="deposit",
    )(plan, heights, shares, moved, turbulence)
    concentration = total.reshape(MBR, MBK, S, LEV, MBC)
    return (moved.transpose(1, 0, 2), turbulence.transpose(1, 0, 2), concentration)


def solution(mesh):
    rows = ("lat", "lon")
    in_specs = (
        P("lat", "lon", None, None, None),
        P(rows, None, None),
        P(rows, None, None),
        P(rows, None, None),
        P(rows, None, None),
        P(rows, None, None),
        P(rows, None),
        P(rows, None),
        P(rows, None),
    )
    out_specs = (
        P(rows, None, None),
        P(rows, None, None),
        P("lat", "lon", None, None, None),
    )
    return jax.shard_map(body, mesh=mesh, in_specs=in_specs, out_specs=out_specs, check_vma=False)
```

```python
import functools

import jax
import jax.numpy as jnp
from jax import lax
from jax.experimental import pallas as pl
from jax.experimental.pallas import tpu as pltpu
from jax.sharding import PartitionSpec as P

BY = 8
BX = 16
MBC = 128
LEV = 40
S = 8
BLK = 128
MBR = 4
MBK = 4
Q = 2
MB = MBR * MBK

DECAY = 0.8
KICK = 0.6
STEP = 0.5

FULL = 65535.0
GUST = 6.1
BUNCH = 4
SHIFT = 64
CHUNKS = 6
SPLIT = 16
SPAN = LEV - SPLIT
VMEM = pl.BlockSpec(memory_space=pltpu.VMEM)
SMEM = pl.BlockSpec(memory_space=pltpu.SMEM)


def up8(rows):
    return -(-rows // 8) * 8


def hat(offset):
    return jnp.maximum(0.0, 1.0 - jnp.abs(offset))


def low(word):
    return (word & 0xFFFF).astype(jnp.float32)


def high(word):
    return lax.shift_right_logical(word, 16).astype(jnp.float32)


def code(value, scale):
    return (value * scale + 0.5).astype(jnp.int32)


def aligned(start):
    return pl.multiple_of(start, 8)


def bits(mask):
    return jnp.where(mask, 1.0, 0.0).astype(jnp.bfloat16)


def halves(value):
    top = (value >> 8).astype(jnp.float32).astype(jnp.bfloat16)
    return top, (value & 255).astype(jnp.float32).astype(jnp.bfloat16)


def product(left, right):
    return jnp.dot(left, right, preferred_element_type=jnp.float32)


def chooser(place, pairs):
    index = lax.broadcasted_iota(jnp.int32, (pairs, place.shape[1]), 0)
    picks = jnp.concatenate(
        [jnp.where(place == 2 * index + odd, 1.0, 0.0) for odd in range(2)], axis=0
    )
    return jnp.concatenate([picks * 256.0, picks], axis=1).astype(jnp.bfloat16)


def chosen(picks, values):
    pairs = picks.shape[0] // 2
    parts = [halves(value) for value in values]
    data = jnp.concatenate(
        [
            jnp.concatenate([top for top, _ in parts], axis=1),
            jnp.concatenate([rest for _, rest in parts], axis=1),
        ],
        axis=0,
    )
    found = product(picks, data).astype(jnp.int32)
    return found[:pairs] | (found[pairs:] << 16)


class Mail:
    def __init__(self, n_lat, n_lon):
        self.n_lat, self.n_lon = n_lat, n_lon
        self.n = n_lat * n_lon
        self.lat = lax.axis_index("lat")
        self.lon = lax.axis_index("lon")
        self.me = self.lat * n_lon + self.lon

    def split(self, i):
        if isinstance(i, int):
            return i // self.n_lon, i % self.n_lon
        return lax.div(i, self.n_lon), lax.rem(i, self.n_lon)

    def device(self, i):
        k, j = self.split(i)
        return lax.rem(self.lat + k, self.n_lat), lax.rem(self.lon + j, self.n_lon)

    def origin(self, i):
        k, j = self.split(i)
        return (
            lax.rem(self.lat - k + self.n_lat, self.n_lat),
            lax.rem(self.lon - j + self.n_lon, self.n_lon),
        )

    def number(self, device):
        return device[0] * self.n_lon + device[1]

    def greet(self):
        barrier = pltpu.get_barrier_semaphore()
        for i in range(1, self.n):
            pl.semaphore_signal(
                barrier, inc=1, device_id=self.device(i), device_id_type=pl.DeviceIdType.MESH
            )

    def meet(self):
        pl.semaphore_wait(pltpu.get_barrier_semaphore(), self.n - 1)


class Parcel:
    def __init__(self, mail, src, dst, rows, used, send, recv):
        self.mail, self.src, self.dst = mail, src, dst
        self.rows, self.used = rows, used
        self.send, self.recv = send, recv

    def part(self, ref, t):
        return ref.at[pl.ds(aligned(t * self.rows), self.used)]

    def copy(self, i, back=False):
        mail = self.mail
        device = mail.origin(i) if back else mail.device(i)
        return pltpu.make_async_remote_copy(
            src_ref=self.part(self.src, mail.number(device)),
            dst_ref=self.part(self.dst, mail.me),
            send_sem=self.send.at[i], recv_sem=self.recv.at[i],
            device_id=device, device_id_type=pl.DeviceIdType.MESH,
        )

    def own(self):
        me = self.mail.me
        return pltpu.make_async_copy(
            self.part(self.src, me), self.part(self.dst, me), self.send.at[0]
        )

    def post(self, order):
        for i in order:
            if i:
                self.copy(i).start()
            else:
                self.own().start()

    def collect(self, back=False):
        self.own().wait()
        for i in range(1, self.mail.n):
            self.copy(i, back).wait_recv()

    def settle(self, back=False):
        for i in range(1, self.mail.n):
            self.copy(i, back).wait_send()


def arrange(heads, room, plan):
    n = heads.shape[0]
    f32 = jnp.float32
    count = n * room
    spaces = plan.shape[1]
    tall = up8(MB + 1)

    def index(shape, dim):
        return lax.broadcasted_iota(jnp.int32, shape, dim)

    place = lax.rem(index((BLK, count), 1), room)
    spread = product(heads.astype(jnp.bfloat16), bits(index((BLK, count), 0) == place + SHIFT))
    entry = index((n, count), 1)
    mine = lax.div(entry, room) == index((n, count), 0)
    held = heads[:, SHIFT + room : SHIFT + room + 1]
    homes = jnp.where(lax.rem(entry, room).astype(f32) < held, spread, float(MB))
    homes = jnp.sum(jnp.where(mine, homes, 0.0), axis=0, keepdims=True).astype(jnp.int32)
    member = jnp.where(index((tall, count), 0) == homes, 1.0, 0.0)
    earlier = bits(index((count, count), 0) < index((count, count), 1))
    rank = product(member.astype(jnp.bfloat16), earlier)
    sizes = jnp.sum(member, axis=1, keepdims=True).astype(jnp.int32)
    sizes = (sizes + (BUNCH - 1)) // BUNCH * BUNCH
    sizes = jnp.where(index((tall, count), 0) < MB, sizes, 0)
    wide = sizes.astype(f32).astype(jnp.bfloat16)
    first = product(bits(index((tall, tall), 1) < index((tall, tall), 0)), wide)
    space = jnp.sum(member * (first + rank), axis=0, keepdims=True).astype(jnp.int32)
    space = jnp.where(homes < MB, space, -1)
    number = (index((8, count), 1) + 1).astype(f32).astype(jnp.bfloat16)
    found = lax.dot_general(
        number, bits(index((spaces, count), 0) == space),
        (((1,), (1,)), ((), ())), preferred_element_type=f32,
    )
    plan[...] = found.astype(jnp.int32)
    ends = first.astype(jnp.int32)[:MB, :BLK] + sizes[:MB, :BLK]
    over = jnp.where(ends <= BUNCH * index((MB, BLK), 1), 1, 0)
    plan[1:2, 0:BLK] = jnp.sum(over, axis=0, keepdims=True)
    plan[2:3, 0:BLK] = jnp.max(ends, axis=0, keepdims=True)


def advect_kernel(dims, *refs):
    far = refs[:9]
    gone = (refs[9], refs[10], refs[13])
    heights, shares = refs[11:13]
    near = refs[14:23]
    slots, targets, requests, positions, velocity, increments, mass, keys, tiles = near
    advect(
        dims, far, near, gone, slots, targets, requests, positions, velocity, increments, mass,
        keys, tiles, heights, shares, *refs[23:],
    )


def advect(
    dims, far, near, gone, slots, targets, requests, positions, velocity, increments, mass,
    keys, tiles, heights, shares, moved, turbulence, plan,
    spot_msg, spots, back_msg, winds, mass_msg, z_msg,
    table, places, sorted_spots, sorted_mass, own_heads, heads, scaled, parts, found, sorted_z,
    asked_of, place, spot_sems, back_sems, mass_sems, z_sems, local,
):
    n_lat, n_lon, blocks, room, spot_rows, back_rows, mass_rows, z_rows = dims
    mail = Mail(n_lat, n_lon)
    mail.greet()
    fetches = [
        pltpu.make_async_copy(far[i], near[i], local.at[2 + i])
        for i in (0, 1, 2, 3, 7, 6, 8, 4, 5)
    ]
    for copy in fetches:
        copy.start()
    for copy in fetches[:3]:
        copy.wait()
    n = mail.n
    entries = Q * room
    half = entries // 2
    few = room // 2
    f32 = jnp.float32
    bf16 = jnp.bfloat16
    rows = lax.broadcasted_iota(jnp.int32, (blocks, blocks), 0)
    cols = lax.broadcasted_iota(jnp.int32, (blocks, blocks), 1)
    tile_ids = lax.broadcasted_iota(jnp.int32, (n, blocks), 0)
    lanes = lax.broadcasted_iota(jnp.int32, (blocks, BLK), 1)
    slot_row = slots[...]
    dest_row = targets[...]
    table[...] = jnp.zeros_like(table)
    table[0:1, :] = slot_row.astype(f32)
    table[1:2, :] = dest_row.astype(f32)
    table[2:4, 0:n] = requests[...].astype(f32)
    turned = table[...].T
    slot_col = turned[:, 0:1].astype(jnp.int32)
    dest_col = turned[:, 1:2].astype(jnp.int32)
    same_slot = jnp.where((slot_col == slot_row) & (rows < cols), 1.0, 0.0)
    slot_rank = jnp.sum(same_slot, axis=0, keepdims=True).astype(jnp.int32)
    same_dest = jnp.where((dest_col == dest_row) & (rows < cols), 1.0, 0.0)
    dest_rank = jnp.sum(same_dest, axis=0, keepdims=True).astype(jnp.int32)
    entry = (slot_row & 1) * room + slot_rank
    places[...] = jnp.zeros_like(places)
    places[0:1, :] = (((slot_row >> 1) * back_rows + (entry >> 1)) << 1) | (entry & 1)

    fetches[3].wait()
    words = chosen(
        chooser(slot_row * room + slot_rank, n * half),
        [
            code(positions[0], FULL / (BY - 1)),
            code(positions[1], FULL / (BX - 1)),
            code(positions[2], FULL / (LEV - 1)),
        ],
    )
    for c in range(3):
        sorted_spots[c] = words[:, c * BLK : (c + 1) * BLK]
    counts = product(bits((slot_row >> 1) == tile_ids), bits(lanes == (slot_col & 1)))
    asked = turned[0:n] if n < BLK else turned
    front = lanes[0:n]
    before = bits((dest_col == dest_row) & (cols < rows))
    rank_col = product(before, jnp.ones((blocks, BLK), bf16)).astype(jnp.int32)
    fetches[4].wait()
    homes = jnp.where(lanes == SHIFT + rank_col, (keys[...] >> 7).astype(f32), 0.0)
    homes = jnp.where(lanes == SHIFT + room, 1.0, homes).astype(bf16)
    landing = product(bits(dest_row == tile_ids), homes)
    counts = jnp.where((front == 2) | (front == 3), asked, counts)
    own_heads[...] = (counts + landing).astype(jnp.int32)

    def address(t, carry):
        for c in range(3):
            spot_msg[pl.ds(t * spot_rows + c * half, half), :] = sorted_spots[
                c, pl.ds(t * half, half), :
            ]
        spot_msg[pl.ds(t * spot_rows + 3 * half, 1), :] = own_heads[pl.ds(t, 1), :]
        return carry

    lax.fori_loop(0, n, address, 0, unroll=8)
    spot_mail = Parcel(
        mail, spot_msg, spots, spot_rows, 3 * half + 1, spot_sems.at[0], spot_sems.at[1]
    )
    back_mail = Parcel(mail, back_msg, winds, back_rows, 3 * half, back_sems.at[0], back_sems.at[1])
    mass_mail = Parcel(
        mail, mass_msg, shares, mass_rows, (S + 1) * few, mass_sems.at[0], mass_sems.at[1]
    )
    z_mail = Parcel(mail, z_msg, heights, z_rows, few, z_sems.at[0], z_sems.at[1])
    dest_place = dest_row * room + dest_rank
    picks = chooser(dest_place, n * few)
    fetches[5].wait()
    for s in range(0, S, 2):
        words = chosen(picks, [code(mass[pl.ds(s + i, blocks, stride=S), :], FULL) for i in range(2)])
        for i in range(2):
            sorted_mass[s + i] = words[:, i * BLK : (i + 1) * BLK]
    sorted_mass[S] = chosen(picks, [keys[...]])

    def wrap_mass(t, carry):
        for s in range(S + 1):
            mass_msg[pl.ds(t * mass_rows + s * few, few), :] = sorted_mass[s, pl.ds(t * few, few), :]
        return carry

    lax.fori_loop(0, n, wrap_mass, 0, unroll=4)
    order = list(range(n))
    lats = [order[k * n_lon : (k + 1) * n_lon] for k in range(n_lat)]
    mail.meet()
    spot_mail.post(order)
    placing = pltpu.make_async_copy(places, place, local.at[1])
    placing.start()

    mass_mail.post(lats[0])
    mass_mail.post(lats[1])
    for copy in fetches[6:]:
        copy.wait()
    for c in range(3):
        turbulence[c] = DECAY * velocity[c] + KICK * increments[c]

    levels = lax.broadcasted_iota(jnp.int32, (LEV, BLK), 0).astype(f32)
    xs_at = lax.broadcasted_iota(jnp.int32, (BX, BLK), 0).astype(f32)
    ys_at = lax.broadcasted_iota(jnp.int32, (BY, BLK), 0).astype(f32)

    def asking(i):
        row = mail.number(mail.origin(i)) * spot_rows + 3 * half
        return pltpu.make_async_copy(
            spots.at[pl.ds(aligned(row) if half % 8 == 0 else row, 1)], asked_of, local.at[0]
        )

    def weights(y, x):
        hy = hat(y - ys_at)
        hx = hat(x - xs_at)
        flat = jnp.concatenate([hy[i : i + 1] * hx for i in range(BY)], axis=0)
        flat_hi = flat.astype(bf16)
        flat_lo = (flat - flat_hi.astype(f32)).astype(bf16)
        return jnp.concatenate([flat_hi, flat_lo], axis=0)

    def interpolate(i, mets):
        o = mail.number(mail.origin(i))
        base = o * spot_rows
        for c, top in enumerate((BY - 1, BX - 1, LEV - 1)):
            word = spots[pl.ds(base + c * half, half), :]
            scaled[c] = low(word) * (top / FULL)
            scaled[3 + c] = high(word) * (top / FULL)
        for k in range(half):
            block = tiles[mets[k // few]]
            seen = product(
                jnp.concatenate([block, block], axis=1),
                jnp.concatenate(
                    [
                        weights(scaled[3 * side, k : k + 1, :], scaled[3 * side + 1, k : k + 1, :])
                        for side in range(2)
                    ],
                    axis=1,
                ),
            )
            for side in range(2):
                wz = hat(scaled[3 * side + 2, k : k + 1, :] - levels).astype(bf16).astype(f32)
                for c in range(3):
                    part = seen[c * LEV : (c + 1) * LEV, side * BLK : (side + 1) * BLK] * wz
                    total = part[0:8]
                    for v in range(8, LEV, 8):
                        total = total + part[v : v + 8]
                    parts[3 * side + c, 8 * k : 8 * k + 8, :] = total
        for c in range(3):
            codes = []
            for side in range(2):
                wind = parts[3 * side + c, pl.ds(0, half, stride=8), :]
                for v in range(1, 8):
                    wind = wind + parts[3 * side + c, pl.ds(v, half, stride=8), :]
                codes.append(code(wind + GUST, FULL / (2 * GUST)))
            back_msg[pl.ds(o * back_rows + c * half, half), :] = codes[0] | (codes[1] << 16)

    spot_mail.own().wait()
    asking(0).start()
    asking(0).wait()

    def serve(i, carry):
        mets = [jnp.clip(asked_of[0, 2 + k], 0, MB - 1) for k in range(Q)]

        @pl.when(i + 1 < n)
        def _():
            spot_mail.copy(i + 1).wait_recv()
            asking(i + 1).start()

        interpolate(i, mets)

        @pl.when(i > 0)
        def _():
            back_mail.copy(i, back=True).start()

        @pl.when(i == 0)
        def _():
            back_mail.own().start()

        @pl.when(i + 1 < n)
        def _():
            asking(i + 1).wait()

        return carry

    lax.fori_loop(0, n, serve, 0)
    for o in range(n):
        row = o * spot_rows + 3 * half
        heads[o : o + 1, :] = spots[row : row + 1, :]
    arrange(heads[...].astype(f32), room, plan)
    mass_mail.post(lats[3])
    placing.wait()
    back_mail.collect()

    def fetch(b, carry):
        spot = place[0, b]
        row = jnp.clip(spot >> 1, 0, n * back_rows - 2 * half - 1)
        odd = 16 * (spot & 1)
        for c in range(3):
            word = winds[pl.ds(row + c * half, 1), :]
            found[c, pl.ds(b, 1), :] = lax.shift_right_logical(word, jnp.full_like(word, odd))
        return carry

    lax.fori_loop(0, blocks, fetch, 0, unroll=8)
    for c, top in enumerate((BY - 1.0, BX - 1.0, LEV - 1.0)):
        wind = low(found[c]) * (2 * GUST / FULL) - GUST
        moved[c] = jnp.clip(positions[c] + STEP * (wind + turbulence[c]), 0.0, top)
    sorted_z[...] = chosen(picks, [code(moved[2], FULL / (LEV - 1))])

    def wrap(t, carry):
        z_msg[pl.ds(t * z_rows, few), :] = sorted_z[pl.ds(t * few, few), :]
        return carry

    lax.fori_loop(0, n, wrap, 0, unroll=8)
    z_mail.post(order)
    leaving = [
        pltpu.make_async_copy(held, gone[i], local.at[2 + i])
        for i, held in enumerate((moved, turbulence, plan))
    ]
    for copy in leaving:
        copy.start()
    mass_mail.post(lats[2])
    for copy in leaving:
        copy.wait()
    z_mail.collect()
    mass_mail.collect()
    spot_mail.settle()
    back_mail.settle()
    mass_mail.settle()
    z_mail.settle()


def deposit_kernel(
    dims, plan_in, heights_in, shares_in, moved_in, turbulence_in,
    moved, turbulence, out,
    plan, heights, shares, made, moved_held, turbulence_held, columns, sems,
):
    room, mass_rows, z_rows = dims
    few = room // 2
    into = [
        pltpu.make_async_copy(moved_in, moved_held, sems.at[0]),
        pltpu.make_async_copy(turbulence_in, turbulence_held, sems.at[1]),
    ]
    onward = [
        pltpu.make_async_copy(moved_held, moved, sems.at[2]),
        pltpu.make_async_copy(turbulence_held, turbulence, sems.at[3]),
    ]
    stock = [
        pltpu.make_async_copy(shares_in, shares, sems.at[4 + MB]),
        pltpu.make_async_copy(heights_in, heights, sems.at[5 + MB]),
        pltpu.make_async_copy(plan_in, plan, sems.at[6 + MB]),
    ]
    for copy in stock + into:
        copy.start()
    levels = lax.broadcasted_iota(jnp.int32, (SPAN, BLK), 0).astype(jnp.float32)
    columns[...] = lax.broadcasted_iota(jnp.int32, (2 * MBC, BLK), 0)

    def clear(h, carry):
        made[h] = jnp.zeros((S * LEV, MBC), jnp.float32)
        return carry

    lax.fori_loop(0, MB, clear, 0)
    for copy in stock:
        copy.wait()

    def operands(number):
        entry = jnp.maximum(number - 1, 0)
        o = lax.div(entry, room)
        q = lax.rem(entry, room)
        base = o * mass_rows + (q >> 1)
        odd = 16 * (q & 1)

        def half_of(word):
            return lax.shift_right_logical(word, jnp.full_like(word, odd))

        key = half_of(shares[pl.ds(base + S * few, 1), :]) & (MBC - 1)
        z = low(half_of(heights[pl.ds(o * z_rows + (q >> 1), 1), :])) * ((LEV - 1) / FULL)
        upper = z >= SPLIT
        z = z - jnp.where(upper, float(SPLIT), 0.0)
        key = key + jnp.where(upper, MBC, 0) + jnp.where(number > 0, 0, 4 * MBC)
        vert = hat(z - levels)
        parts = low(half_of(shares[pl.ds(base, S, stride=few), :])) * (1 / FULL)
        weights = jnp.concatenate([parts[s : s + 1] * vert for s in range(S)], axis=0)
        return weights.astype(jnp.bfloat16), bits(key == columns[...])

    def multiply(c):
        h = jnp.minimum(plan[1, c], MB - 1)
        pairs = [operands(plan[0, c * BUNCH + j]) for j in range(BUNCH)]
        found = lax.dot_general(
            jnp.concatenate([w for w, _ in pairs], axis=1),
            jnp.concatenate([p for _, p in pairs], axis=1),
            (((1,), (1,)), ((), ())),
            preferred_element_type=jnp.float32,
        )
        shared = SPAN - SPLIT
        for s in range(S):
            low_part = found[s * SPAN : (s + 1) * SPAN, 0:MBC]
            high_part = found[s * SPAN : (s + 1) * SPAN, MBC : 2 * MBC]
            made[h, s * LEV : s * LEV + SPLIT, :] += low_part[:SPLIT]
            made[h, s * LEV + SPLIT : s * LEV + SPAN, :] += low_part[SPLIT:] + high_part[:shared]
            made[h, s * LEV + SPAN : (s + 1) * LEV, :] += high_part[shared:]

    def leave(h):
        return pltpu.make_async_copy(made.at[h], out.at[h], sems.at[4 + h])

    def release(h, carry):
        leave(h).start()
        return carry

    def several(i, ready):
        for j in range(CHUNKS):
            multiply(CHUNKS * i + j)
        done = jnp.minimum(plan[1, CHUNKS * (i + 1)], MB)
        lax.fori_loop(ready, done, release, 0)
        return jnp.maximum(ready, done)

    for copy in into:
        copy.wait()
    for copy in onward:
        copy.start()
    chunks = plan[2, 0] // BUNCH
    ready = lax.fori_loop(0, (chunks + CHUNKS - 1) // CHUNKS, several, 0)
    lax.fori_loop(ready, MB, release, 0)
    for copy in onward:
        copy.wait()
    for h in range(MB):
        leave(h).wait()


def body(
    winds, positions, velocity, increments, mass, requests, block_slots, destinations, cell_keys
):
    n_lat = lax.axis_size("lat")
    n_lon = lax.axis_size("lon")
    n = n_lat * n_lon
    blocks = positions.shape[0]
    room = 2 * blocks // n
    half = Q * room // 2
    few = room // 2
    spot_rows = up8(3 * half + 1)
    back_rows = up8(3 * half)
    mass_rows = up8((S + 1) * few)
    z_rows = up8(few)
    spaces = -(-(n * room + (MB + CHUNKS) * BUNCH) // BLK) * BLK
    i32 = jnp.int32
    f32 = jnp.float32
    like = jax.ShapeDtypeStruct
    dma = pltpu.SemaphoreType.DMA

    anywhere = pl.BlockSpec(memory_space=pl.ANY)
    mass = mass.reshape(-1, BLK)
    winds = winds.reshape(MB, 3 * LEV, MBC)
    positions, velocity, increments = (
        each.transpose(1, 0, 2) for each in (positions, velocity, increments)
    )
    inputs = (
        block_slots.reshape(1, -1), destinations.reshape(1, -1), requests[0].T,
        positions, velocity, increments, mass, cell_keys, winds,
    )
    moved, turbulence, heights, shares, plan = pl.pallas_call(
        functools.partial(
            advect_kernel,
            (n_lat, n_lon, blocks, room, spot_rows, back_rows, mass_rows, z_rows),
        ),
        out_shape=(
            like(positions.shape, f32),
            like(positions.shape, f32),
            like((n * z_rows, BLK), i32),
            like((n * mass_rows, BLK), i32),
            like((8, spaces), i32),
        ),
        in_specs=[pl.BlockSpec(memory_space=pltpu.HBM)] * 9,
        out_specs=(anywhere,) * 5,
        scratch_shapes=[
            pltpu.VMEM(each.shape, each.dtype)
            for each in inputs + (positions, positions)
        ]
        + [pltpu.VMEM((8, spaces), i32)]
        + [
            pltpu.VMEM((n * spot_rows, BLK), i32),
            pltpu.VMEM((n * spot_rows, BLK), i32),
            pltpu.VMEM((n * back_rows, BLK), i32),
            pltpu.VMEM((n * back_rows, BLK), i32),
            pltpu.VMEM((n * mass_rows, BLK), i32),
            pltpu.VMEM((n * z_rows, BLK), i32),
            pltpu.VMEM((BLK, BLK), f32),
            pltpu.VMEM((8, blocks), i32),
            pltpu.VMEM((3, n * half, BLK), i32),
            pltpu.VMEM((S + 1, n * few, BLK), i32),
            pltpu.VMEM((n, BLK), i32),
            pltpu.VMEM((n, BLK), i32),
            pltpu.VMEM((6, half, BLK), f32),
            pltpu.VMEM((6, 8 * half, BLK), f32),
            pltpu.VMEM((3, blocks, BLK), i32),
            pltpu.VMEM((n * few, BLK), i32),
            pltpu.SMEM((1, BLK), i32),
            pltpu.SMEM((8, blocks), i32),
            dma((2, n)),
            dma((2, n)),
            dma((2, n)),
            dma((2, n)),
            dma((2 + len(inputs),)),
        ],
        compiler_params=pltpu.CompilerParams(collective_id=0, has_side_effects=True),
        name="advect",
    )(*inputs)
    moved, turbulence, total = pl.pallas_call(
        functools.partial(deposit_kernel, (room, mass_rows, z_rows)),
        out_shape=(
            like(positions.shape, f32),
            like(positions.shape, f32),
            like((MB, S * LEV, MBC), f32),
        ),
        in_specs=[anywhere] * 5,
        out_specs=(anywhere,) * 3,
        scratch_shapes=[
            pltpu.SMEM(plan.shape, i32),
            pltpu.VMEM(heights.shape, i32),
            pltpu.VMEM(shares.shape, i32),
            pltpu.VMEM((MB, S * LEV, MBC), f32),
            pltpu.VMEM(positions.shape, f32),
            pltpu.VMEM(positions.shape, f32),
            pltpu.VMEM((2 * MBC, BLK), i32),
            dma((7 + MB,)),
        ],
        name="deposit",
    )(plan, heights, shares, moved, turbulence)
    concentration = total.reshape(MBR, MBK, S, LEV, MBC)
    return (moved.transpose(1, 0, 2), turbulence.transpose(1, 0, 2), concentration)


def solution(mesh):
    rows = ("lat", "lon")
    in_specs = (
        P("lat", "lon", None, None, None),
        P(rows, None, None),
        P(rows, None, None),
        P(rows, None, None),
        P(rows, None, None),
        P(rows, None, None),
        P(rows, None),
        P(rows, None),
        P(rows, None),
    )
    out_specs = (
        P(rows, None, None),
        P(rows, None, None),
        P("lat", "lon", None, None, None),
    )
    return jax.shard_map(body, mesh=mesh, in_specs=in_specs, out_specs=out_specs, check_vma=False)
```

```python
import functools

import jax
import jax.numpy as jnp
from jax import lax
from jax.experimental import pallas as pl
from jax.experimental.pallas import tpu as pltpu
from jax.sharding import PartitionSpec as P

BY = 8
BX = 16
MBC = 128
LEV = 40
S = 8
BLK = 128
MBR = 4
MBK = 4
Q = 2
MB = MBR * MBK

DECAY = 0.8
KICK = 0.6
STEP = 0.5

FULL = 65535.0
GUST = 6.1
BUNCH = 4
SHIFT = 64
CHUNKS = 6
SPLIT = 16
SPAN = LEV - SPLIT
VMEM = pl.BlockSpec(memory_space=pltpu.VMEM)
SMEM = pl.BlockSpec(memory_space=pltpu.SMEM)


def up8(rows):
    return -(-rows // 8) * 8


def hat(offset):
    return jnp.maximum(0.0, 1.0 - jnp.abs(offset))


def low(word):
    return (word & 0xFFFF).astype(jnp.float32)


def high(word):
    return lax.shift_right_logical(word, 16).astype(jnp.float32)


def code(value, scale):
    return (value * scale + 0.5).astype(jnp.int32)


def aligned(start):
    return pl.multiple_of(start, 8)


def bits(mask):
    return jnp.where(mask, 1.0, 0.0).astype(jnp.bfloat16)


def halves(value):
    top = (value >> 8).astype(jnp.float32).astype(jnp.bfloat16)
    return top, (value & 255).astype(jnp.float32).astype(jnp.bfloat16)


def product(left, right):
    return jnp.dot(left, right, preferred_element_type=jnp.float32)


def chooser(place, pairs):
    index = lax.broadcasted_iota(jnp.int32, (pairs, place.shape[1]), 0)
    picks = jnp.concatenate(
        [jnp.where(place == 2 * index + odd, 1.0, 0.0) for odd in range(2)], axis=0
    )
    return jnp.concatenate([picks * 256.0, picks], axis=1).astype(jnp.bfloat16)


def chosen(picks, values):
    pairs = picks.shape[0] // 2
    parts = [halves(value) for value in values]
    data = jnp.concatenate(
        [
            jnp.concatenate([top for top, _ in parts], axis=1),
            jnp.concatenate([rest for _, rest in parts], axis=1),
        ],
        axis=0,
    )
    found = product(picks, data).astype(jnp.int32)
    return found[:pairs] | (found[pairs:] << 16)


class Mail:
    def __init__(self, n_lat, n_lon):
        self.n_lat, self.n_lon = n_lat, n_lon
        self.n = n_lat * n_lon
        self.lat = lax.axis_index("lat")
        self.lon = lax.axis_index("lon")
        self.me = self.lat * n_lon + self.lon

    def split(self, i):
        if isinstance(i, int):
            return i // self.n_lon, i % self.n_lon
        return lax.div(i, self.n_lon), lax.rem(i, self.n_lon)

    def device(self, i):
        k, j = self.split(i)
        return lax.rem(self.lat + k, self.n_lat), lax.rem(self.lon + j, self.n_lon)

    def origin(self, i):
        k, j = self.split(i)
        return (
            lax.rem(self.lat - k + self.n_lat, self.n_lat),
            lax.rem(self.lon - j + self.n_lon, self.n_lon),
        )

    def number(self, device):
        return device[0] * self.n_lon + device[1]

    def greet(self):
        barrier = pltpu.get_barrier_semaphore()
        for i in range(1, self.n):
            pl.semaphore_signal(
                barrier, inc=1, device_id=self.device(i), device_id_type=pl.DeviceIdType.MESH
            )

    def meet(self):
        pl.semaphore_wait(pltpu.get_barrier_semaphore(), self.n - 1)


class Parcel:
    def __init__(self, mail, src, dst, rows, used, send, recv):
        self.mail, self.src, self.dst = mail, src, dst
        self.rows, self.used = rows, used
        self.send, self.recv = send, recv

    def part(self, ref, t):
        return ref.at[pl.ds(aligned(t * self.rows), self.used)]

    def copy(self, i, back=False):
        mail = self.mail
        device = mail.origin(i) if back else mail.device(i)
        return pltpu.make_async_remote_copy(
            src_ref=self.part(self.src, mail.number(device)),
            dst_ref=self.part(self.dst, mail.me),
            send_sem=self.send.at[i], recv_sem=self.recv.at[i],
            device_id=device, device_id_type=pl.DeviceIdType.MESH,
        )

    def own(self):
        me = self.mail.me
        return pltpu.make_async_copy(
            self.part(self.src, me), self.part(self.dst, me), self.send.at[0]
        )

    def post(self, order):
        for i in order:
            if i:
                self.copy(i).start()
            else:
                self.own().start()

    def collect(self, back=False):
        self.own().wait()
        for i in range(1, self.mail.n):
            self.copy(i, back).wait_recv()

    def settle(self, back=False):
        for i in range(1, self.mail.n):
            self.copy(i, back).wait_send()


def arrange(heads, room, plan):
    n = heads.shape[0]
    f32 = jnp.float32
    count = n * room
    spaces = plan.shape[1]
    tall = up8(MB + 1)

    def index(shape, dim):
        return lax.broadcasted_iota(jnp.int32, shape, dim)

    place = lax.rem(index((BLK, count), 1), room)
    spread = product(heads.astype(jnp.bfloat16), bits(index((BLK, count), 0) == place + SHIFT))
    entry = index((n, count), 1)
    mine = lax.div(entry, room) == index((n, count), 0)
    held = heads[:, SHIFT + room : SHIFT + room + 1]
    homes = jnp.where(lax.rem(entry, room).astype(f32) < held, spread, float(MB))
    homes = jnp.sum(jnp.where(mine, homes, 0.0), axis=0, keepdims=True).astype(jnp.int32)
    member = jnp.where(index((tall, count), 0) == homes, 1.0, 0.0)
    earlier = bits(index((count, count), 0) < index((count, count), 1))
    rank = product(member.astype(jnp.bfloat16), earlier)
    sizes = jnp.sum(member, axis=1, keepdims=True).astype(jnp.int32)
    sizes = (sizes + (BUNCH - 1)) // BUNCH * BUNCH
    sizes = jnp.where(index((tall, count), 0) < MB, sizes, 0)
    wide = sizes.astype(f32).astype(jnp.bfloat16)
    first = product(bits(index((tall, tall), 1) < index((tall, tall), 0)), wide)
    space = jnp.sum(member * (first + rank), axis=0, keepdims=True).astype(jnp.int32)
    space = jnp.where(homes < MB, space, -1)
    number = (index((8, count), 1) + 1).astype(f32).astype(jnp.bfloat16)
    found = lax.dot_general(
        number, bits(index((spaces, count), 0) == space),
        (((1,), (1,)), ((), ())), preferred_element_type=f32,
    )
    plan[...] = found.astype(jnp.int32)
    ends = first.astype(jnp.int32)[:MB, :BLK] + sizes[:MB, :BLK]
    over = jnp.where(ends <= BUNCH * index((MB, BLK), 1), 1, 0)
    plan[1:2, 0:BLK] = jnp.sum(over, axis=0, keepdims=True)
    plan[2:3, 0:BLK] = jnp.max(ends, axis=0, keepdims=True)


def advect_kernel(dims, *refs):
    far = refs[:9]
    gone = (refs[9], refs[10], refs[13])
    heights, shares = refs[11:13]
    near = refs[14:23]
    slots, targets, requests, positions, velocity, increments, mass, keys, tiles = near
    advect(
        dims, far, near, gone, slots, targets, requests, positions, velocity, increments, mass,
        keys, tiles, heights, shares, *refs[23:],
    )


def advect(
    dims, far, near, gone, slots, targets, requests, positions, velocity, increments, mass,
    keys, tiles, heights, shares, moved, turbulence, plan,
    spot_msg, spots, back_msg, winds, mass_msg, z_msg,
    table, places, sorted_spots, sorted_mass, own_heads, heads, scaled, parts, found, sorted_z,
    asked_of, place, spot_sems, back_sems, mass_sems, z_sems, local,
):
    n_lat, n_lon, blocks, room, spot_rows, back_rows, mass_rows, z_rows = dims
    mail = Mail(n_lat, n_lon)
    mail.greet()
    fetches = [
        pltpu.make_async_copy(far[i], near[i], local.at[2 + i])
        for i in (0, 1, 2, 3, 7, 6, 8, 4, 5)
    ]
    for copy in fetches:
        copy.start()
    for copy in fetches[:3]:
        copy.wait()
    n = mail.n
    entries = Q * room
    half = entries // 2
    few = room // 2
    f32 = jnp.float32
    bf16 = jnp.bfloat16
    rows = lax.broadcasted_iota(jnp.int32, (blocks, blocks), 0)
    cols = lax.broadcasted_iota(jnp.int32, (blocks, blocks), 1)
    tile_ids = lax.broadcasted_iota(jnp.int32, (n, blocks), 0)
    lanes = lax.broadcasted_iota(jnp.int32, (blocks, BLK), 1)
    slot_row = slots[...]
    dest_row = targets[...]
    table[...] = jnp.zeros_like(table)
    table[0:1, :] = slot_row.astype(f32)
    table[1:2, :] = dest_row.astype(f32)
    table[2:4, 0:n] = requests[...].astype(f32)
    turned = table[...].T
    slot_col = turned[:, 0:1].astype(jnp.int32)
    dest_col = turned[:, 1:2].astype(jnp.int32)
    same_slot = jnp.where((slot_col == slot_row) & (rows < cols), 1.0, 0.0)
    slot_rank = jnp.sum(same_slot, axis=0, keepdims=True).astype(jnp.int32)
    same_dest = jnp.where((dest_col == dest_row) & (rows < cols), 1.0, 0.0)
    dest_rank = jnp.sum(same_dest, axis=0, keepdims=True).astype(jnp.int32)
    entry = (slot_row & 1) * room + slot_rank
    places[...] = jnp.zeros_like(places)
    places[0:1, :] = (((slot_row >> 1) * back_rows + (entry >> 1)) << 1) | (entry & 1)

    fetches[3].wait()
    words = chosen(
        chooser(slot_row * room + slot_rank, n * half),
        [
            code(positions[0], FULL / (BY - 1)),
            code(positions[1], FULL / (BX - 1)),
            code(positions[2], FULL / (LEV - 1)),
        ],
    )
    for c in range(3):
        sorted_spots[c] = words[:, c * BLK : (c + 1) * BLK]
    counts = product(bits((slot_row >> 1) == tile_ids), bits(lanes == (slot_col & 1)))
    asked = turned[0:n] if n < BLK else turned
    front = lanes[0:n]
    before = bits((dest_col == dest_row) & (cols < rows))
    rank_col = product(before, jnp.ones((blocks, BLK), bf16)).astype(jnp.int32)
    fetches[4].wait()
    homes = jnp.where(lanes == SHIFT + rank_col, (keys[...] >> 7).astype(f32), 0.0)
    homes = jnp.where(lanes == SHIFT + room, 1.0, homes).astype(bf16)
    landing = product(bits(dest_row == tile_ids), homes)
    counts = jnp.where((front == 2) | (front == 3), asked, counts)
    own_heads[...] = (counts + landing).astype(jnp.int32)

    def address(t, carry):
        for c in range(3):
            spot_msg[pl.ds(t * spot_rows + c * half, half), :] = sorted_spots[
                c, pl.ds(t * half, half), :
            ]
        spot_msg[pl.ds(t * spot_rows + 3 * half, 1), :] = own_heads[pl.ds(t, 1), :]
        return carry

    lax.fori_loop(0, n, address, 0, unroll=8)
    spot_mail = Parcel(
        mail, spot_msg, spots, spot_rows, 3 * half + 1, spot_sems.at[0], spot_sems.at[1]
    )
    back_mail = Parcel(mail, back_msg, winds, back_rows, 3 * half, back_sems.at[0], back_sems.at[1])
    mass_mail = Parcel(
        mail, mass_msg, shares, mass_rows, (S + 1) * few, mass_sems.at[0], mass_sems.at[1]
    )
    z_mail = Parcel(mail, z_msg, heights, z_rows, few, z_sems.at[0], z_sems.at[1])
    dest_place = dest_row * room + dest_rank
    picks = chooser(dest_place, n * few)
    fetches[5].wait()
    for s in range(0, S, 2):
        words = chosen(picks, [code(mass[pl.ds(s + i, blocks, stride=S), :], FULL) for i in range(2)])
        for i in range(2):
            sorted_mass[s + i] = words[:, i * BLK : (i + 1) * BLK]
    sorted_mass[S] = chosen(picks, [keys[...]])

    def wrap_mass(t, carry):
        for s in range(S + 1):
            mass_msg[pl.ds(t * mass_rows + s * few, few), :] = sorted_mass[s, pl.ds(t * few, few), :]
        return carry

    lax.fori_loop(0, n, wrap_mass, 0, unroll=4)
    order = list(range(n))
    lats = [order[k * n_lon : (k + 1) * n_lon] for k in range(n_lat)]
    mail.meet()
    spot_mail.post(order)
    placing = pltpu.make_async_copy(places, place, local.at[1])
    placing.start()

    mass_mail.post(lats[1])
    for copy in fetches[6:]:
        copy.wait()
    for c in range(3):
        turbulence[c] = DECAY * velocity[c] + KICK * increments[c]

    levels = lax.broadcasted_iota(jnp.int32, (LEV, BLK), 0).astype(f32)
    xs_at = lax.broadcasted_iota(jnp.int32, (BX, BLK), 0).astype(f32)
    ys_at = lax.broadcasted_iota(jnp.int32, (BY, BLK), 0).astype(f32)

    def asking(i):
        row = mail.number(mail.origin(i)) * spot_rows + 3 * half
        return pltpu.make_async_copy(
            spots.at[pl.ds(aligned(row) if half % 8 == 0 else row, 1)], asked_of, local.at[0]
        )

    def weights(y, x):
        hy = hat(y - ys_at)
        hx = hat(x - xs_at)
        flat = jnp.concatenate([hy[i : i + 1] * hx for i in range(BY)], axis=0)
        flat_hi = flat.astype(bf16)
        flat_lo = (flat - flat_hi.astype(f32)).astype(bf16)
        return jnp.concatenate([flat_hi, flat_lo], axis=0)

    def interpolate(i, mets):
        o = mail.number(mail.origin(i))
        base = o * spot_rows
        for c, top in enumerate((BY - 1, BX - 1, LEV - 1)):
            word = spots[pl.ds(base + c * half, half), :]
            scaled[c] = low(word) * (top / FULL)
            scaled[3 + c] = high(word) * (top / FULL)
        for k in range(half):
            block = tiles[mets[k // few]]
            seen = product(
                jnp.concatenate([block, block], axis=1),
                jnp.concatenate(
                    [
                        weights(scaled[3 * side, k : k + 1, :], scaled[3 * side + 1, k : k + 1, :])
                        for side in range(2)
                    ],
                    axis=1,
                ),
            )
            for side in range(2):
                wz = hat(scaled[3 * side + 2, k : k + 1, :] - levels).astype(bf16).astype(f32)
                for c in range(3):
                    part = seen[c * LEV : (c + 1) * LEV, side * BLK : (side + 1) * BLK] * wz
                    total = part[0:8]
                    for v in range(8, LEV, 8):
                        total = total + part[v : v + 8]
                    parts[3 * side + c, 8 * k : 8 * k + 8, :] = total
        for c in range(3):
            codes = []
            for side in range(2):
                wind = parts[3 * side + c, pl.ds(0, half, stride=8), :]
                for v in range(1, 8):
                    wind = wind + parts[3 * side + c, pl.ds(v, half, stride=8), :]
                codes.append(code(wind + GUST, FULL / (2 * GUST)))
            back_msg[pl.ds(o * back_rows + c * half, half), :] = codes[0] | (codes[1] << 16)

    spot_mail.own().wait()
    asking(0).start()
    asking(0).wait()

    def serve(i, carry):
        mets = [jnp.clip(asked_of[0, 2 + k], 0, MB - 1) for k in range(Q)]

        @pl.when(i + 1 < n)
        def _():
            spot_mail.copy(i + 1).wait_recv()
            asking(i + 1).start()

        interpolate(i, mets)

        @pl.when(i > 0)
        def _():
            back_mail.copy(i, back=True).start()

        @pl.when(i == 0)
        def _():
            back_mail.own().start()

        @pl.when(i + 1 < n)
        def _():
            asking(i + 1).wait()

        return carry

    lax.fori_loop(0, n, serve, 0)
    for o in range(n):
        row = o * spot_rows + 3 * half
        heads[o : o + 1, :] = spots[row : row + 1, :]
    arrange(heads[...].astype(f32), room, plan)
    mass_mail.post(lats[3])
    placing.wait()
    back_mail.collect()

    def fetch(b, carry):
        spot = place[0, b]
        row = jnp.clip(spot >> 1, 0, n * back_rows - 2 * half - 1)
        odd = 16 * (spot & 1)
        for c in range(3):
            word = winds[pl.ds(row + c * half, 1), :]
            found[c, pl.ds(b, 1), :] = lax.shift_right_logical(word, jnp.full_like(word, odd))
        return carry

    lax.fori_loop(0, blocks, fetch, 0, unroll=8)
    for c, top in enumerate((BY - 1.0, BX - 1.0, LEV - 1.0)):
        wind = low(found[c]) * (2 * GUST / FULL) - GUST
        moved[c] = jnp.clip(positions[c] + STEP * (wind + turbulence[c]), 0.0, top)
    sorted_z[...] = chosen(picks, [code(moved[2], FULL / (LEV - 1))])

    def wrap(t, carry):
        z_msg[pl.ds(t * z_rows, few), :] = sorted_z[pl.ds(t * few, few), :]
        return carry

    lax.fori_loop(0, n, wrap, 0, unroll=8)
    z_mail.post(order)
    leaving = [
        pltpu.make_async_copy(held, gone[i], local.at[2 + i])
        for i, held in enumerate((moved, turbulence, plan))
    ]
    for copy in leaving:
        copy.start()
    mass_mail.post(lats[2])
    mass_mail.post(lats[0])
    for copy in leaving:
        copy.wait()
    z_mail.collect()
    mass_mail.collect()
    spot_mail.settle()
    back_mail.settle()
    mass_mail.settle()
    z_mail.settle()


def deposit_kernel(
    dims, plan_in, heights_in, shares_in, moved_in, turbulence_in,
    moved, turbulence, out,
    plan, heights, shares, made, moved_held, turbulence_held, columns, sems,
):
    room, mass_rows, z_rows = dims
    few = room // 2
    into = [
        pltpu.make_async_copy(moved_in, moved_held, sems.at[0]),
        pltpu.make_async_copy(turbulence_in, turbulence_held, sems.at[1]),
    ]
    onward = [
        pltpu.make_async_copy(moved_held, moved, sems.at[2]),
        pltpu.make_async_copy(turbulence_held, turbulence, sems.at[3]),
    ]
    stock = [
        pltpu.make_async_copy(shares_in, shares, sems.at[4 + MB]),
        pltpu.make_async_copy(heights_in, heights, sems.at[5 + MB]),
        pltpu.make_async_copy(plan_in, plan, sems.at[6 + MB]),
    ]
    for copy in stock + into:
        copy.start()
    levels = lax.broadcasted_iota(jnp.int32, (SPAN, BLK), 0).astype(jnp.float32)
    columns[...] = lax.broadcasted_iota(jnp.int32, (2 * MBC, BLK), 0)

    def clear(h, carry):
        made[h] = jnp.zeros((S * LEV, MBC), jnp.float32)
        return carry

    lax.fori_loop(0, MB, clear, 0)
    for copy in stock:
        copy.wait()

    def operands(number):
        entry = jnp.maximum(number - 1, 0)
        o = lax.div(entry, room)
        q = lax.rem(entry, room)
        base = o * mass_rows + (q >> 1)
        odd = 16 * (q & 1)

        def half_of(word):
            return lax.shift_right_logical(word, jnp.full_like(word, odd))

        key = half_of(shares[pl.ds(base + S * few, 1), :]) & (MBC - 1)
        z = low(half_of(heights[pl.ds(o * z_rows + (q >> 1), 1), :])) * ((LEV - 1) / FULL)
        upper = z >= SPLIT
        z = z - jnp.where(upper, float(SPLIT), 0.0)
        key = key + jnp.where(upper, MBC, 0) + jnp.where(number > 0, 0, 4 * MBC)
        vert = hat(z - levels)
        parts = low(half_of(shares[pl.ds(base, S, stride=few), :])) * (1 / FULL)
        weights = jnp.concatenate([parts[s : s + 1] * vert for s in range(S)], axis=0)
        return weights.astype(jnp.bfloat16), bits(key == columns[...])

    def multiply(c):
        h = jnp.minimum(plan[1, c], MB - 1)
        pairs = [operands(plan[0, c * BUNCH + j]) for j in range(BUNCH)]
        found = lax.dot_general(
            jnp.concatenate([w for w, _ in pairs], axis=1),
            jnp.concatenate([p for _, p in pairs], axis=1),
            (((1,), (1,)), ((), ())),
            preferred_element_type=jnp.float32,
        )
        shared = SPAN - SPLIT
        for s in range(S):
            low_part = found[s * SPAN : (s + 1) * SPAN, 0:MBC]
            high_part = found[s * SPAN : (s + 1) * SPAN, MBC : 2 * MBC]
            made[h, s * LEV : s * LEV + SPLIT, :] += low_part[:SPLIT]
            made[h, s * LEV + SPLIT : s * LEV + SPAN, :] += low_part[SPLIT:] + high_part[:shared]
            made[h, s * LEV + SPAN : (s + 1) * LEV, :] += high_part[shared:]

    def leave(h):
        return pltpu.make_async_copy(made.at[h], out.at[h], sems.at[4 + h])

    def release(h, carry):
        leave(h).start()
        return carry

    def several(i, ready):
        for j in range(CHUNKS):
            multiply(CHUNKS * i + j)
        done = jnp.minimum(plan[1, CHUNKS * (i + 1)], MB)
        lax.fori_loop(ready, done, release, 0)
        return jnp.maximum(ready, done)

    for copy in into:
        copy.wait()
    for copy in onward:
        copy.start()
    chunks = plan[2, 0] // BUNCH
    ready = lax.fori_loop(0, (chunks + CHUNKS - 1) // CHUNKS, several, 0)
    lax.fori_loop(ready, MB, release, 0)
    for copy in onward:
        copy.wait()
    for h in range(MB):
        leave(h).wait()


def body(
    winds, positions, velocity, increments, mass, requests, block_slots, destinations, cell_keys
):
    n_lat = lax.axis_size("lat")
    n_lon = lax.axis_size("lon")
    n = n_lat * n_lon
    blocks = positions.shape[0]
    room = 2 * blocks // n
    half = Q * room // 2
    few = room // 2
    spot_rows = up8(3 * half + 1)
    back_rows = up8(3 * half)
    mass_rows = up8((S + 1) * few)
    z_rows = up8(few)
    spaces = -(-(n * room + (MB + CHUNKS) * BUNCH) // BLK) * BLK
    i32 = jnp.int32
    f32 = jnp.float32
    like = jax.ShapeDtypeStruct
    dma = pltpu.SemaphoreType.DMA

    anywhere = pl.BlockSpec(memory_space=pl.ANY)
    mass = mass.reshape(-1, BLK)
    winds = winds.reshape(MB, 3 * LEV, MBC)
    positions, velocity, increments = (
        each.transpose(1, 0, 2) for each in (positions, velocity, increments)
    )
    inputs = (
        block_slots.reshape(1, -1), destinations.reshape(1, -1), requests[0].T,
        positions, velocity, increments, mass, cell_keys, winds,
    )
    moved, turbulence, heights, shares, plan = pl.pallas_call(
        functools.partial(
            advect_kernel,
            (n_lat, n_lon, blocks, room, spot_rows, back_rows, mass_rows, z_rows),
        ),
        out_shape=(
            like(positions.shape, f32),
            like(positions.shape, f32),
            like((n * z_rows, BLK), i32),
            like((n * mass_rows, BLK), i32),
            like((8, spaces), i32),
        ),
        in_specs=[pl.BlockSpec(memory_space=pltpu.HBM)] * 9,
        out_specs=(anywhere,) * 5,
        scratch_shapes=[
            pltpu.VMEM(each.shape, each.dtype)
            for each in inputs + (positions, positions)
        ]
        + [pltpu.VMEM((8, spaces), i32)]
        + [
            pltpu.VMEM((n * spot_rows, BLK), i32),
            pltpu.VMEM((n * spot_rows, BLK), i32),
            pltpu.VMEM((n * back_rows, BLK), i32),
            pltpu.VMEM((n * back_rows, BLK), i32),
            pltpu.VMEM((n * mass_rows, BLK), i32),
            pltpu.VMEM((n * z_rows, BLK), i32),
            pltpu.VMEM((BLK, BLK), f32),
            pltpu.VMEM((8, blocks), i32),
            pltpu.VMEM((3, n * half, BLK), i32),
            pltpu.VMEM((S + 1, n * few, BLK), i32),
            pltpu.VMEM((n, BLK), i32),
            pltpu.VMEM((n, BLK), i32),
            pltpu.VMEM((6, half, BLK), f32),
            pltpu.VMEM((6, 8 * half, BLK), f32),
            pltpu.VMEM((3, blocks, BLK), i32),
            pltpu.VMEM((n * few, BLK), i32),
            pltpu.SMEM((1, BLK), i32),
            pltpu.SMEM((8, blocks), i32),
            dma((2, n)),
            dma((2, n)),
            dma((2, n)),
            dma((2, n)),
            dma((2 + len(inputs),)),
        ],
        compiler_params=pltpu.CompilerParams(collective_id=0, has_side_effects=True),
        name="advect",
    )(*inputs)
    moved, turbulence, total = pl.pallas_call(
        functools.partial(deposit_kernel, (room, mass_rows, z_rows)),
        out_shape=(
            like(positions.shape, f32),
            like(positions.shape, f32),
            like((MB, S * LEV, MBC), f32),
        ),
        in_specs=[anywhere] * 5,
        out_specs=(anywhere,) * 3,
        scratch_shapes=[
            pltpu.SMEM(plan.shape, i32),
            pltpu.VMEM(heights.shape, i32),
            pltpu.VMEM(shares.shape, i32),
            pltpu.VMEM((MB, S * LEV, MBC), f32),
            pltpu.VMEM(positions.shape, f32),
            pltpu.VMEM(positions.shape, f32),
            pltpu.VMEM((2 * MBC, BLK), i32),
            dma((7 + MB,)),
        ],
        name="deposit",
    )(plan, heights, shares, moved, turbulence)
    concentration = total.reshape(MBR, MBK, S, LEV, MBC)
    return (moved.transpose(1, 0, 2), turbulence.transpose(1, 0, 2), concentration)


def solution(mesh):
    rows = ("lat", "lon")
    in_specs = (
        P("lat", "lon", None, None, None),
        P(rows, None, None),
        P(rows, None, None),
        P(rows, None, None),
        P(rows, None, None),
        P(rows, None, None),
        P(rows, None),
        P(rows, None),
        P(rows, None),
    )
    out_specs = (
        P(rows, None, None),
        P(rows, None, None),
        P("lat", "lon", None, None, None),
    )
    return jax.shard_map(body, mesh=mesh, in_specs=in_specs, out_specs=out_specs, check_vma=False)
```

```python
import functools

import jax
import jax.numpy as jnp
from jax import lax
from jax.experimental import pallas as pl
from jax.experimental.pallas import tpu as pltpu
from jax.sharding import PartitionSpec as P

BY = 8
BX = 16
MBC = 128
LEV = 40
S = 8
BLK = 128
MBR = 4
MBK = 4
Q = 2
MB = MBR * MBK

DECAY = 0.8
KICK = 0.6
STEP = 0.5

FULL = 65535.0
GUST = 6.1
BUNCH = 4
SHIFT = 64
CHUNKS = 8
SPLIT = 16
SPAN = LEV - SPLIT
VMEM = pl.BlockSpec(memory_space=pltpu.VMEM)
SMEM = pl.BlockSpec(memory_space=pltpu.SMEM)


def up8(rows):
    return -(-rows // 8) * 8


def hat(offset):
    return jnp.maximum(0.0, 1.0 - jnp.abs(offset))


def low(word):
    return (word & 0xFFFF).astype(jnp.float32)


def high(word):
    return lax.shift_right_logical(word, 16).astype(jnp.float32)


def code(value, scale):
    return (value * scale + 0.5).astype(jnp.int32)


def aligned(start):
    return pl.multiple_of(start, 8)


def bits(mask):
    return jnp.where(mask, 1.0, 0.0).astype(jnp.bfloat16)


def halves(value):
    top = (value >> 8).astype(jnp.float32).astype(jnp.bfloat16)
    return top, (value & 255).astype(jnp.float32).astype(jnp.bfloat16)


def product(left, right):
    return jnp.dot(left, right, preferred_element_type=jnp.float32)


def chooser(place, pairs):
    index = lax.broadcasted_iota(jnp.int32, (pairs, place.shape[1]), 0)
    picks = jnp.concatenate(
        [jnp.where(place == 2 * index + odd, 1.0, 0.0) for odd in range(2)], axis=0
    )
    return jnp.concatenate([picks * 256.0, picks], axis=1).astype(jnp.bfloat16)


def chosen(picks, values):
    pairs = picks.shape[0] // 2
    parts = [halves(value) for value in values]
    data = jnp.concatenate(
        [
            jnp.concatenate([top for top, _ in parts], axis=1),
            jnp.concatenate([rest for _, rest in parts], axis=1),
        ],
        axis=0,
    )
    found = product(picks, data).astype(jnp.int32)
    return found[:pairs] | (found[pairs:] << 16)


class Mail:
    def __init__(self, n_lat, n_lon):
        self.n_lat, self.n_lon = n_lat, n_lon
        self.n = n_lat * n_lon
        self.lat = lax.axis_index("lat")
        self.lon = lax.axis_index("lon")
        self.me = self.lat * n_lon + self.lon

    def split(self, i):
        if isinstance(i, int):
            return i // self.n_lon, i % self.n_lon
        return lax.div(i, self.n_lon), lax.rem(i, self.n_lon)

    def device(self, i):
        k, j = self.split(i)
        return lax.rem(self.lat + k, self.n_lat), lax.rem(self.lon + j, self.n_lon)

    def origin(self, i):
        k, j = self.split(i)
        return (
            lax.rem(self.lat - k + self.n_lat, self.n_lat),
            lax.rem(self.lon - j + self.n_lon, self.n_lon),
        )

    def number(self, device):
        return device[0] * self.n_lon + device[1]

    def greet(self):
        barrier = pltpu.get_barrier_semaphore()
        for i in range(1, self.n):
            pl.semaphore_signal(
                barrier, inc=1, device_id=self.device(i), device_id_type=pl.DeviceIdType.MESH
            )

    def meet(self):
        pl.semaphore_wait(pltpu.get_barrier_semaphore(), self.n - 1)


class Parcel:
    def __init__(self, mail, src, dst, rows, used, send, recv):
        self.mail, self.src, self.dst = mail, src, dst
        self.rows, self.used = rows, used
        self.send, self.recv = send, recv

    def part(self, ref, t):
        return ref.at[pl.ds(aligned(t * self.rows), self.used)]

    def copy(self, i, back=False):
        mail = self.mail
        device = mail.origin(i) if back else mail.device(i)
        return pltpu.make_async_remote_copy(
            src_ref=self.part(self.src, mail.number(device)),
            dst_ref=self.part(self.dst, mail.me),
            send_sem=self.send.at[i], recv_sem=self.recv.at[i],
            device_id=device, device_id_type=pl.DeviceIdType.MESH,
        )

    def own(self):
        me = self.mail.me
        return pltpu.make_async_copy(
            self.part(self.src, me), self.part(self.dst, me), self.send.at[0]
        )

    def post(self, order):
        for i in order:
            if i:
                self.copy(i).start()
            else:
                self.own().start()

    def collect(self, back=False):
        self.own().wait()
        for i in range(1, self.mail.n):
            self.copy(i, back).wait_recv()

    def settle(self, back=False):
        for i in range(1, self.mail.n):
            self.copy(i, back).wait_send()


def arrange(heads, room, plan):
    n = heads.shape[0]
    f32 = jnp.float32
    count = n * room
    spaces = plan.shape[1]
    tall = up8(MB + 1)

    def index(shape, dim):
        return lax.broadcasted_iota(jnp.int32, shape, dim)

    place = lax.rem(index((BLK, count), 1), room)
    spread = product(heads.astype(jnp.bfloat16), bits(index((BLK, count), 0) == place + SHIFT))
    entry = index((n, count), 1)
    mine = lax.div(entry, room) == index((n, count), 0)
    held = heads[:, SHIFT + room : SHIFT + room + 1]
    homes = jnp.where(lax.rem(entry, room).astype(f32) < held, spread, float(MB))
    homes = jnp.sum(jnp.where(mine, homes, 0.0), axis=0, keepdims=True).astype(jnp.int32)
    member = jnp.where(index((tall, count), 0) == homes, 1.0, 0.0)
    earlier = bits(index((count, count), 0) < index((count, count), 1))
    rank = product(member.astype(jnp.bfloat16), earlier)
    sizes = jnp.sum(member, axis=1, keepdims=True).astype(jnp.int32)
    sizes = (sizes + (BUNCH - 1)) // BUNCH * BUNCH
    sizes = jnp.where(index((tall, count), 0) < MB, sizes, 0)
    wide = sizes.astype(f32).astype(jnp.bfloat16)
    first = product(bits(index((tall, tall), 1) < index((tall, tall), 0)), wide)
    space = jnp.sum(member * (first + rank), axis=0, keepdims=True).astype(jnp.int32)
    space = jnp.where(homes < MB, space, -1)
    number = (index((8, count), 1) + 1).astype(f32).astype(jnp.bfloat16)
    found = lax.dot_general(
        number, bits(index((spaces, count), 0) == space),
        (((1,), (1,)), ((), ())), preferred_element_type=f32,
    )
    plan[...] = found.astype(jnp.int32)
    ends = first.astype(jnp.int32)[:MB, :BLK] + sizes[:MB, :BLK]
    over = jnp.where(ends <= BUNCH * index((MB, BLK), 1), 1, 0)
    plan[1:2, 0:BLK] = jnp.sum(over, axis=0, keepdims=True)
    plan[2:3, 0:BLK] = jnp.max(ends, axis=0, keepdims=True)


def advect_kernel(dims, *refs):
    far = refs[:9]
    gone = (refs[9], refs[10], refs[13])
    heights, shares = refs[11:13]
    near = refs[14:23]
    slots, targets, requests, positions, velocity, increments, mass, keys, tiles = near
    advect(
        dims, far, near, gone, slots, targets, requests, positions, velocity, increments, mass,
        keys, tiles, heights, shares, *refs[23:],
    )


def advect(
    dims, far, near, gone, slots, targets, requests, positions, velocity, increments, mass,
    keys, tiles, heights, shares, moved, turbulence, plan,
    spot_msg, spots, back_msg, winds, mass_msg, z_msg,
    table, places, sorted_spots, sorted_mass, own_heads, heads, scaled, parts, found, sorted_z,
    asked_of, place, spot_sems, back_sems, mass_sems, z_sems, local,
):
    n_lat, n_lon, blocks, room, spot_rows, back_rows, mass_rows, z_rows = dims
    mail = Mail(n_lat, n_lon)
    mail.greet()
    fetches = [
        pltpu.make_async_copy(far[i], near[i], local.at[2 + i])
        for i in (0, 1, 2, 3, 7, 6, 8, 4, 5)
    ]
    for copy in fetches:
        copy.start()
    for copy in fetches[:3]:
        copy.wait()
    n = mail.n
    entries = Q * room
    half = entries // 2
    few = room // 2
    f32 = jnp.float32
    bf16 = jnp.bfloat16
    rows = lax.broadcasted_iota(jnp.int32, (blocks, blocks), 0)
    cols = lax.broadcasted_iota(jnp.int32, (blocks, blocks), 1)
    tile_ids = lax.broadcasted_iota(jnp.int32, (n, blocks), 0)
    lanes = lax.broadcasted_iota(jnp.int32, (blocks, BLK), 1)
    slot_row = slots[...]
    dest_row = targets[...]
    table[...] = jnp.zeros_like(table)
    table[0:1, :] = slot_row.astype(f32)
    table[1:2, :] = dest_row.astype(f32)
    table[2:4, 0:n] = requests[...].astype(f32)
    turned = table[...].T
    slot_col = turned[:, 0:1].astype(jnp.int32)
    dest_col = turned[:, 1:2].astype(jnp.int32)
    same_slot = jnp.where((slot_col == slot_row) & (rows < cols), 1.0, 0.0)
    slot_rank = jnp.sum(same_slot, axis=0, keepdims=True).astype(jnp.int32)
    same_dest = jnp.where((dest_col == dest_row) & (rows < cols), 1.0, 0.0)
    dest_rank = jnp.sum(same_dest, axis=0, keepdims=True).astype(jnp.int32)
    entry = (slot_row & 1) * room + slot_rank
    places[...] = jnp.zeros_like(places)
    places[0:1, :] = (((slot_row >> 1) * back_rows + (entry >> 1)) << 1) | (entry & 1)

    fetches[3].wait()
    words = chosen(
        chooser(slot_row * room + slot_rank, n * half),
        [
            code(positions[0], FULL / (BY - 1)),
            code(positions[1], FULL / (BX - 1)),
            code(positions[2], FULL / (LEV - 1)),
        ],
    )
    for c in range(3):
        sorted_spots[c] = words[:, c * BLK : (c + 1) * BLK]
    counts = product(bits((slot_row >> 1) == tile_ids), bits(lanes == (slot_col & 1)))
    asked = turned[0:n] if n < BLK else turned
    front = lanes[0:n]
    before = bits((dest_col == dest_row) & (cols < rows))
    rank_col = product(before, jnp.ones((blocks, BLK), bf16)).astype(jnp.int32)
    fetches[4].wait()
    homes = jnp.where(lanes == SHIFT + rank_col, (keys[...] >> 7).astype(f32), 0.0)
    homes = jnp.where(lanes == SHIFT + room, 1.0, homes).astype(bf16)
    landing = product(bits(dest_row == tile_ids), homes)
    counts = jnp.where((front == 2) | (front == 3), asked, counts)
    own_heads[...] = (counts + landing).astype(jnp.int32)

    def address(t, carry):
        for c in range(3):
            spot_msg[pl.ds(t * spot_rows + c * half, half), :] = sorted_spots[
                c, pl.ds(t * half, half), :
            ]
        spot_msg[pl.ds(t * spot_rows + 3 * half, 1), :] = own_heads[pl.ds(t, 1), :]
        return carry

    lax.fori_loop(0, n, address, 0, unroll=8)
    spot_mail = Parcel(
        mail, spot_msg, spots, spot_rows, 3 * half + 1, spot_sems.at[0], spot_sems.at[1]
    )
    back_mail = Parcel(mail, back_msg, winds, back_rows, 3 * half, back_sems.at[0], back_sems.at[1])
    mass_mail = Parcel(
        mail, mass_msg, shares, mass_rows, (S + 1) * few, mass_sems.at[0], mass_sems.at[1]
    )
    z_mail = Parcel(mail, z_msg, heights, z_rows, few, z_sems.at[0], z_sems.at[1])
    dest_place = dest_row * room + dest_rank
    picks = chooser(dest_place, n * few)
    fetches[5].wait()
    for s in range(0, S, 2):
        words = chosen(picks, [code(mass[pl.ds(s + i, blocks, stride=S), :], FULL) for i in range(2)])
        for i in range(2):
            sorted_mass[s + i] = words[:, i * BLK : (i + 1) * BLK]
    sorted_mass[S] = chosen(picks, [keys[...]])

    def wrap_mass(t, carry):
        for s in range(S + 1):
            mass_msg[pl.ds(t * mass_rows + s * few, few), :] = sorted_mass[s, pl.ds(t * few, few), :]
        return carry

    lax.fori_loop(0, n, wrap_mass, 0, unroll=4)
    order = list(range(n))
    some = n_lat // 4
    soon = order[n_lon : (1 + some) * n_lon]
    next_up = order[(n_lat - some) * n_lon :]
    late = order[(1 + some) * n_lon : (n_lat - some) * n_lon] + order[:n_lon]
    mail.meet()
    spot_mail.post(order)
    placing = pltpu.make_async_copy(places, place, local.at[1])
    placing.start()

    mass_mail.post(soon)
    for copy in fetches[6:]:
        copy.wait()
    for c in range(3):
        turbulence[c] = DECAY * velocity[c] + KICK * increments[c]

    levels = lax.broadcasted_iota(jnp.int32, (LEV, BLK), 0).astype(f32)
    xs_at = lax.broadcasted_iota(jnp.int32, (BX, BLK), 0).astype(f32)
    ys_at = lax.broadcasted_iota(jnp.int32, (BY, BLK), 0).astype(f32)

    def asking(i):
        row = mail.number(mail.origin(i)) * spot_rows + 3 * half
        return pltpu.make_async_copy(
            spots.at[pl.ds(aligned(row) if half % 8 == 0 else row, 1)], asked_of, local.at[0]
        )

    def weights(y, x):
        hy = hat(y - ys_at)
        hx = hat(x - xs_at)
        flat = jnp.concatenate([hy[i : i + 1] * hx for i in range(BY)], axis=0)
        flat_hi = flat.astype(bf16)
        flat_lo = (flat - flat_hi.astype(f32)).astype(bf16)
        return jnp.concatenate([flat_hi, flat_lo], axis=0)

    def interpolate(i, mets):
        o = mail.number(mail.origin(i))
        base = o * spot_rows
        for c, top in enumerate((BY - 1, BX - 1, LEV - 1)):
            word = spots[pl.ds(base + c * half, half), :]
            scaled[c] = low(word) * (top / FULL)
            scaled[3 + c] = high(word) * (top / FULL)
        for k in range(half):
            block = tiles[mets[k // few]]
            seen = product(
                jnp.concatenate([block, block], axis=1),
                jnp.concatenate(
                    [
                        weights(scaled[3 * side, k : k + 1, :], scaled[3 * side + 1, k : k + 1, :])
                        for side in range(2)
                    ],
                    axis=1,
                ),
            )
            for side in range(2):
                wz = hat(scaled[3 * side + 2, k : k + 1, :] - levels).astype(bf16).astype(f32)
                for c in range(3):
                    part = seen[c * LEV : (c + 1) * LEV, side * BLK : (side + 1) * BLK] * wz
                    total = part[0:8]
                    for v in range(8, LEV, 8):
                        total = total + part[v : v + 8]
                    parts[3 * side + c, 8 * k : 8 * k + 8, :] = total
        for c in range(3):
            codes = []
            for side in range(2):
                wind = parts[3 * side + c, pl.ds(0, half, stride=8), :]
                for v in range(1, 8):
                    wind = wind + parts[3 * side + c, pl.ds(v, half, stride=8), :]
                codes.append(code(wind + GUST, FULL / (2 * GUST)))
            back_msg[pl.ds(o * back_rows + c * half, half), :] = codes[0] | (codes[1] << 16)

    spot_mail.own().wait()
    asking(0).start()
    asking(0).wait()

    def serve(i, carry):
        mets = [jnp.clip(asked_of[0, 2 + k], 0, MB - 1) for k in range(Q)]

        @pl.when(i + 1 < n)
        def _():
            spot_mail.copy(i + 1).wait_recv()
            asking(i + 1).start()

        interpolate(i, mets)

        @pl.when(i > 0)
        def _():
            back_mail.copy(i, back=True).start()

        @pl.when(i == 0)
        def _():
            back_mail.own().start()

        @pl.when(i + 1 < n)
        def _():
            asking(i + 1).wait()

        return carry

    lax.fori_loop(0, n, serve, 0)
    for o in range(n):
        row = o * spot_rows + 3 * half
        heads[o : o + 1, :] = spots[row : row + 1, :]
    arrange(heads[...].astype(f32), room, plan)
    mass_mail.post(next_up)
    placing.wait()
    back_mail.collect()

    def fetch(b, carry):
        spot = place[0, b]
        row = jnp.clip(spot >> 1, 0, n * back_rows - 2 * half - 1)
        odd = 16 * (spot & 1)
        for c in range(3):
            word = winds[pl.ds(row + c * half, 1), :]
            found[c, pl.ds(b, 1), :] = lax.shift_right_logical(word, jnp.full_like(word, odd))
        return carry

    lax.fori_loop(0, blocks, fetch, 0, unroll=8)
    for c, top in enumerate((BY - 1.0, BX - 1.0, LEV - 1.0)):
        wind = low(found[c]) * (2 * GUST / FULL) - GUST
        moved[c] = jnp.clip(positions[c] + STEP * (wind + turbulence[c]), 0.0, top)
    sorted_z[...] = chosen(picks, [code(moved[2], FULL / (LEV - 1))])

    def wrap(t, carry):
        z_msg[pl.ds(t * z_rows, few), :] = sorted_z[pl.ds(t * few, few), :]
        return carry

    lax.fori_loop(0, n, wrap, 0, unroll=8)
    z_mail.post(order)
    leaving = [
        pltpu.make_async_copy(held, gone[i], local.at[2 + i])
        for i, held in enumerate((moved, turbulence, plan))
    ]
    for copy in leaving:
        copy.start()
    mass_mail.post(late)
    for copy in leaving:
        copy.wait()
    z_mail.collect()
    mass_mail.collect()
    spot_mail.settle()
    back_mail.settle()
    mass_mail.settle()
    z_mail.settle()


def deposit_kernel(
    dims, plan_in, heights_in, shares_in, moved_in, turbulence_in,
    moved, turbulence, out,
    plan, heights, shares, made, moved_held, turbulence_held, columns, sems,
):
    room, mass_rows, z_rows = dims
    few = room // 2
    into = [
        pltpu.make_async_copy(moved_in, moved_held, sems.at[0]),
        pltpu.make_async_copy(turbulence_in, turbulence_held, sems.at[1]),
    ]
    onward = [
        pltpu.make_async_copy(moved_held, moved, sems.at[2]),
        pltpu.make_async_copy(turbulence_held, turbulence, sems.at[3]),
    ]
    stock = [
        pltpu.make_async_copy(shares_in, shares, sems.at[4 + MB]),
        pltpu.make_async_copy(heights_in, heights, sems.at[5 + MB]),
        pltpu.make_async_copy(plan_in, plan, sems.at[6 + MB]),
    ]
    for copy in stock + into:
        copy.start()
    levels = lax.broadcasted_iota(jnp.int32, (SPAN, BLK), 0).astype(jnp.float32)
    columns[...] = lax.broadcasted_iota(jnp.int32, (2 * MBC, BLK), 0)

    def clear(h, carry):
        made[h] = jnp.zeros((S * LEV, MBC), jnp.float32)
        return carry

    lax.fori_loop(0, MB, clear, 0)
    for copy in stock:
        copy.wait()

    def operands(number):
        entry = jnp.maximum(number - 1, 0)
        o = lax.div(entry, room)
        q = lax.rem(entry, room)
        base = o * mass_rows + (q >> 1)
        odd = 16 * (q & 1)

        def half_of(word):
            return lax.shift_right_logical(word, jnp.full_like(word, odd))

        key = half_of(shares[pl.ds(base + S * few, 1), :]) & (MBC - 1)
        z = low(half_of(heights[pl.ds(o * z_rows + (q >> 1), 1), :])) * ((LEV - 1) / FULL)
        upper = z >= SPLIT
        z = z - jnp.where(upper, float(SPLIT), 0.0)
        key = key + jnp.where(upper, MBC, 0) + jnp.where(number > 0, 0, 4 * MBC)
        vert = hat(z - levels)
        parts = low(half_of(shares[pl.ds(base, S, stride=few), :])) * (1 / FULL)
        weights = jnp.concatenate([parts[s : s + 1] * vert for s in range(S)], axis=0)
        return weights.astype(jnp.bfloat16), bits(key == columns[...])

    def multiply(c):
        h = jnp.minimum(plan[1, c], MB - 1)
        pairs = [operands(plan[0, c * BUNCH + j]) for j in range(BUNCH)]
        found = lax.dot_general(
            jnp.concatenate([w for w, _ in pairs], axis=1),
            jnp.concatenate([p for _, p in pairs], axis=1),
            (((1,), (1,)), ((), ())),
            preferred_element_type=jnp.float32,
        )
        shared = SPAN - SPLIT
        for s in range(S):
            low_part = found[s * SPAN : (s + 1) * SPAN, 0:MBC]
            high_part = found[s * SPAN : (s + 1) * SPAN, MBC : 2 * MBC]
            made[h, s * LEV : s * LEV + SPLIT, :] += low_part[:SPLIT]
            made[h, s * LEV + SPLIT : s * LEV + SPAN, :] += low_part[SPLIT:] + high_part[:shared]
            made[h, s * LEV + SPAN : (s + 1) * LEV, :] += high_part[shared:]

    def leave(h):
        return pltpu.make_async_copy(made.at[h], out.at[h], sems.at[4 + h])

    def release(h, carry):
        leave(h).start()
        return carry

    def several(i, ready):
        for j in range(CHUNKS):
            multiply(CHUNKS * i + j)
        done = jnp.minimum(plan[1, CHUNKS * (i + 1)], MB)
        lax.fori_loop(ready, done, release, 0)
        return jnp.maximum(ready, done)

    for copy in into:
        copy.wait()
    for copy in onward:
        copy.start()
    chunks = plan[2, 0] // BUNCH
    ready = lax.fori_loop(0, (chunks + CHUNKS - 1) // CHUNKS, several, 0)
    lax.fori_loop(ready, MB, release, 0)
    for copy in onward:
        copy.wait()
    for h in range(MB):
        leave(h).wait()


def body(
    winds, positions, velocity, increments, mass, requests, block_slots, destinations, cell_keys
):
    n_lat = lax.axis_size("lat")
    n_lon = lax.axis_size("lon")
    n = n_lat * n_lon
    blocks = positions.shape[0]
    room = 2 * blocks // n
    half = Q * room // 2
    few = room // 2
    spot_rows = up8(3 * half + 1)
    back_rows = up8(3 * half)
    mass_rows = up8((S + 1) * few)
    z_rows = up8(few)
    spaces = -(-(n * room + (MB + CHUNKS) * BUNCH) // BLK) * BLK
    i32 = jnp.int32
    f32 = jnp.float32
    like = jax.ShapeDtypeStruct
    dma = pltpu.SemaphoreType.DMA

    anywhere = pl.BlockSpec(memory_space=pl.ANY)
    mass = mass.reshape(-1, BLK)
    winds = winds.reshape(MB, 3 * LEV, MBC)
    positions, velocity, increments = (
        each.transpose(1, 0, 2) for each in (positions, velocity, increments)
    )
    inputs = (
        block_slots.reshape(1, -1), destinations.reshape(1, -1), requests[0].T,
        positions, velocity, increments, mass, cell_keys, winds,
    )
    moved, turbulence, heights, shares, plan = pl.pallas_call(
        functools.partial(
            advect_kernel,
            (n_lat, n_lon, blocks, room, spot_rows, back_rows, mass_rows, z_rows),
        ),
        out_shape=(
            like(positions.shape, f32),
            like(positions.shape, f32),
            like((n * z_rows, BLK), i32),
            like((n * mass_rows, BLK), i32),
            like((8, spaces), i32),
        ),
        in_specs=[pl.BlockSpec(memory_space=pltpu.HBM)] * 9,
        out_specs=(anywhere,) * 5,
        scratch_shapes=[
            pltpu.VMEM(each.shape, each.dtype)
            for each in inputs + (positions, positions)
        ]
        + [pltpu.VMEM((8, spaces), i32)]
        + [
            pltpu.VMEM((n * spot_rows, BLK), i32),
            pltpu.VMEM((n * spot_rows, BLK), i32),
            pltpu.VMEM((n * back_rows, BLK), i32),
            pltpu.VMEM((n * back_rows, BLK), i32),
            pltpu.VMEM((n * mass_rows, BLK), i32),
            pltpu.VMEM((n * z_rows, BLK), i32),
            pltpu.VMEM((BLK, BLK), f32),
            pltpu.VMEM((8, blocks), i32),
            pltpu.VMEM((3, n * half, BLK), i32),
            pltpu.VMEM((S + 1, n * few, BLK), i32),
            pltpu.VMEM((n, BLK), i32),
            pltpu.VMEM((n, BLK), i32),
            pltpu.VMEM((6, half, BLK), f32),
            pltpu.VMEM((6, 8 * half, BLK), f32),
            pltpu.VMEM((3, blocks, BLK), i32),
            pltpu.VMEM((n * few, BLK), i32),
            pltpu.SMEM((1, BLK), i32),
            pltpu.SMEM((8, blocks), i32),
            dma((2, n)),
            dma((2, n)),
            dma((2, n)),
            dma((2, n)),
            dma((2 + len(inputs),)),
        ],
        compiler_params=pltpu.CompilerParams(collective_id=0, has_side_effects=True),
        name="advect",
    )(*inputs)
    moved, turbulence, total = pl.pallas_call(
        functools.partial(deposit_kernel, (room, mass_rows, z_rows)),
        out_shape=(
            like(positions.shape, f32),
            like(positions.shape, f32),
            like((MB, S * LEV, MBC), f32),
        ),
        in_specs=[anywhere] * 5,
        out_specs=(anywhere,) * 3,
        scratch_shapes=[
            pltpu.SMEM(plan.shape, i32),
            pltpu.VMEM(heights.shape, i32),
            pltpu.VMEM(shares.shape, i32),
            pltpu.VMEM((MB, S * LEV, MBC), f32),
            pltpu.VMEM(positions.shape, f32),
            pltpu.VMEM(positions.shape, f32),
            pltpu.VMEM((2 * MBC, BLK), i32),
            dma((7 + MB,)),
        ],
        name="deposit",
    )(plan, heights, shares, moved, turbulence)
    concentration = total.reshape(MBR, MBK, S, LEV, MBC)
    return (moved.transpose(1, 0, 2), turbulence.transpose(1, 0, 2), concentration)


def solution(mesh):
    rows = ("lat", "lon")
    in_specs = (
        P("lat", "lon", None, None, None),
        P(rows, None, None),
        P(rows, None, None),
        P(rows, None, None),
        P(rows, None, None),
        P(rows, None, None),
        P(rows, None),
        P(rows, None),
        P(rows, None),
    )
    out_specs = (
        P(rows, None, None),
        P(rows, None, None),
        P("lat", "lon", None, None, None),
    )
    return jax.shard_map(body, mesh=mesh, in_specs=in_specs, out_specs=out_specs, check_vma=False)
```
